32 devices in a mesh: dp: 16 (over z, x, core), tensor: 2 (over y).
Axes of the slice: x: 2, y: 2, z: 4, core: 2. Of those that a mesh axis runs over, the one named last changes fastest.
Arguments:
- inputs: bfloat16 [32768, 1024], P('dp'), may hold values from -6 to 6
- cotangent: bfloat16 [32768, 1024], P('dp'), may hold values from -6 to 6
- segment_ids: int32 [16, 2048], P('dp'), may hold values from 0 to 7, never falling along the last dimension, each value on 1 to 1024 neighbouring positions
- w_qkv: float32 [3, 1024, 1024], P(None, 'dp', 'tensor'), may hold values from -0.1875 to 0.1875
- w_out: float32 [1024, 1024], P('tensor', 'dp'), may hold values from -1.5 to 1.5
- w_fc1: float32 [1024, 4096], P('dp', 'tensor'), may hold values from -0.1875 to 0.1875
- w_fc2: float32 [4096, 1024], P('tensor', 'dp'), may hold values from -0.09375 to 0.09375
- norm_gain: float32 [4, 1024], replicated, may hold values from 0.5 to 1.5
- norm_bias: float32 [4, 1024], replicated, may hold values from -1.8 to 1.8
- head_bias: float32 [2, 1024], replicated, may hold values from -3 to 3
- out_bias: float32 [2, 1024], replicated, may hold values from -1.2 to 1.2
- fc1_bias: float32 [4096], replicated, may hold values from -1.8 to 1.8
Outputs:
- output: bfloat16 [32768, 1024], P(('dp', 'tensor'))
- d_inputs: bfloat16 [32768, 1024], P(('dp', 'tensor'))
- grad_qkv: float32 [3, 1024, 1024], P(None, 'dp', 'tensor')
- grad_out: float32 [1024, 1024], P('tensor', 'dp')
- grad_fc1: float32 [1024, 4096], P('dp', 'tensor')
- grad_fc2: float32 [4096, 1024], P('tensor', 'dp')
- grad_norm_gain: float32 [4, 1024], replicated
- grad_norm_bias: float32 [4, 1024], replicated
- grad_head_bias: float32 [2, 1024], replicated
- grad_out_bias: float32 [2, 1024], replicated
- grad_fc1_bias: float32 [4096], replicated
The draws below stay inside these ranges and needn't reach their ends.
Inputs may be any that keep to these rules, and one draw needn't show every extreme that they name: `segment_ids`: in each packed sequence the segment numbers start at 0, never fall, and every number up to the sequence's largest appears; a segment is a document or the padding at the sequence's end. A segment has at most 1024 tokens, and some segment has exactly that many.
All inputs are finite; a program needn't handle non-finite values.
Results may differ from the reference program's by a relative error of at most 0.02.
Values may be sent and summed in bfloat16 or wider, within the bound.
No kernel may reach another device: no remote copies, remote signals or barrier semaphores. Data moves between devices by JAX's collectives and lax.ppermute only.
A program may use at most 512 MiB of HBM per device.

```python
import math
import jax
import jax.numpy as jnp
import numpy as np
from jax import lax

D = 1024
HEADS = 16
HD = 64
FF = 4096
SEQ_LEN = 2048
SEQUENCES = 16
TOKENS = 32768
N_TENSOR = 2


def shard_levels(own_key, dims, split, least, top_value):
    level = 1.0
    for axis_at, parts in split:
        heights = jax.random.uniform(jax.random.fold_in(jax.random.fold_in(own_key, 6), axis_at), (parts,), jnp.float32, least / len(split), top_value / len(split))
        level = level * jnp.repeat(jnp.exp(heights), dims[axis_at] // parts).reshape((-1,) + (1,) * (len(dims) - 1 - axis_at))
    return level


def length_profile(amount, total, most, slope):
    weights = [(1 << 20) // math.isqrt(standing ** slope) + 1 for standing in range(2, amount + 1)]
    spare, counts = total - most - (amount - 1), [1] * (amount - 1)
    while spare > 0:
        candidates = [i for i in range(amount - 1) if counts[i] < most]
        whole, budget = sum([weights[i] for i in candidates]), spare
        for i in candidates:
            more = min(most - counts[i], max(1, budget * weights[i] // whole), spare)
            counts[i] = counts[i] + more
            spare = spare - more
    return np.array([most] + counts)


def ragged(rng, number_of, total, most, slope):
    if number_of == 2:
        one = jax.random.randint(rng, (), max(1, total - most), min(most, total - 1) + 1)
        return jnp.stack([one, total - one])
    tallies = jnp.asarray(length_profile(number_of, total, most, slope), jnp.int32)
    pairs = (number_of - 1) // 2
    giver, receiver = tallies[1:1 + 2 * pairs:2], tallies[2:2 + 2 * pairs:2]
    slack = jnp.minimum(giver - 1, most - receiver)
    shifted = jax.random.randint(jax.random.fold_in(rng, 1), (pairs,), 0, 1 << 20) % (slack + 1)
    tallies = tallies.at[1:1 + 2 * pairs:2].set(giver - shifted).at[2:2 + 2 * pairs:2].set(receiver + shifted)
    return tallies[jax.random.permutation(jax.random.fold_in(rng, 2), number_of)]


def noise(stream_key, shape, width, limit, cuts=(), kind=jnp.bfloat16):
    array = jax.random.normal(stream_key, shape, jnp.float32) * width
    if len(cuts) > 0:
        array = shard_levels(stream_key, shape, cuts, -0.22, 0.18) * array
    return jnp.clip(array, min=-limit, max=limit).astype(kind)


def setup_inputs(seed: int = 0) -> dict:
    arg_keys = jax.random.split(jax.random.key(seed), 13)
    inputs = noise(arg_keys[0], (TOKENS, D), 1.0, 6.0, ((0, 16),))
    cotangent = noise(arg_keys[1], (TOKENS, D), 1.0, 6.0, ((0, 16),))
    segment_ids = jax.vmap(lambda own: jnp.searchsorted(jnp.cumsum(ragged(own, max(4, SEQ_LEN // 256), SEQ_LEN, SEQ_LEN // 2, 1)), jnp.arange(SEQ_LEN), side="right"))(jax.random.split(arg_keys[2], SEQUENCES)).reshape((SEQUENCES, SEQ_LEN)).astype(jnp.int32)
    w_qkv = noise(arg_keys[3], (3, D, D), D ** -0.5, 0.1875, ((1, 16), (2, 2)), jnp.float32)
    w_out = noise(arg_keys[4], (D, D), (max(1, D // 64)) ** -0.5, 1.5, ((0, 2), (1, 16)), jnp.float32)
    w_fc1 = noise(arg_keys[5], (D, FF), D ** -0.5, 0.1875, ((0, 16), (1, 2)), jnp.float32)
    w_fc2 = noise(arg_keys[6], (FF, D), FF ** -0.5, 0.09375, ((0, 2), (1, 16)), jnp.float32)
    norm_gain = jnp.clip(1.0 + 0.1 * jax.random.normal(arg_keys[7], (4, D), jnp.float32), 0.5, 1.5)
    norm_bias = noise(arg_keys[8], (4, D), 0.3, 1.8, (), jnp.float32)
    head_bias = noise(arg_keys[9], (2, D), 0.5, 3.0, (), jnp.float32)
    out_bias = noise(arg_keys[10], (2, D), 0.2, 1.2, (), jnp.float32)
    fc1_bias = noise(arg_keys[11], (FF,), 0.3, 1.8, (), jnp.float32)
    return {"inputs": inputs, "cotangent": cotangent, "segment_ids": segment_ids, "w_qkv": w_qkv, "w_out": w_out, "w_fc1": w_fc1, "w_fc2": w_fc2, "norm_gain": norm_gain, "norm_bias": norm_bias, "head_bias": head_bias, "out_bias": out_bias, "fc1_bias": fc1_bias}


@jax.custom_vjp
def low(v):
    return lax.optimization_barrier(v.astype(jnp.bfloat16)).astype(jnp.float32)

@jax.custom_vjp
def low_back(v):
    return v

def low_keep(v):
    return (low(v), None)

def low_pass(kept, grad):
    return (grad,)

def back_keep(v):
    return (v, None)

def back_low(kept, grad):
    return (low(grad),)
low.defvjp(low_keep, low_pass)
low_back.defvjp(back_keep, back_low)
eps_norm = 1e-05
query_scale = 0.00390625
relax_alpha = 32.0
masked_score = -1000000000.0

def exact_dot(left_side, right_side):
    return jnp.dot(left_side, right_side, precision=lax.Precision.HIGHEST)

def layer_norm(values, gain_row, shift_row):
    row_mean = lax.optimization_barrier(jnp.mean(values, axis=-1, keepdims=True))
    centered = values - row_mean
    variance = lax.optimization_barrier(jnp.mean(centered * centered, axis=-1, keepdims=True))
    return centered * lax.rsqrt(variance + eps_norm) * gain_row + shift_row

def attend_head(queries, key_rows, values, segment):
    positions = jnp.arange(segment.shape[0], dtype=jnp.int32)
    allowed = (segment[:, None] == segment[None, :]) & (positions[None, :] <= positions[:, None])
    scores = low_back(exact_dot(queries * query_scale, key_rows.T))
    masked = jnp.where(allowed, scores, masked_score)
    row_peak = lax.optimization_barrier(jnp.max(masked, axis=1, keepdims=True))
    exponent = jnp.exp(relax_alpha * (masked - row_peak))
    probability = low(exponent / lax.optimization_barrier(jnp.sum(exponent, axis=1, keepdims=True)))
    return exact_dot(probability, values)

def split_heads(matrix):
    return matrix.reshape(SEQ_LEN, HEADS, HD).transpose(1, 0, 2)

def layer_forward(tokens_in, segment, w_qkv, w_out, w_fc1, w_fc2, norm_gain, norm_bias, head_bias, out_bias, fc1_bias):
    group_count = N_TENSOR
    group_width = D // group_count
    hidden_width = FF // group_count
    w_attn = low(w_qkv)
    w_proj = low(w_out)
    w_up = low(w_fc1)
    w_down = low(w_fc2)
    normed_in = low(layer_norm(tokens_in, norm_gain[0], norm_bias[0]))
    query_parts, key_parts, value_parts = ([], [], [])
    for group_index in range(group_count):
        columns = slice(group_index * group_width, (group_index + 1) * group_width)
        member = low_back(normed_in)
        query_parts.append(exact_dot(member, w_attn[0][:, columns]) + head_bias[0][columns])
        key_parts.append(exact_dot(member, w_attn[1][:, columns]))
        value_parts.append(exact_dot(member, w_attn[2][:, columns]) + head_bias[1][columns])
    queries = low_back(low(jnp.concatenate(query_parts, axis=1)))
    key_rows = low_back(low(jnp.concatenate(key_parts, axis=1)))
    values = low_back(low(jnp.concatenate(value_parts, axis=1)))
    checked = jax.checkpoint(attend_head)
    attended = lax.map(lambda head_trio: checked(head_trio[0], head_trio[1], head_trio[2], segment), (split_heads(queries), split_heads(key_rows), split_heads(values)))
    attended = low_back(low(attended.transpose(1, 0, 2).reshape(SEQ_LEN, D)))
    attn_sum = jnp.zeros((SEQ_LEN, D), jnp.float32)
    for group_index in range(group_count):
        columns = slice(group_index * group_width, (group_index + 1) * group_width)
        attn_sum = attn_sum + low(exact_dot(attended[:, columns], w_proj[columns, :]))
    attn_rows = low_back(attn_sum + out_bias[0])
    resid = tokens_in + layer_norm(attn_rows, norm_gain[1], norm_bias[1])
    normed_mid = low(layer_norm(resid, norm_gain[2], norm_bias[2]))
    mlp_sum = jnp.zeros((SEQ_LEN, D), jnp.float32)
    for group_index in range(group_count):
        hidden_cols = slice(group_index * hidden_width, (group_index + 1) * hidden_width)
        member = low_back(normed_mid)
        pre_act = low_back(exact_dot(member, w_up[:, hidden_cols]) + fc1_bias[hidden_cols])
        activated = low(jax.nn.gelu(pre_act, approximate=True))
        mlp_sum = mlp_sum + low(exact_dot(activated, w_down[hidden_cols, :]))
    mlp_rows = low_back(mlp_sum + out_bias[1])
    return resid + layer_norm(mlp_rows, norm_gain[3], norm_bias[3])

def reference(inputs, cotangent, segment_ids, w_qkv, w_out, w_fc1, w_fc2, norm_gain, norm_bias, head_bias, out_bias, fc1_bias):
    seq_inputs = inputs.astype(jnp.float32).reshape(SEQUENCES, SEQ_LEN, D)
    seq_cots = cotangent.astype(jnp.float32).reshape(SEQUENCES, SEQ_LEN, D)
    params = (w_qkv, w_out, w_fc1, w_fc2, norm_gain, norm_bias, head_bias, out_bias, fc1_bias)

    def seq_step(totals, packed):
        seq_in, cot_seq, segment = packed
        layer_out, pull_back = jax.vjp(lambda tokens_in, *weights_all: layer_forward(tokens_in, segment, *weights_all), seq_in, *params)
        grads_all = pull_back(cot_seq)
        totals = tuple((first_grad + second_grad for first_grad, second_grad in zip(totals, grads_all[1:])))
        return (totals, (layer_out.astype(jnp.bfloat16), grads_all[0].astype(jnp.bfloat16)))
    start_totals = tuple((jnp.zeros(param.shape, jnp.float32) for param in params))
    totals, (outputs, d_inputs) = lax.scan(seq_step, start_totals, (seq_inputs, seq_cots, segment_ids))
    return (outputs.reshape(TOKENS, D), d_inputs.reshape(TOKENS, D), totals[0], totals[1], totals[2], totals[3], totals[4], totals[5], totals[6], totals[7], totals[8])
```

```python
import functools
import math

import jax
import jax.numpy as jnp
from jax import lax
from jax.experimental import pallas as pl
from jax.experimental.pallas import tpu as pltpu
from jax.sharding import PartitionSpec as P

HD = 64
QB = 256
KB = 256
MAX_SEGMENT = 1024
max_chunks = MAX_SEGMENT // KB + 1
SCORE_SCALE = 0.125 * math.log2(math.e)
NEG = -1e30
EPS = 1e-05
BF16 = jnp.bfloat16
F32 = jnp.float32
NT = (((1,), (1,)), ((), ()))
NN = (((1,), (0,)), ((), ()))
TN = (((0,), (0,)), ((), ()))

def dot(a, b, dims):
    return lax.dot_general(a, b, dims, preferred_element_type=jnp.float32)


def split_pair(block):
    lane = lax.broadcasted_iota(jnp.int32, block.shape, 1)
    zero = jnp.zeros_like(block)
    return (jnp.where(lane < HD, block, zero), jnp.where(lane >= HD, block, zero))


def fwd_kernel(pairs, lo_ref, off_ref, q_ref, k_ref, v_ref, start_ref, o_ref, l_ref, vt_ref):
    step = pl.program_id(1)
    block = off_ref[0] + step

    @pl.when(step == 0)
    def _():
        vt_ref[...] = v_ref[...].T

    pair_step = math.gcd(pairs, 4)
    row_start = start_ref[...]
    query_pos = block * QB + lax.broadcasted_iota(jnp.int32, (1, QB), 1)
    first = lo_ref[pl.program_id(0), block]
    count = block + 1 - first
    base = pl.multiple_of(first * KB, KB)

    for chunks in range(1, max_chunks + 1):

        @pl.when(count == chunks)
        def _(size=chunks * KB):
            window = pl.ds(base, size)
            key_pos = lax.broadcasted_iota(jnp.int32, (size, QB), 0) + base
            ok = (key_pos >= row_start) & (key_pos <= query_pos)

            def body(group, _):
                for sub in range(pair_step):
                    pair = group * pair_step + sub
                    cols = pl.ds(pl.multiple_of(pair * 128, 128), 128)
                    q_heads = split_pair(q_ref[:, cols])
                    keys = k_ref[window, cols]
                    outs = []
                    for h in range(2):
                        s = jnp.where(ok, dot(keys, q_heads[h], NT) * SCORE_SCALE, NEG)
                        peak = jnp.max(s, axis=0, keepdims=True)
                        p = jnp.exp2(s - peak)
                        total = jnp.sum(p, axis=0, keepdims=True)
                        vt = vt_ref[pl.ds(pl.multiple_of(pair * 128 + h * HD, HD), HD), window]
                        outs.append(dot(vt, p.astype(jnp.bfloat16), NN) / total)
                        l_ref[pl.ds(2 * pair + h, 1), :] = peak + jnp.log2(total)
                    o_ref[:, cols] = jnp.concatenate(outs, axis=0).T.astype(jnp.bfloat16)
                return 0

            lax.fori_loop(0, pairs // pair_step, body, 0)


def attention_forward(qkv, starts, lo, offset, blocks):
    seqs, length = starts.shape
    width = qkv.shape[1] // 3
    heads, pairs = width // HD, width // 128
    nq = length // QB
    grid_spec = pltpu.PrefetchScalarGridSpec(
        num_scalar_prefetch=2,
        grid=(seqs, blocks),
        in_specs=[
            pl.BlockSpec((QB, width), lambda s, b, lo, off: (s * nq + off[0] + b, 0)),
            pl.BlockSpec((length, width), lambda s, b, lo, off: (s, 1)),
            pl.BlockSpec((length, width), lambda s, b, lo, off: (s, 2)),
            pl.BlockSpec((None, 1, QB), lambda s, b, lo, off: (s, 0, off[0] + b)),
        ],
        out_specs=[
            pl.BlockSpec((QB, width), lambda s, b, lo, off: (s * blocks + b, 0)),
            pl.BlockSpec((None, heads, QB), lambda s, b, lo, off: (s, 0, b)),
        ],
        scratch_shapes=[pltpu.VMEM((width, length), jnp.bfloat16)],
    )
    rows = seqs * blocks * QB
    return pl.pallas_call(
        functools.partial(fwd_kernel, pairs),
        grid_spec=grid_spec,
        out_shape=(
            jax.ShapeDtypeStruct((rows, width), jnp.bfloat16),
            jax.ShapeDtypeStruct((seqs, heads, blocks * QB), jnp.float32),
        ),
        compiler_params=pltpu.CompilerParams(
            dimension_semantics=("arbitrary", "arbitrary"), vmem_limit_bytes=48 << 20
        ),
        cost_estimate=pl.CostEstimate(
            flops=4 * rows * 640 * width, bytes_accessed=8 * rows * width, transcendentals=rows * heads * 640
        ),
        name="attention_forward",
    )(lo, offset, qkv, qkv, qkv, starts[:, None, :])


def bwd_kernel(pairs, lo_ref, q_ref, k_ref, v_ref, o_ref, do_ref, l_ref, start_ref, out_ref, kt_ref, dk_ref, dv_ref):
    block = pl.program_id(1)
    width = pairs * 128

    @pl.when(block == 0)
    def _():
        kt_ref[...] = k_ref[...].T
        dk_ref[...] = jnp.zeros_like(dk_ref)
        dv_ref[...] = jnp.zeros_like(dv_ref)

    row_start = start_ref[...]
    query_pos = block * QB + lax.broadcasted_iota(jnp.int32, (1, QB), 1)
    key_iota = lax.broadcasted_iota(jnp.int32, (KB, QB), 0)
    first = lo_ref[pl.program_id(0), block]
    last = (block + 1) * (QB // KB)
    rows = pl.ds(pl.multiple_of(block * QB, QB), QB)
    for pair in range(pairs):
        cols = slice(pair * 128, (pair + 1) * 128)
        q_heads = split_pair(q_ref[:, cols])
        g_pair = do_ref[:, cols]
        g_heads = split_pair(g_pair)
        prod = (g_pair.astype(jnp.float32) * o_ref[:, cols].astype(jnp.float32)).T
        deltas = [jnp.sum(prod[h * HD : (h + 1) * HD], axis=0, keepdims=True) for h in range(2)]
        lses = [l_ref[2 * pair + h : 2 * pair + h + 1, :] for h in range(2)]

        def chunk(j, carry):
            base = pl.multiple_of(j * KB, KB)
            window = pl.ds(base, KB)
            keys = k_ref[window, cols]
            vals = v_ref[window, cols]
            key_pos = key_iota + base
            ok = (key_pos >= row_start) & (key_pos <= query_pos)
            new = []
            dv = dv_ref[window, cols]
            dk = dk_ref[window, cols]
            for h in range(2):
                s = jnp.where(ok, dot(keys, q_heads[h], NT) * SCORE_SCALE, NEG)
                p = jnp.exp2(s - lses[h])
                dp = dot(vals, g_heads[h], NT)
                ds = (p * (dp - deltas[h])).astype(jnp.bfloat16)
                dv = dv + dot(p.astype(jnp.bfloat16), g_heads[h], NN)
                dk = dk + dot(ds, q_heads[h], NN)
                kt = kt_ref[pair * 128 + h * HD : pair * 128 + (h + 1) * HD, window]
                new.append(carry[h] + dot(kt, ds, NN))
            dv_ref[window, cols] = dv
            dk_ref[window, cols] = dk
            return tuple(new)

        dq = lax.fori_loop(
            first, last, chunk, tuple(jnp.zeros((HD, QB), jnp.float32) for _ in range(2))
        )
        out_ref[rows, cols] = (jnp.concatenate(dq, axis=0) * 0.125).T.astype(jnp.bfloat16)

    @pl.when(block == pl.num_programs(1) - 1)
    def _():
        out_ref[:, width : 2 * width] = (dk_ref[...] * 0.125).astype(jnp.bfloat16)
        out_ref[:, 2 * width :] = dv_ref[...].astype(jnp.bfloat16)


def attention_backward(qkv, o, d_o, lse, starts, lo):
    seqs, length = starts.shape
    width = qkv.shape[1] // 3
    heads, pairs = width // HD, width // 128
    nq = length // QB
    row = lambda s, b, lo: (s * nq + b, 0)
    grid_spec = pltpu.PrefetchScalarGridSpec(
        num_scalar_prefetch=1,
        grid=(seqs, nq),
        in_specs=[
            pl.BlockSpec((QB, width), row),
            pl.BlockSpec((length, width), lambda s, b, lo: (s, 1)),
            pl.BlockSpec((length, width), lambda s, b, lo: (s, 2)),
            pl.BlockSpec((QB, width), row),
            pl.BlockSpec((QB, width), row),
            pl.BlockSpec((None, heads, QB), lambda s, b, lo: (s, 0, b)),
            pl.BlockSpec((None, 1, QB), lambda s, b, lo: (s, 0, b)),
        ],
        out_specs=pl.BlockSpec((length, 3 * width), lambda s, b, lo: (s, 0)),
        scratch_shapes=[
            pltpu.VMEM((width, length), jnp.bfloat16),
            pltpu.VMEM((length, width), jnp.float32),
            pltpu.VMEM((length, width), jnp.float32),
        ],
    )
    rows = seqs * length
    return pl.pallas_call(
        functools.partial(bwd_kernel, pairs),
        grid_spec=grid_spec,
        out_shape=jax.ShapeDtypeStruct((rows, 3 * width), jnp.bfloat16),
        compiler_params=pltpu.CompilerParams(
            dimension_semantics=("arbitrary", "arbitrary"), vmem_limit_bytes=56 << 20
        ),
        cost_estimate=pl.CostEstimate(
            flops=10 * rows * 640 * width, bytes_accessed=16 * rows * width, transcendentals=rows * heads * 640
        ),
        name="attention_backward",
    )(lo, qkv, qkv, qkv, o, d_o, lse, starts[:, None, :])


def segment_bounds(segment_ids):
    starts = jnp.sum((segment_ids[:, None, :] < segment_ids[:, :, None]).astype(jnp.int32), axis=2)
    return starts, starts[:, ::QB] // KB


def stats(values):
    mean = jnp.mean(values, axis=-1, keepdims=True)
    centered = values - mean
    scale = lax.rsqrt(jnp.mean(centered * centered, axis=-1, keepdims=True) + EPS)
    return centered * scale, scale


def norm_back(normed, scale, gain_row, grad_rows):
    inner = grad_rows * gain_row
    return scale * (
        inner
        - jnp.mean(inner, axis=-1, keepdims=True)
        - normed * jnp.mean(inner * normed, axis=-1, keepdims=True)
    )


def gelu_pair(z):
    c = math.sqrt(2.0 / math.pi)
    t = jnp.tanh(c * (z + 0.044715 * z * z * z))
    value = 0.5 * z * (1.0 + t)
    slope = 0.5 * (1.0 + t) + 0.5 * z * (1.0 - t * t) * (c * (1.0 + 3 * 0.044715 * z * z))
    return value, slope


NZ, NX, NC = 4, 2, 2


def core_pairs():
    return [(i, i ^ 1) for i in range(NZ * NX * NC)]


def x_pairs():
    return [(i, i ^ 2) for i in range(NZ * NX * NC)]


def z_pairs(shift):
    return [(i, (i + shift * NX * NC) % (NZ * NX * NC)) for i in range(NZ * NX * NC)]


Y_PAIRS = [(0, 1), (1, 0)]


def swap_core(a):
    return lax.ppermute(a, "dp", core_pairs())


def swap_x(a):
    return lax.ppermute(a, "dp", x_pairs())


def swap_y(a):
    return lax.ppermute(a, "tensor", Y_PAIRS)


def assemble_kernel(pos_ref, *refs):
    out_ref = refs[-1]
    z, x, c = pos_ref[0], pos_ref[1], pos_ref[2]
    for n, ref in enumerate(refs[:-1]):
        dx, dc = n % 2, n // 2
        for k in range(NZ):
            out_ref[lax.rem(z - k + NZ, NZ), lax.bitwise_xor(x, dx), lax.bitwise_xor(c, dc)] = ref[k]


def assemble(position, pieces):
    _, rows, width = pieces[0].shape
    block = math.gcd(width, 512)
    out = pl.pallas_call(
        assemble_kernel,
        grid_spec=pltpu.PrefetchScalarGridSpec(
            num_scalar_prefetch=1,
            grid=(width // block,),
            in_specs=[pl.BlockSpec((NZ, rows, block), lambda j, pos: (0, 0, j))] * 4,
            out_specs=pl.BlockSpec((NZ, NX, NC, rows, block), lambda j, pos: (0, 0, 0, 0, j)),
        ),
        out_shape=jax.ShapeDtypeStruct((NZ, NX, NC, rows, width), BF16),
        compiler_params=pltpu.CompilerParams(
            dimension_semantics=("arbitrary",), vmem_limit_bytes=32 << 20
        ),
        cost_estimate=pl.CostEstimate(
            flops=0, bytes_accessed=2 * 16 * rows * width * 2, transcendentals=0
        ),
        name="assemble",
    )(position, *pieces)
    return out.reshape(NZ * NX * NC * rows, width)


def gather_z(shard):
    return jnp.stack([shard] + [lax.ppermute(shard, "dp", z_pairs(k)) for k in range(1, NZ)])


def finish_gather(position, column, from_x):
    mine = [column, from_x]
    return assemble(position, mine + [swap_core(a) for a in mine])


def gather_own(position, shard):
    column = gather_z(shard)
    return finish_gather(position, column, swap_x(column))


def gather_both(position, shard, y_first):
    column = gather_z(shard)
    other = swap_y(column)
    own_x = swap_x(column)
    other_x = swap_x(other) if y_first else swap_y(own_x)
    return [finish_gather(position, column, own_x), finish_gather(position, other, other_x)]


def reduce_rows(z, x, c, grads):
    wide = []
    for g in grads:
        parts = g.reshape(NZ, NX, NC, g.shape[0] // (NZ * NX * NC), g.shape[1])
        there = swap_core(lax.dynamic_index_in_dim(parts, 1 - c, 2, keepdims=False))
        here = lax.dynamic_index_in_dim(parts, c, 2, keepdims=False)
        wide.append((here.astype(F32) + there.astype(F32)).astype(BF16))
    mid = []
    for h in wide:
        there = swap_x(lax.dynamic_index_in_dim(h, 1 - x, 1, keepdims=False))
        here = lax.dynamic_index_in_dim(h, x, 1, keepdims=False)
        mid.append((here.astype(F32) + there.astype(F32)).astype(BF16))
    total = mid[0]
    if len(mid) == 2:
        total = (total.astype(F32) + swap_y(mid[1]).astype(F32)).astype(BF16)
    out = lax.dynamic_index_in_dim(total, z, 0, keepdims=False).astype(F32)
    for k in range(1, NZ):
        piece = lax.dynamic_index_in_dim(total, lax.rem(z + k, NZ), 0, keepdims=False)
        out = out + lax.ppermute(piece, "dp", z_pairs(k)).astype(F32)
    return out


def sum_everywhere(vector, over_tensor=True):
    vector = vector + swap_core(vector)
    vector = vector + swap_x(vector)
    if over_tensor:
        vector = vector + swap_y(vector)
    size = NZ * NX * NC
    near = [(i, i ^ 4) for i in range(size)]
    far = [(i, i ^ 8) for i in range(size)]
    vector = vector + lax.ppermute(vector, "dp", near)
    return vector + lax.ppermute(vector, "dp", far)


class Staged:
    def __init__(self):
        index = lax.axis_index("dp")
        self.z, self.x, self.c = index // 4, (index // 2) % 2, index % 2
        self.position = jnp.stack([self.z, self.x, self.c]).astype(jnp.int32)

    def gather_own(self, shard):
        return gather_own(self.position, shard)

    def gather_groups(self, shard, y_first):
        return gather_both(self.position, shard, y_first)

    def reduce_own(self, grad):
        return reduce_rows(self.z, self.x, self.c, [grad])

    def reduce_groups(self, grads):
        return reduce_rows(self.z, self.x, self.c, grads)

    def exchange(self, parts):
        return [parts[0], swap_y(parts[1])]

    def total(self, vector, over_tensor=True):
        return sum_everywhere(vector, over_tensor)


class Plain:
    def __init__(self):
        self.n = lax.axis_size("tensor")
        self.rank = lax.axis_index("tensor")

    def gather_own(self, shard):
        return lax.all_gather(shard, "dp", axis=0, tiled=True)

    def gather_groups(self, shard, y_first):
        own = lax.all_gather(shard, "dp", axis=0, tiled=True)
        every = lax.all_gather(own, "tensor", axis=0)
        return [
            lax.dynamic_index_in_dim(every, (self.rank + g) % self.n, 0, keepdims=False)
            for g in range(self.n)
        ]

    def reduce_own(self, grad):
        return lax.psum_scatter(grad, "dp", scatter_dimension=0, tiled=True).astype(F32)

    def absolute(self, parts):
        stacked = jnp.stack(parts)
        order = (jnp.arange(self.n) - self.rank) % self.n
        return jnp.take(stacked, order, axis=0)

    def reduce_groups(self, grads):
        own = lax.psum_scatter(self.absolute(grads), "tensor", scatter_dimension=0, tiled=True)
        return lax.psum_scatter(own[0], "dp", scatter_dimension=0, tiled=True).astype(F32)

    def exchange(self, parts):
        got = lax.all_to_all(self.absolute(parts), "tensor", 0, 0, tiled=True)
        return [
            lax.dynamic_index_in_dim(got, (self.rank + g) % self.n, 0, keepdims=False)
            for g in range(self.n)
        ]

    def total(self, vector, over_tensor=True):
        return lax.psum(vector, ("dp", "tensor") if over_tensor else "dp")


def per_device(
    staged,
    inputs,
    cotangent,
    segment_ids,
    w_qkv,
    w_out,
    w_fc1,
    w_fc2,
    norm_gain,
    norm_bias,
    head_bias,
    out_bias,
    fc1_bias,
):
    n = lax.axis_size("tensor")
    rank = lax.axis_index("tensor")
    comm = Staged() if staged else Plain()
    tokens, features = inputs.shape
    seqs, length = segment_ids.shape
    own_rows = tokens // n
    width = w_qkv.shape[2]
    hidden = w_fc1.shape[1]

    def group_slice(array, g, size, axis=0):
        return lax.dynamic_slice_in_dim(array, ((rank + g) % n) * size, size, axis)

    shard_qkv = jnp.concatenate([w_qkv[0], w_qkv[1], w_qkv[2]], axis=1).astype(BF16)
    weight_qkv = comm.gather_own(shard_qkv)
    out_groups = comm.gather_groups(w_out.T.astype(BF16), True)
    up_groups = comm.gather_groups(w_fc1.astype(BF16), True)
    down_groups = comm.gather_groups(w_fc2.T.astype(BF16), False)

    wide = inputs.astype(F32)
    normed0, scale0 = stats(wide)
    u1 = (normed0 * norm_gain[0] + norm_bias[0]).astype(BF16)
    heads_bias = group_slice(head_bias, 0, width, 1)
    qkv_bias = jnp.concatenate([heads_bias[0], jnp.zeros((width,), F32), heads_bias[1]])
    qkv = (dot(u1, weight_qkv, NN) + qkv_bias).astype(BF16)

    starts, lo = segment_bounds(segment_ids)
    blocks = length // QB
    if staged and seqs == 1:
        half = blocks // 2
        there = jnp.full((1,), (1 - rank) * half, jnp.int32)
        here = jnp.full((1,), rank * half, jnp.int32)
        o_there, lse_there = attention_forward(qkv, starts, lo, there, half)
        o_here, lse_here = attention_forward(qkv, starts, lo, here, half)
        o_parts = [o_here, o_there]
        first = rank == 0
        o_all = jnp.concatenate(
            [jnp.where(first, o_here, o_there), jnp.where(first, o_there, o_here)], axis=0
        )
        lse = jnp.concatenate(
            [jnp.where(first, lse_here, lse_there), jnp.where(first, lse_there, lse_here)], axis=2
        )
    else:
        o_all, lse = attention_forward(qkv, starts, lo, jnp.zeros((1,), jnp.int32), blocks)
        o_parts = [group_slice(o_all, g, own_rows) for g in range(n)]
    o_groups = comm.exchange(o_parts)

    def group_sum(terms):
        return sum(t.astype(BF16).astype(F32) for t in terms)

    attn = group_sum([dot(o, w, NT) for o, w in zip(o_groups, out_groups)]) + out_bias[0]
    mine = group_slice(inputs, 0, own_rows).astype(F32)
    normed1, scale1 = stats(attn)
    resid = mine + normed1 * norm_gain[1] + norm_bias[1]
    normed2, scale2 = stats(resid)
    u2 = (normed2 * norm_gain[2] + norm_bias[2]).astype(BF16)

    act_groups, slope_groups, mlp_terms = [], [], []
    for g in range(n):
        pre = dot(u2, up_groups[g], NN) + group_slice(fc1_bias, g, hidden)
        act, slope = gelu_pair(pre)
        act_groups.append(act.astype(BF16))
        slope_groups.append(pre)
        mlp_terms.append(dot(act_groups[g], down_groups[g], NT))
    mlp = group_sum(mlp_terms) + out_bias[1]
    normed3, scale3 = stats(mlp)
    output = (resid + normed3 * norm_gain[3] + norm_bias[3]).astype(BF16)

    dy = group_slice(cotangent, 0, own_rows).astype(F32)
    d_mlp = norm_back(normed3, scale3, norm_gain[3], dy).astype(BF16)
    gain3, shift3 = jnp.sum(normed3 * dy, axis=0), jnp.sum(dy, axis=0)
    bias_mlp = jnp.sum(d_mlp.astype(F32), axis=0)

    grad_down = comm.reduce_groups([dot(d_mlp, act, TN).astype(BF16) for act in act_groups])
    d_pre_groups = [
        (gelu_pair(slope_groups[g])[1] * dot(d_mlp, down_groups[g], NN)).astype(BF16) for g in range(n)
    ]
    d_u2 = group_sum([dot(d_pre, w, NT) for d_pre, w in zip(d_pre_groups, up_groups)])
    grad_up = comm.reduce_groups([dot(u2, d_pre, TN).astype(BF16) for d_pre in d_pre_groups])
    bias_hidden = [jnp.sum(d_pre.astype(F32), axis=0) for d_pre in d_pre_groups]

    gain2, shift2 = jnp.sum(normed2 * d_u2, axis=0), jnp.sum(d_u2, axis=0)
    d_resid = dy + norm_back(normed2, scale2, norm_gain[2], d_u2)
    gain1, shift1 = jnp.sum(normed1 * d_resid, axis=0), jnp.sum(d_resid, axis=0)
    d_attn = norm_back(normed1, scale1, norm_gain[1], d_resid).astype(BF16)
    bias_attn = jnp.sum(d_attn.astype(F32), axis=0)

    d_o_parts = [dot(d_attn, w, NN).astype(BF16) for w in out_groups]
    d_o_groups = comm.exchange(d_o_parts)
    grad_out = comm.reduce_groups([dot(d_attn, o, TN).astype(BF16) for o in o_groups])
    if n == 2:
        first = rank == 0
        d_o = jnp.concatenate(
            [
                jnp.where(first, d_o_groups[0], d_o_groups[1]),
                jnp.where(first, d_o_groups[1], d_o_groups[0]),
            ],
            axis=0,
        )
    else:
        d_o = jnp.take(jnp.stack(d_o_groups), (jnp.arange(n) - rank) % n, axis=0).reshape(tokens, width)

    d_qkv = attention_backward(qkv, o_all, d_o, lse, starts, lo)

    d_u1_parts = [
        dot(group_slice(d_qkv, g, own_rows), weight_qkv, NT).astype(BF16) for g in reversed(range(n))
    ][::-1]
    d_u1 = group_sum(comm.exchange(d_u1_parts))
    grad_qkv = comm.reduce_own(dot(u1, d_qkv, TN).astype(BF16))
    gain0 = shift0 = 0.0
    for g in range(n):
        part = d_u1_parts[g].astype(F32)
        gain0 = gain0 + jnp.sum(group_slice(normed0, g, own_rows) * part, axis=0)
        shift0 = shift0 + jnp.sum(part, axis=0)
    head_terms = jnp.sum(d_qkv.astype(F32), axis=0)

    own_normed0 = group_slice(normed0, 0, own_rows)
    own_scale0 = group_slice(scale0, 0, own_rows)
    d_inputs = (d_resid + norm_back(own_normed0, own_scale0, norm_gain[0], d_u1)).astype(BF16)

    def place(groups, like, axis):
        full = jnp.zeros(like.shape, F32)
        for g, part in enumerate(groups):
            at = ((rank + g) % n) * part.shape[axis]
            full = lax.dynamic_update_slice_in_dim(full, part, at, axis)
        return full

    early = jnp.concatenate(
        [
            jnp.stack([gain1, gain2, gain3, shift1, shift2, shift3, bias_attn, bias_mlp]).reshape(-1),
            place(bias_hidden, fc1_bias, 0),
        ]
    ).reshape(-1, 1024)
    early = comm.total(early)
    head_full = place([jnp.stack([head_terms[:width], head_terms[2 * width :]])], head_bias, 1)
    late = comm.total(jnp.concatenate([gain0[None], shift0[None], head_full]))
    grad_gain = jnp.concatenate([late[0:1], early[0:3]])
    grad_shift = jnp.concatenate([late[1:2], early[3:6]])
    grad_qkv = jnp.stack([grad_qkv[:, i * width : (i + 1) * width] for i in range(3)])
    return (
        output,
        d_inputs,
        grad_qkv,
        grad_out.T,
        grad_up,
        grad_down.T,
        grad_gain,
        grad_shift,
        late[2:4],
        early[6:8],
        early[8:].reshape(-1),
    )


def solution(mesh):
    staged = mesh.shape["dp"] == NZ * NX * NC and mesh.shape["tensor"] == 2
    return jax.shard_map(
        functools.partial(per_device, staged),
        mesh=mesh,
        in_specs=(
            P("dp", None),
            P("dp", None),
            P("dp", None),
            P(None, "dp", "tensor"),
            P("tensor", "dp"),
            P("dp", "tensor"),
            P("tensor", "dp"),
            P(),
            P(),
            P(),
            P(),
            P(),
        ),
        out_specs=(
            P(("dp", "tensor"), None),
            P(("dp", "tensor"), None),
            P(None, "dp", "tensor"),
            P("tensor", "dp"),
            P("dp", "tensor"),
            P("tensor", "dp"),
            P(),
            P(),
            P(),
            P(),
            P(),
        ),
        check_vma=False,
    )
```

```python
import functools
import math

import jax
import jax.numpy as jnp
from jax import lax
from jax.experimental import pallas as pl
from jax.experimental.pallas import tpu as pltpu
from jax.sharding import PartitionSpec as P

HD = 64
QB = 256
KB = 256
MAX_SEGMENT = 1024
max_chunks = MAX_SEGMENT // KB + 1
SCORE_SCALE = 0.125 * math.log2(math.e)
NEG = -1e30
EPS = 1e-05
BF16 = jnp.bfloat16
F32 = jnp.float32
NT = (((1,), (1,)), ((), ()))
NN = (((1,), (0,)), ((), ()))
TN = (((0,), (0,)), ((), ()))

def dot(a, b, dims):
    return lax.dot_general(a, b, dims, preferred_element_type=jnp.float32)


def split_pair(block):
    lane = lax.broadcasted_iota(jnp.int32, block.shape, 1)
    zero = jnp.zeros_like(block)
    return (jnp.where(lane < HD, block, zero), jnp.where(lane >= HD, block, zero))


def fwd_kernel(pairs, lo_ref, off_ref, q_ref, k_ref, v_ref, start_ref, o_ref, l_ref, vt_ref):
    step = pl.program_id(2)
    block = off_ref[0] + step

    @pl.when(step == 0)
    def _():
        vt_ref[...] = v_ref[...].T

    pair_step = math.gcd(pairs, 4)
    row_start = start_ref[...]
    query_pos = block * QB + lax.broadcasted_iota(jnp.int32, (1, QB), 1)
    first = lo_ref[pl.program_id(0), block]
    count = block + 1 - first
    base = pl.multiple_of(first * KB, KB)

    for chunks in range(1, max_chunks + 1):

        @pl.when(count == chunks)
        def _(size=chunks * KB):
            window = pl.ds(base, size)
            key_pos = lax.broadcasted_iota(jnp.int32, (size, QB), 0) + base
            ok = (key_pos >= row_start) & (key_pos <= query_pos)
            for pair in range(pairs):
                cols = slice(pair * 128, (pair + 1) * 128)
                q_heads = split_pair(q_ref[:, cols])
                keys = k_ref[window, cols]
                outs = []
                for h in range(2):
                    s = jnp.where(ok, dot(keys, q_heads[h], NT) * SCORE_SCALE, NEG)
                    peak = jnp.max(s, axis=0, keepdims=True)
                    p = jnp.exp2(s - peak)
                    total = jnp.sum(p, axis=0, keepdims=True)
                    vt = vt_ref[pair * 128 + h * HD : pair * 128 + (h + 1) * HD, window]
                    outs.append(dot(vt, p.astype(BF16), NN) / total)
                    l_ref[2 * pair + h : 2 * pair + h + 1, :] = peak + jnp.log2(total)
                o_ref[:, cols] = jnp.concatenate(outs, axis=0).T.astype(BF16)


def attention_forward(calls, qkv, starts, lo, offset, blocks):
    seqs, length = starts.shape
    width = qkv.shape[1] // 3
    part = width // calls
    heads = part // HD
    nq = length // QB
    grid_spec = pltpu.PrefetchScalarGridSpec(
        num_scalar_prefetch=2,
        grid=(seqs, calls, blocks),
        in_specs=[
            pl.BlockSpec((QB, part), lambda s, c, b, lo, off: (s * nq + off[0] + b, 3 * c)),
            pl.BlockSpec((length, part), lambda s, c, b, lo, off: (s, 3 * c + 1)),
            pl.BlockSpec((length, part), lambda s, c, b, lo, off: (s, 3 * c + 2)),
            pl.BlockSpec((None, 1, QB), lambda s, c, b, lo, off: (s, 0, off[0] + b)),
        ],
        out_specs=[
            pl.BlockSpec((QB, part), lambda s, c, b, lo, off: (s * blocks + b, c)),
            pl.BlockSpec((None, None, heads, QB), lambda s, c, b, lo, off: (s, c, 0, b)),
        ],
        scratch_shapes=[pltpu.VMEM((part, length), BF16)],
    )
    rows = seqs * blocks * QB
    return pl.pallas_call(
        functools.partial(fwd_kernel, part // 128),
        grid_spec=grid_spec,
        out_shape=(
            jax.ShapeDtypeStruct((rows, width), BF16),
            jax.ShapeDtypeStruct((seqs, calls, heads, blocks * QB), F32),
        ),
        compiler_params=pltpu.CompilerParams(
            dimension_semantics=("arbitrary",) * 3, vmem_limit_bytes=48 << 20
        ),
        cost_estimate=pl.CostEstimate(
            flops=4 * rows * 640 * width,
            bytes_accessed=8 * rows * width,
            transcendentals=rows * width * 10,
        ),
        name="attention_forward",
    )(lo, offset, qkv, qkv, qkv, starts[:, None, :])


def bwd_kernel(pairs, halves, lo_ref, place_ref, q_ref, k_ref, v_ref, start_ref, *refs):
    o_refs, do_refs, l_refs = refs[:halves], refs[halves : 2 * halves], refs[2 * halves : 3 * halves]
    out_ref, kt_ref, dk_ref, dv_ref = refs[-4:]
    block = pl.program_id(1)
    blocks = pl.num_programs(1)
    width = pairs * 128

    @pl.when(block == 0)
    def _():
        kt_ref[...] = k_ref[...].T
        dk_ref[...] = jnp.zeros_like(dk_ref)
        dv_ref[...] = jnp.zeros_like(dv_ref)

    mine = block // (blocks // halves) == place_ref[0]

    def pick(two, index):
        if halves == 1:
            return two[0][index]
        return jnp.where(mine, two[0][index], two[1][index])

    row_start = start_ref[...]
    query_pos = block * QB + lax.broadcasted_iota(jnp.int32, (1, QB), 1)
    key_iota = lax.broadcasted_iota(jnp.int32, (KB, QB), 0)
    first = lo_ref[pl.program_id(0), block]
    last = (block + 1) * (QB // KB)
    rows = pl.ds(pl.multiple_of(block * QB, QB), QB)
    every = slice(None)
    for pair in range(pairs):
        cols = slice(pair * 128, (pair + 1) * 128)
        q_heads = split_pair(q_ref[:, cols])
        g_pair = pick(do_refs, (every, cols))
        g_heads = split_pair(g_pair)
        prod = (g_pair.astype(F32) * pick(o_refs, (every, cols)).astype(F32)).T
        deltas = [jnp.sum(prod[h * HD : (h + 1) * HD], axis=0, keepdims=True) for h in range(2)]
        lses = [pick(l_refs, (slice(2 * pair + h, 2 * pair + h + 1), every)) for h in range(2)]

        def chunk(j, carry):
            base = pl.multiple_of(j * KB, KB)
            window = pl.ds(base, KB)
            keys = k_ref[window, cols]
            vals = v_ref[window, cols]
            key_pos = key_iota + base
            ok = (key_pos >= row_start) & (key_pos <= query_pos)
            new = []
            dv = dv_ref[window, cols]
            dk = dk_ref[window, cols]
            for h in range(2):
                s = jnp.where(ok, dot(keys, q_heads[h], NT) * SCORE_SCALE, NEG)
                p = jnp.exp2(s - lses[h])
                dp = dot(vals, g_heads[h], NT)
                ds = (p * (dp - deltas[h])).astype(BF16)
                dv = dv + dot(p.astype(BF16), g_heads[h], NN)
                dk = dk + dot(ds, q_heads[h], NN)
                kt = kt_ref[pair * 128 + h * HD : pair * 128 + (h + 1) * HD, window]
                new.append(carry[h] + dot(kt, ds, NN))
            dv_ref[window, cols] = dv
            dk_ref[window, cols] = dk
            return tuple(new)

        dq = lax.fori_loop(first, last, chunk, tuple(jnp.zeros((HD, QB), F32) for _ in range(2)))
        out_ref[rows, cols] = (jnp.concatenate(dq, axis=0) * 0.125).T.astype(BF16)

    @pl.when(block == blocks - 1)
    def _():
        out_ref[:, width : 2 * width] = (dk_ref[...] * 0.125).astype(BF16)
        out_ref[:, 2 * width :] = dv_ref[...].astype(BF16)


def attention_backward(calls, call, qkv, o_rows, d_o_rows, lse_rows, starts, lo, place, before):
    seqs, length = starts.shape
    width = qkv.shape[1] // 3 // calls
    heads, pairs = width // HD, width // 128
    nq = length // QB
    halves = len(o_rows)
    half = nq // halves

    def rows_of(g):
        if halves == 1:
            return lambda s, b, lo, place: (s * nq + b, call)
        at = lambda b, place: jnp.clip(b - jnp.bitwise_xor(place[0], g) * half, 0, half - 1)
        return lambda s, b, lo, place: (at(b, place), call)

    def lse_of(g):
        index = rows_of(g)
        if halves == 1:
            return lambda s, b, lo, place: (s, call, 0, b)
        return lambda s, b, lo, place: (s, call, 0, index(s, b, lo, place)[0])

    in_specs = [
        pl.BlockSpec((QB, width), lambda s, b, lo, place: (s * nq + b, 3 * call)),
        pl.BlockSpec((length, width), lambda s, b, lo, place: (s, 3 * call + 1)),
        pl.BlockSpec((length, width), lambda s, b, lo, place: (s, 3 * call + 2)),
        pl.BlockSpec((None, 1, QB), lambda s, b, lo, place: (s, 0, b)),
        *[pl.BlockSpec((QB, width), rows_of(g)) for g in range(halves)],
        *[pl.BlockSpec((QB, width), rows_of(g)) for g in range(halves)],
        *[pl.BlockSpec((None, None, heads, QB), lse_of(g)) for g in range(halves)],
    ]
    operands = [qkv, qkv, qkv, starts[:, None, :], *o_rows, *d_o_rows, *lse_rows]
    alias = {}
    if before is not None:
        alias = {2 + len(operands): 0}
        in_specs.append(pl.BlockSpec(memory_space=pl.ANY))
        operands.append(before)
    rows = seqs * length
    return pl.pallas_call(
        functools.partial(bwd_kernel, pairs, halves),
        grid_spec=pltpu.PrefetchScalarGridSpec(
            num_scalar_prefetch=2,
            grid=(seqs, nq),
            in_specs=in_specs,
            out_specs=pl.BlockSpec((length, 3 * width), lambda s, b, lo, place: (s, call)),
            scratch_shapes=[
                pltpu.VMEM((width, length), BF16),
                pltpu.VMEM((length, width), F32),
                pltpu.VMEM((length, width), F32),
            ],
        ),
        out_shape=jax.ShapeDtypeStruct((rows, qkv.shape[1]), BF16),
        input_output_aliases=alias,
        compiler_params=pltpu.CompilerParams(
            dimension_semantics=("arbitrary", "arbitrary"), vmem_limit_bytes=48 << 20
        ),
        cost_estimate=pl.CostEstimate(
            flops=10 * rows * 640 * width,
            bytes_accessed=16 * rows * width,
            transcendentals=rows * width * 10,
        ),
        name="attention_backward",
    )(lo, place, *operands)


def segment_bounds(segment_ids):
    starts = jnp.sum((segment_ids[:, None, :] < segment_ids[:, :, None]).astype(jnp.int32), axis=2)
    return starts, starts[:, ::QB] // KB


def stats(values):
    mean = jnp.mean(values, axis=-1, keepdims=True)
    centered = values - mean
    scale = lax.rsqrt(jnp.mean(centered * centered, axis=-1, keepdims=True) + EPS)
    return centered * scale, scale


def norm_back(normed, scale, gain_row, grad_rows):
    inner = grad_rows * gain_row
    return scale * (
        inner
        - jnp.mean(inner, axis=-1, keepdims=True)
        - normed * jnp.mean(inner * normed, axis=-1, keepdims=True)
    )


def gelu_pair(z):
    c = math.sqrt(2.0 / math.pi)
    t = jnp.tanh(c * (z + 0.044715 * z * z * z))
    value = 0.5 * z * (1.0 + t)
    slope = 0.5 * (1.0 + t) + 0.5 * z * (1.0 - t * t) * (c * (1.0 + 3 * 0.044715 * z * z))
    return value, slope


NZ, NX, NC = 4, 2, 2


def core_pairs():
    return [(i, i ^ 1) for i in range(NZ * NX * NC)]


def x_pairs():
    return [(i, i ^ 2) for i in range(NZ * NX * NC)]


def z_pairs(shift):
    return [(i, (i + shift * NX * NC) % (NZ * NX * NC)) for i in range(NZ * NX * NC)]


Y_PAIRS = [(0, 1), (1, 0)]


def swap_core(a):
    return lax.ppermute(a, "dp", core_pairs())


def swap_x(a):
    return lax.ppermute(a, "dp", x_pairs())


def swap_y(a):
    return lax.ppermute(a, "tensor", Y_PAIRS)


def assemble_kernel(pos_ref, *refs):
    out_ref = refs[-1]
    z, x, c = pos_ref[0], pos_ref[1], pos_ref[2]
    for n, ref in enumerate(refs[:-1]):
        dx, dc = n % 2, n // 2
        for k in range(NZ):
            out_ref[lax.rem(z - k + NZ, NZ), lax.bitwise_xor(x, dx), lax.bitwise_xor(c, dc)] = ref[k]


def assemble_part(position, pieces, first, width, before, at, total):
    rows = pieces[0].shape[1]
    block = math.gcd(width, 512)
    skip, base = first // block, at * width // block
    piece = pl.BlockSpec((NZ, rows, block), lambda j, pos: (0, 0, skip + j))
    out = pl.BlockSpec((NZ, NX, NC, rows, block), lambda j, pos: (0, 0, 0, 0, base + j))
    shape = (NZ, NX, NC, rows, total)
    body, ins, extra, alias = assemble_kernel, [piece] * 4, [], {}
    if before is not None:
        body = lambda pos, *refs: assemble_kernel(pos, *refs[:4], refs[5])
        ins, extra, alias = ins + [pl.BlockSpec(memory_space=pl.ANY)], [before], {5: 0}
    return pl.pallas_call(
        body,
        grid_spec=pltpu.PrefetchScalarGridSpec(
            num_scalar_prefetch=1, grid=(width // block,), in_specs=ins, out_specs=out
        ),
        out_shape=jax.ShapeDtypeStruct(shape, BF16),
        input_output_aliases=alias,
        compiler_params=pltpu.CompilerParams(
            dimension_semantics=("arbitrary",), vmem_limit_bytes=32 << 20
        ),
        cost_estimate=pl.CostEstimate(
            flops=0, bytes_accessed=2 * 16 * rows * width * 2, transcendentals=0
        ),
        name="assemble",
    )(position, *pieces, *extra)


def assemble(position, groups, first, width):
    total = width * len(groups)
    out = None
    for at, pieces in enumerate(groups):
        out = assemble_part(position, pieces, first, width, out, at, total)
    return out.reshape(-1, total)


def gather_z(shard):
    return jnp.stack([shard] + [lax.ppermute(shard, "dp", z_pairs(k)) for k in range(1, NZ)])


def with_core(pieces):
    return pieces + [swap_core(a) for a in pieces]


def half_rows(h, index, axis):
    return lax.dynamic_index_in_dim(h, index, axis, keepdims=False)


def add(a, b):
    return (a.astype(F32) + b.astype(F32)).astype(BF16)


def reduce_core_x(x, c, grad):
    parts = grad.reshape(NZ, NX, NC, grad.shape[0] // (NZ * NX * NC), grad.shape[1])
    h = add(half_rows(parts, c, 2), swap_core(half_rows(parts, 1 - c, 2)))
    return add(half_rows(h, x, 1), swap_x(half_rows(h, 1 - x, 1)))


def reduce_z(z, total):
    out = half_rows(total, z, 0).astype(F32)
    for k in range(1, NZ):
        piece = half_rows(total, lax.rem(z + k, NZ), 0)
        out = out + lax.ppermute(piece, "dp", z_pairs(k)).astype(F32)
    return out


def sum_everywhere(vector):
    vector = vector + swap_core(vector)
    vector = vector + swap_x(vector)
    vector = vector + swap_y(vector)
    size = NZ * NX * NC
    near = [(i, i ^ 4) for i in range(size)]
    far = [(i, i ^ 8) for i in range(size)]
    vector = vector + lax.ppermute(vector, "dp", near)
    return vector + lax.ppermute(vector, "dp", far)


class Staged:
    def __init__(self):
        index = lax.axis_index("dp")
        self.z, self.x, self.c = index // 4, (index // 2) % 2, index % 2
        self.position = jnp.stack([self.z, self.x, self.c]).astype(jnp.int32)

    def gather(self, shard_qkv, shard_out, shard_up, shard_down):
        column = gather_z(shard_qkv)
        pieces = with_core([column, swap_x(column)])
        qkv = assemble(self.position, [pieces], 0, shard_qkv.shape[1])
        down = lax.all_gather(
            jnp.concatenate([shard_down, swap_y(shard_down)], axis=1), "dp", axis=0, tiled=True
        )
        own = gather_z(jnp.concatenate([shard_out, shard_up], axis=1))
        other = swap_y(own)
        groups = [with_core([a, swap_x(a)]) for a in (own, other)]
        width = shard_out.shape[1]
        out = assemble(self.position, groups, 0, width)
        up = assemble(self.position, groups, width, shard_up.shape[1])
        return qkv, out, up, down

    def reduce_qkv(self, grad):
        return reduce_z(self.z, reduce_core_x(self.x, self.c, grad))

    def reduce_down(self, grad):
        total = lax.psum_scatter(grad, "dp", scatter_dimension=0, tiled=True)
        half = grad.shape[1] // 2
        return total[:, :half].astype(F32) + swap_y(total[:, half:]).astype(F32)

    def reduce_out_up(self, grad_out, grad_up):
        wide_out = reduce_core_x(self.x, self.c, grad_out)
        wide_up = reduce_core_x(self.x, self.c, grad_up)
        half_out, half_up = grad_out.shape[1] // 2, grad_up.shape[1] // 2
        own = jnp.concatenate([wide_out[..., :half_out], wide_up[..., :half_up]], axis=2)
        other = jnp.concatenate([wide_out[..., half_out:], wide_up[..., half_up:]], axis=2)
        total = reduce_z(self.z, add(own, swap_y(other)))
        return total[:, :half_out], total[:, half_out:]

    def exchange(self, parts):
        return [parts[0], swap_y(parts[1])]

    def total(self, vector):
        return sum_everywhere(vector)


class Plain:
    def __init__(self):
        self.n = lax.axis_size("tensor")
        self.rank = lax.axis_index("tensor")

    def gather_groups(self, shard):
        own = lax.all_gather(shard, "dp", axis=0, tiled=True)
        every = lax.all_gather(own, "tensor", axis=0)
        groups = [
            lax.dynamic_index_in_dim(every, (self.rank + g) % self.n, 0, keepdims=False)
            for g in range(self.n)
        ]
        return jnp.concatenate(groups, axis=1)

    def gather(self, shard_qkv, shard_out, shard_up, shard_down):
        qkv = lax.all_gather(shard_qkv, "dp", axis=0, tiled=True)
        return (qkv, *(self.gather_groups(w) for w in (shard_out, shard_up, shard_down)))

    def reduce_qkv(self, grad):
        return lax.psum_scatter(grad, "dp", scatter_dimension=0, tiled=True).astype(F32)

    def reduce_down(self, grad):
        return self.reduce_groups(jnp.split(grad, self.n, axis=1))

    def reduce_out_up(self, grad_out, grad_up):
        return self.reduce_down(grad_out), self.reduce_down(grad_up)

    def absolute(self, parts):
        stacked = jnp.stack(parts)
        order = (jnp.arange(self.n) - self.rank) % self.n
        return jnp.take(stacked, order, axis=0)

    def reduce_groups(self, grads):
        own = lax.psum_scatter(self.absolute(grads), "tensor", scatter_dimension=0, tiled=True)
        return lax.psum_scatter(own[0], "dp", scatter_dimension=0, tiled=True).astype(F32)

    def exchange(self, parts):
        got = lax.all_to_all(self.absolute(parts), "tensor", 0, 0, tiled=True)
        return [
            lax.dynamic_index_in_dim(got, (self.rank + g) % self.n, 0, keepdims=False)
            for g in range(self.n)
        ]

    def total(self, vector):
        return lax.psum(vector, ("dp", "tensor"))


def per_device(
    staged,
    inputs,
    cotangent,
    segment_ids,
    w_qkv,
    w_out,
    w_fc1,
    w_fc2,
    norm_gain,
    norm_bias,
    head_bias,
    out_bias,
    fc1_bias,
):
    n = lax.axis_size("tensor")
    rank = lax.axis_index("tensor")
    comm = Staged() if staged else Plain()
    tokens, features = inputs.shape
    seqs, length = segment_ids.shape
    own_rows = tokens // n
    width = w_qkv.shape[2]
    hidden = w_fc1.shape[1]

    def group_slice(array, g, size, axis=0):
        return lax.dynamic_slice_in_dim(array, ((rank + g) % n) * size, size, axis)

    calls = 2 if width % 256 == 0 else 1
    call_width = width // calls

    def by_call(query, key, value, axis):
        parts = [jnp.split(a, calls, axis=axis) for a in (query, key, value)]
        return jnp.concatenate([p[i] for i in range(calls) for p in parts], axis=axis)

    weight_qkv, weight_out, weight_up, weight_down = comm.gather(
        by_call(w_qkv[0], w_qkv[1], w_qkv[2], 1).astype(BF16),
        w_out.T.astype(BF16),
        w_fc1.astype(BF16),
        w_fc2.T.astype(BF16),
    )

    wide = inputs.astype(F32)
    normed0, scale0 = stats(wide)
    u1 = (normed0 * norm_gain[0] + norm_bias[0]).astype(BF16)
    heads_bias = group_slice(head_bias, 0, width, 1)
    qkv_bias = by_call(heads_bias[0], jnp.zeros((width,), F32), heads_bias[1], 0)
    qkv = (dot(u1, weight_qkv, NN) + qkv_bias).astype(BF16)

    starts, lo = segment_bounds(segment_ids)
    blocks = length // QB
    halves = 2 if n == 2 and seqs == 1 else 1
    half = blocks // halves
    places = [(rank + g) % halves for g in range(halves)]
    at = [jnp.reshape(place * half, (1,)).astype(jnp.int32) for place in places]
    attended = [None] * halves
    for g in reversed(range(halves)):
        attended[g] = attention_forward(calls, qkv, starts, lo, at[g], half)
    o_rows, lse_rows = [a[0] for a in attended], [a[1] for a in attended]
    o_parts = o_rows if halves == n else [group_slice(o_rows[0], g, own_rows) for g in range(n)]
    o_own = jnp.concatenate(comm.exchange(o_parts), axis=1)

    attn = dot(o_own, weight_out, NT) + out_bias[0]
    mine = group_slice(inputs, 0, own_rows).astype(F32)
    normed1, scale1 = stats(attn)
    resid = mine + normed1 * norm_gain[1] + norm_bias[1]
    normed2, scale2 = stats(resid)
    u2 = (normed2 * norm_gain[2] + norm_bias[2]).astype(BF16)

    hidden_bias = jnp.concatenate([group_slice(fc1_bias, g, hidden) for g in range(n)])
    pre = dot(u2, weight_up, NN) + hidden_bias
    act, slope = gelu_pair(pre)
    act, slope = act.astype(BF16), slope.astype(BF16)
    mlp = dot(act, weight_down, NT) + out_bias[1]
    normed3, scale3 = stats(mlp)
    output = (resid + normed3 * norm_gain[3] + norm_bias[3]).astype(BF16)

    dy = group_slice(cotangent, 0, own_rows).astype(F32)
    d_mlp = norm_back(normed3, scale3, norm_gain[3], dy).astype(BF16)
    gain3, shift3 = jnp.sum(normed3 * dy, axis=0), jnp.sum(dy, axis=0)
    bias_mlp = jnp.sum(d_mlp.astype(F32), axis=0)

    grad_down = comm.reduce_down(dot(d_mlp, act, TN).astype(BF16))
    d_pre = (slope.astype(F32) * dot(d_mlp, weight_down, NN)).astype(BF16)
    d_u2 = dot(d_pre, weight_up, NT)
    bias_hidden = jnp.sum(d_pre.astype(F32), axis=0)

    gain2, shift2 = jnp.sum(normed2 * d_u2, axis=0), jnp.sum(d_u2, axis=0)
    d_resid = dy + norm_back(normed2, scale2, norm_gain[2], d_u2)
    gain1, shift1 = jnp.sum(normed1 * d_resid, axis=0), jnp.sum(d_resid, axis=0)
    d_attn = norm_back(normed1, scale1, norm_gain[1], d_resid).astype(BF16)
    bias_attn = jnp.sum(d_attn.astype(F32), axis=0)

    if halves == n:
        weight_parts = jnp.split(weight_out, n, axis=1)
        d_o_parts = [dot(d_attn, w, NN).astype(BF16) for w in weight_parts]
        d_o_rows = comm.exchange(d_o_parts)
    else:
        d_o_all = dot(d_attn, weight_out, NN).astype(BF16)
        d_o_groups = comm.exchange(jnp.split(d_o_all, n, axis=1))
        order = (jnp.arange(n) - rank) % n
        d_o_rows = [jnp.take(jnp.stack(d_o_groups), order, axis=0).reshape(tokens, width)]

    grad_up_part = dot(u2, d_pre, TN).astype(BF16)
    grad_out_part = dot(d_attn, o_own, TN).astype(BF16)
    grad_out, grad_up = comm.reduce_out_up(grad_out_part, grad_up_part)

    d_qkv = None
    place = jnp.reshape(places[0], (1,)).astype(jnp.int32)
    for call in range(calls):
        d_qkv = attention_backward(
            calls, call, qkv, o_rows, d_o_rows, lse_rows, starts, lo, place, d_qkv
        )

    d_u1_parts = [None] * n
    for g in reversed(range(n)):
        d_u1_parts[g] = dot(group_slice(d_qkv, g, own_rows), weight_qkv, NT).astype(BF16)
    d_u1 = sum(t.astype(F32) for t in comm.exchange(d_u1_parts))
    grad_qkv = comm.reduce_qkv(dot(u1, d_qkv, TN).astype(BF16))
    gain0 = shift0 = 0.0
    for g in range(n):
        part = d_u1_parts[g].astype(F32)
        gain0 = gain0 + jnp.sum(group_slice(normed0, g, own_rows) * part, axis=0)
        shift0 = shift0 + jnp.sum(part, axis=0)
    sums = jnp.split(jnp.sum(d_qkv.astype(F32), axis=0), 3 * calls)
    head_terms = jnp.stack([jnp.concatenate(sums[0::3]), jnp.concatenate(sums[2::3])])

    own_normed0 = group_slice(normed0, 0, own_rows)
    own_scale0 = group_slice(scale0, 0, own_rows)
    d_inputs = (d_resid + norm_back(own_normed0, own_scale0, norm_gain[0], d_u1)).astype(BF16)

    hidden_full = jnp.roll(bias_hidden, rank * hidden)
    head_full = lax.dynamic_update_slice_in_dim(
        jnp.zeros(head_bias.shape, F32), head_terms, rank * width, 1
    )
    sums = [gain0, gain1, gain2, gain3, shift0, shift1, shift2, shift3, bias_attn, bias_mlp]
    small = comm.total(
        jnp.concatenate([jnp.stack(sums), head_full, hidden_full.reshape(-1, features)])
    )
    sums = jnp.split(grad_qkv, 3 * calls, axis=1)
    grad_qkv = jnp.stack([jnp.concatenate(sums[i::3], axis=1) for i in range(3)])
    return (
        output,
        d_inputs,
        grad_qkv,
        grad_out.T,
        grad_up,
        grad_down.T,
        small[0:4],
        small[4:8],
        small[10:12],
        small[8:10],
        small[12:].reshape(-1),
    )


def solution(mesh):
    staged = mesh.shape["dp"] == NZ * NX * NC and mesh.shape["tensor"] == 2
    return jax.shard_map(
        functools.partial(per_device, staged),
        mesh=mesh,
        in_specs=(
            P("dp", None),
            P("dp", None),
            P("dp", None),
            P(None, "dp", "tensor"),
            P("tensor", "dp"),
            P("dp", "tensor"),
            P("tensor", "dp"),
            P(),
            P(),
            P(),
            P(),
            P(),
        ),
        out_specs=(
            P(("dp", "tensor"), None),
            P(("dp", "tensor"), None),
            P(None, "dp", "tensor"),
            P("tensor", "dp"),
            P("dp", "tensor"),
            P("tensor", "dp"),
            P(),
            P(),
            P(),
            P(),
            P(),
        ),
        check_vma=False,
    )
```

```python
import functools
import math

import jax
import jax.numpy as jnp
from jax import lax
from jax.experimental import pallas as pl
from jax.experimental.pallas import tpu as pltpu
from jax.sharding import PartitionSpec as P

HD = 64
QB = 256
KB = 256
MAX_SEGMENT = 1024
max_chunks = MAX_SEGMENT // KB + 1
SCORE_SCALE = 0.125 * math.log2(math.e)
NEG = -1e30
EPS = 1e-05
BF16 = jnp.bfloat16
F32 = jnp.float32
NT = (((1,), (1,)), ((), ()))
NN = (((1,), (0,)), ((), ()))
TN = (((0,), (0,)), ((), ()))

SMALL = pl.CostEstimate(flops=1, bytes_accessed=1, transcendentals=0)
VMEM = 60 << 20
PAIR = 2 * HD


def dot(a, b, dims):
    return lax.dot_general(a, b, dims, preferred_element_type=jnp.float32)


def split_pair(block):
    lane = lax.broadcasted_iota(jnp.int32, block.shape, 1)
    zero = jnp.zeros_like(block)
    return (jnp.where(lane < HD, block, zero), jnp.where(lane >= HD, block, zero))


def fwd_kernel(pairs, lo_ref, off_ref, *refs):
    q_refs, k_refs, v_refs = refs[:pairs], refs[pairs : 2 * pairs], refs[2 * pairs : 3 * pairs]
    start_ref, o_ref, l_ref, vt_ref = refs[3 * pairs :]
    step = pl.program_id(1)
    block = off_ref[0] + step

    @pl.when(step == 0)
    def _():
        for pair in range(pairs):
            vt_ref[pair] = v_refs[pair][...].T

    pair_step = math.gcd(pairs, 4)
    row_start = start_ref[...]
    query_pos = block * QB + lax.broadcasted_iota(jnp.int32, (1, QB), 1)
    first = lo_ref[pl.program_id(0), block]
    count = block + 1 - first
    base = pl.multiple_of(first * KB, KB)

    for chunks in range(1, max_chunks + 1):

        @pl.when(count == chunks)
        def _(size=chunks * KB):
            window = pl.ds(base, size)
            key_pos = lax.broadcasted_iota(jnp.int32, (size, QB), 0) + base
            ok = (key_pos >= row_start) & (key_pos <= query_pos)
            for pair in range(pairs):
                q_heads = split_pair(q_refs[pair][...])
                keys = k_refs[pair][window, :]
                outs = []
                for h in range(2):
                    s = jnp.where(ok, dot(keys, q_heads[h], NT) * SCORE_SCALE, NEG)
                    peak = jnp.max(s, axis=0, keepdims=True)
                    p = jnp.exp2(s - peak)
                    total = jnp.sum(p, axis=0, keepdims=True)
                    vt = vt_ref[pair, h * HD : (h + 1) * HD, window]
                    outs.append(dot(vt, p.astype(BF16), NN) / total)
                    l_ref[pair, h : h + 1, :] = peak + jnp.log2(total)
                cols = slice(pair * PAIR, (pair + 1) * PAIR)
                o_ref[:, cols] = jnp.concatenate(outs, axis=0).T.astype(BF16)


def attention_forward(first, pairs, qkv, starts, lo, offset, blocks):
    seqs, length = starts.shape
    nq = length // QB
    every = range(first, first + pairs)

    def rows_at(p):
        return pl.BlockSpec((QB, PAIR), lambda s, b, lo, off: (s * nq + off[0] + b, 3 * p))

    def all_at(p, kind):
        return pl.BlockSpec((length, PAIR), lambda s, b, lo, off: (s, 3 * p + kind))

    grid_spec = pltpu.PrefetchScalarGridSpec(
        num_scalar_prefetch=2,
        grid=(seqs, blocks),
        in_specs=[rows_at(p) for p in every]
        + [all_at(p, kind) for kind in (1, 2) for p in every]
        + [pl.BlockSpec((None, 1, QB), lambda s, b, lo, off: (s, 0, off[0] + b))],
        out_specs=[
            pl.BlockSpec((QB, pairs * PAIR), lambda s, b, lo, off: (s * blocks + b, 0)),
            pl.BlockSpec((None, pairs, 2, QB), lambda s, b, lo, off: (s, 0, 0, b)),
        ],
        scratch_shapes=[pltpu.VMEM((pairs, PAIR, length), BF16)],
    )
    return pl.pallas_call(
        functools.partial(fwd_kernel, pairs),
        grid_spec=grid_spec,
        out_shape=(
            jax.ShapeDtypeStruct((seqs * blocks * QB, pairs * PAIR), BF16),
            jax.ShapeDtypeStruct((seqs, pairs, 2, blocks * QB), F32),
        ),
        compiler_params=pltpu.CompilerParams(
            dimension_semantics=("arbitrary",) * 2, vmem_limit_bytes=VMEM
        ),
        cost_estimate=SMALL,
        name="attention_forward",
    )(lo, offset, *[qkv] * (3 * pairs), starts[:, None, :])


def bwd_kernel(halves, lo_ref, place_ref, q_ref, k_ref, v_ref, start_ref, *refs):
    o_refs, do_refs, l_refs = refs[:halves], refs[halves : 2 * halves], refs[2 * halves : 3 * halves]
    out_ref, kt_ref, dk_ref, dv_ref = refs[-4:]
    block = pl.program_id(1)
    blocks = pl.num_programs(1)
    @pl.when(block == 0)
    def _():
        kt_ref[...] = k_ref[...].T
        dk_ref[...] = jnp.zeros_like(dk_ref)
        dv_ref[...] = jnp.zeros_like(dv_ref)

    mine = block // (blocks // halves) == place_ref[0]

    def pick(two, index=slice(None)):
        if halves == 1:
            return two[0][index]
        return jnp.where(mine, two[0][index], two[1][index])

    row_start = start_ref[...]
    query_pos = block * QB + lax.broadcasted_iota(jnp.int32, (1, QB), 1)
    key_iota = lax.broadcasted_iota(jnp.int32, (KB, QB), 0)
    first = lo_ref[pl.program_id(0), block]
    last = (block + 1) * (QB // KB)
    rows = pl.ds(pl.multiple_of(block * QB, QB), QB)
    q_heads = split_pair(q_ref[...])
    g_pair = pick(do_refs)
    g_heads = split_pair(g_pair)
    prod = (g_pair.astype(F32) * pick(o_refs).astype(F32)).T
    deltas = [jnp.sum(prod[h * HD : (h + 1) * HD], axis=0, keepdims=True) for h in range(2)]
    lses = [pick(l_refs, slice(h, h + 1)) for h in range(2)]

    def chunk(j, carry):
        base = pl.multiple_of(j * KB, KB)
        window = pl.ds(base, KB)
        keys = k_ref[window, :]
        vals = v_ref[window, :]
        key_pos = key_iota + base
        ok = (key_pos >= row_start) & (key_pos <= query_pos)
        new = []
        dv = dv_ref[window, :]
        dk = dk_ref[window, :]
        for h in range(2):
            s = jnp.where(ok, dot(keys, q_heads[h], NT) * SCORE_SCALE, NEG)
            p = jnp.exp2(s - lses[h])
            dp = dot(vals, g_heads[h], NT)
            ds = (p * (dp - deltas[h])).astype(BF16)
            dv = dv + dot(p.astype(BF16), g_heads[h], NN)
            dk = dk + dot(ds, q_heads[h], NN)
            kt = kt_ref[h * HD : (h + 1) * HD, window]
            new.append(carry[h] + dot(kt, ds, NN))
        dv_ref[window, :] = dv
        dk_ref[window, :] = dk
        return tuple(new)

    dq = lax.fori_loop(first, last, chunk, tuple(jnp.zeros((HD, QB), F32) for _ in range(2)))
    out_ref[rows, :PAIR] = (jnp.concatenate(dq, axis=0) * 0.125).T.astype(BF16)

    @pl.when(block == blocks - 1)
    def _():
        out_ref[:, PAIR : 2 * PAIR] = (dk_ref[...] * 0.125).astype(BF16)
        out_ref[:, 2 * PAIR :] = dv_ref[...].astype(BF16)


def attention_backward(pair, qkv, o_rows, d_o_rows, lse_rows, column, starts, lo, place, before):
    seqs, length = starts.shape
    nq = length // QB
    halves = len(o_rows)
    half = nq // halves

    def row(g, s, b, place):
        if halves == 1:
            return s, b, s * nq + b
        at = jnp.clip(b - jnp.bitwise_xor(place[0], g) * half, 0, half - 1)
        return s, at, at

    def rows_of(g, col):
        return pl.BlockSpec((QB, PAIR), lambda s, b, lo, place: (row(g, s, b, place)[2], col))

    def lse_of(g):
        return pl.BlockSpec(
            (None, None, 2, QB), lambda s, b, lo, place: (s, column, 0, row(g, s, b, place)[1])
        )

    in_specs = [
        pl.BlockSpec((QB, PAIR), lambda s, b, lo, place: (s * nq + b, 3 * pair)),
        pl.BlockSpec((length, PAIR), lambda s, b, lo, place: (s, 3 * pair + 1)),
        pl.BlockSpec((length, PAIR), lambda s, b, lo, place: (s, 3 * pair + 2)),
        pl.BlockSpec((None, 1, QB), lambda s, b, lo, place: (s, 0, b)),
        *[rows_of(g, column) for g in range(halves)],
        *[rows_of(g, pair) for g in range(halves)],
        *[lse_of(g) for g in range(halves)],
    ]
    operands = [qkv, qkv, qkv, starts[:, None, :], *o_rows, *d_o_rows, *lse_rows]
    alias = {}
    if before is not None:
        alias = {2 + len(operands): 0}
        in_specs.append(pl.BlockSpec(memory_space=pl.ANY))
        operands.append(before)
    return pl.pallas_call(
        functools.partial(bwd_kernel, halves),
        grid_spec=pltpu.PrefetchScalarGridSpec(
            num_scalar_prefetch=2,
            grid=(seqs, nq),
            in_specs=in_specs,
            out_specs=pl.BlockSpec((length, 3 * PAIR), lambda s, b, lo, place: (s, pair)),
            scratch_shapes=[
                pltpu.VMEM((PAIR, length), BF16),
                pltpu.VMEM((length, PAIR), F32),
                pltpu.VMEM((length, PAIR), F32),
            ],
        ),
        out_shape=jax.ShapeDtypeStruct(qkv.shape, BF16),
        input_output_aliases=alias,
        compiler_params=pltpu.CompilerParams(
            dimension_semantics=("arbitrary", "arbitrary"), vmem_limit_bytes=VMEM
        ),
        cost_estimate=SMALL,
        name="attention_backward",
    )(lo, place, *operands)


def segment_bounds(segment_ids):
    starts = jnp.sum((segment_ids[:, None, :] < segment_ids[:, :, None]).astype(jnp.int32), axis=2)
    return starts, starts[:, ::QB] // KB


ROWS = 256
HIDDEN_BLOCK = 1024
NZ, NX, NC = 4, 2, 2


def unit_rows(v):
    centered = v - jnp.mean(v, axis=-1, keepdims=True)
    scale = lax.rsqrt(jnp.mean(centered * centered, axis=-1, keepdims=True) + EPS)
    return centered * scale, scale


def norm_back(normed, scale, inner):
    return scale * (
        inner
        - jnp.mean(inner, axis=-1, keepdims=True)
        - normed * jnp.mean(inner * normed, axis=-1, keepdims=True)
    )


def rows_sum(v):
    return jnp.sum(v, axis=0, keepdims=True)


def store_turned(ref, block, by_device):
    turned = block.T
    if not by_device:
        ref[...] = turned
        return
    size = turned.shape[0] // (NZ * NX * NC)
    for z in range(NZ):
        for x in range(NX):
            for c in range(NC):
                old = ((z * NX + x) * NC + c) * size
                new = ((c * NX + x) * NZ + z) * size
                ref[new : new + size, :] = turned[old : old + size]


def turned_spec(features):
    return pl.BlockSpec((features, ROWS), lambda i, *_: (0, i))


def fixed(shape):
    return pl.BlockSpec(shape, lambda *_: (0,) * len(shape), pipeline_mode=pl.Buffered(1))


def call(body, name, grid, ins, outs, shapes, operands, prefetch=(), scratch=(), vmem=VMEM):
    return pl.pallas_call(
        body,
        grid_spec=pltpu.PrefetchScalarGridSpec(
            num_scalar_prefetch=len(prefetch),
            grid=grid,
            in_specs=ins,
            out_specs=outs,
            scratch_shapes=scratch,
        ),
        out_shape=shapes,
        compiler_params=pltpu.CompilerParams(
            dimension_semantics=("arbitrary",) * len(grid), vmem_limit_bytes=vmem
        ),
        cost_estimate=SMALL,
        name=name,
    )(*prefetch, *operands)


def shaped(rows, cols, dtype):
    return jax.ShapeDtypeStruct((rows, cols), dtype)


def row_spec(cols):
    return pl.BlockSpec((ROWS, cols), lambda i, *_: (i, 0))


def shifted_spec(cols):
    return pl.BlockSpec((ROWS, cols), lambda i, at, *_: (at[0] + i, 0))


def first_norm_kernel(turn, x_ref, gain_ref, bias_ref, u_ref, turned_ref):
    normed, _ = unit_rows(x_ref[...].astype(F32))
    u = (normed * gain_ref[0:1, :] + bias_ref[0:1, :]).astype(BF16)
    u_ref[...] = u
    store_turned(turned_ref, u, turn)


def first_norm(turn, inputs, gain, bias):
    tokens, features = inputs.shape
    return call(
        functools.partial(first_norm_kernel, turn),
        "first_norm",
        (tokens // ROWS,),
        [row_spec(features), fixed(gain.shape), fixed(bias.shape)],
        [row_spec(features), turned_spec(features)],
        [shaped(tokens, features, BF16), shaped(features, tokens, BF16)],
        [inputs, gain, bias],
        vmem=24 << 20,
    )


class Blocks:
    def __init__(self, operands, specs, load):
        self.operands, self.specs, self.load = operands, specs, load


def whole_blocks(weight):
    steps = weight.shape[1] // HIDDEN_BLOCK
    spec = pl.BlockSpec(
        (weight.shape[0], HIDDEN_BLOCK), lambda j, *_: (0, jnp.minimum(j, steps - 1))
    )

    def load(at_ref, step, refs, hold_ref):
        hold_ref[...] = refs[0][...]

    return Blocks([weight], [spec], load)


def piece_blocks(groups, columns):
    rows = groups[0][0].shape[1]
    steps = columns // HIDDEN_BLOCK
    operands, specs = [], []
    for g, pieces in enumerate(groups):
        for piece in pieces:
            operands.append(piece)
            specs.append(
                pl.BlockSpec(
                    (NZ, rows, HIDDEN_BLOCK),
                    lambda j, *_, g=g: (0, 0, jnp.clip(j - g * steps, 0, steps - 1)),
                )
            )

    def load(at_ref, step, refs, hold_ref):
        for g in range(len(groups)):

            @pl.when(step // steps == g)
            def _(g=g):
                place_pieces(at_ref, refs[4 * g : 4 * g + 4], hold_ref, rows)

    return Blocks(operands, specs, load)


def place_pieces(at_ref, refs, hold_ref, rows):
    z, x, c = at_ref[1], at_ref[2], at_ref[3]
    for n, ref in enumerate(refs):
        dx, dc = n % 2, n // 2
        for k in range(NZ):
            index = lax.rem(z - k + NZ, NZ) * NX + lax.bitwise_xor(x, dx)
            row = pl.multiple_of((index * NC + lax.bitwise_xor(c, dc)) * rows, rows)
            hold_ref[pl.ds(row, rows), :] = ref[k]


def middle_kernel(turn, groups, pieces, at_ref, *refs):
    o_refs, w_refs = refs[:groups], refs[groups : groups + pieces]
    x_ref, gain_ref, bias_ref, ob_ref = refs[groups + pieces : groups + pieces + 4]
    attn_ref, resid_ref, u_ref, o_ref, turned_ref, w_ref = refs[groups + pieces + 4 :]
    width = w_refs[0].shape[2] if pieces > 1 else 0

    @pl.when(pl.program_id(0) == 0)
    def _():
        if pieces == 1:
            w_ref[...] = w_refs[0][...]
        else:
            for g in range(pieces // 4):
                place_pieces(
                    at_ref,
                    w_refs[4 * g : 4 * g + 4],
                    w_ref.at[:, g * width : (g + 1) * width],
                    w_refs[0].shape[1],
                )

    attn = ob_ref[0:1, :]
    width = o_refs[0].shape[1]
    for g in range(groups):
        cols = slice(g * width, (g + 1) * width)
        o_ref[:, cols] = o_refs[g][...]
        attn = attn + dot(o_refs[g][...], w_ref[:, cols], NT)
    attn_ref[...] = attn
    normed, _ = unit_rows(attn)
    resid = x_ref[...].astype(F32) + normed * gain_ref[1:2, :] + bias_ref[1:2, :]
    resid_ref[...] = resid
    normed, _ = unit_rows(resid)
    u = (normed * gain_ref[2:3, :] + bias_ref[2:3, :]).astype(BF16)
    u_ref[...] = u
    store_turned(turned_ref, u, turn)


def middle(turn, at, o_groups, weight_out, inputs, gain, bias, out_bias):
    rows, width = o_groups[0].shape
    features = inputs.shape[1]
    if len(weight_out) == 1:
        weight_specs = [fixed(weight_out[0].shape)]
    else:
        part = features * 4 // len(weight_out)
        last = weight_out[0].shape[2] // part - 1
        shape = (NZ, weight_out[0].shape[1], part)
        spec = pl.BlockSpec(shape, lambda *_: (0, 0, last), pipeline_mode=pl.Buffered(1))
        weight_specs = [spec] * len(weight_out)
    return call(
        functools.partial(middle_kernel, turn, len(o_groups), len(weight_out)),
        "middle",
        (rows // ROWS,),
        [row_spec(width)] * len(o_groups)
        + weight_specs
        + [shifted_spec(features)]
        + [fixed(a.shape) for a in (gain, bias, out_bias)],
        [row_spec(features)] * 4 + [turned_spec(features), fixed((features, features))],
        [shaped(rows, features, d) for d in (F32, F32, BF16, BF16)]
        + [shaped(features, rows, BF16), shaped(features, features, BF16)],
        [*o_groups, *weight_out, inputs, gain, bias, out_bias],
        prefetch=[at],
    )


GELU_C = math.sqrt(2.0 / math.pi)


def gelu_tanh_of(z):
    square = z * z
    return square, jnp.tanh(z * (GELU_C + (GELU_C * 0.044715) * square))


def later_spec(cols, steps, shift=False):
    if shift:
        return pl.BlockSpec((ROWS, cols), lambda j, at, *_: (at[0] + jnp.maximum(j - steps, 0), 0))
    return pl.BlockSpec((ROWS, cols), lambda j, *_: (jnp.maximum(j - steps, 0), 0))


def later_turned(features, steps):
    return pl.BlockSpec((features, ROWS), lambda j, *_: (0, jnp.maximum(j - steps, 0)))


def column_spec(rows, steps):
    return pl.BlockSpec((rows, HIDDEN_BLOCK), lambda j, *_: (0, jnp.minimum(j, steps - 1)))


def feed_kernel(up, down, steps, at_ref, u_ref, b_ref, *refs):
    n, m = len(up.operands), len(down.operands)
    up_refs, down_refs = refs[:n], refs[n : n + m]
    resid_ref, dy_ref, gain_ref, bias_ref, ob_ref = refs[n + m : n + m + 5]
    pre_ref, out_ref, d_ref, turned_ref, sum_ref, up_hold, down_hold, total_ref = refs[n + m + 5 :]
    step = pl.program_id(0)
    rows = u_ref.shape[0]

    @pl.when(step == 0)
    def _():
        total_ref[...] = jnp.zeros_like(total_ref)
        sum_ref[...] = jnp.zeros_like(sum_ref)

    @pl.when(step < steps)
    def _():
        up.load(at_ref, step, up_refs, up_hold)
        down.load(at_ref, step, down_refs, down_hold)
        for r in range(0, rows, ROWS):
            part = slice(r, r + ROWS)
            z = dot(u_ref[part, :], up_hold[...], NN) + b_ref[...]
            pre_ref[part, :] = z.astype(BF16)
            _, t = gelu_tanh_of(z)
            act = (z * (0.5 + 0.5 * t)).astype(BF16)
            total_ref[part, :] += dot(act, down_hold[...], NT)

    @pl.when(step >= steps)
    def _():
        mlp = total_ref[pl.ds(pl.multiple_of((step - steps) * ROWS, ROWS), ROWS), :] + ob_ref[1:2, :]
        normed, scale = unit_rows(mlp)
        out_ref[...] = (resid_ref[...] + normed * gain_ref[3:4, :] + bias_ref[3:4, :]).astype(BF16)
        dy = dy_ref[...].astype(F32)
        d_mlp = norm_back(normed, scale, dy * gain_ref[3:4, :]).astype(BF16)
        d_ref[...] = d_mlp
        store_turned(turned_ref, d_mlp, False)
        sum_ref[0:1, :] += rows_sum(normed * dy)
        sum_ref[1:2, :] += rows_sum(dy)
        sum_ref[2:3, :] += rows_sum(d_mlp.astype(F32))


def feed(at, u, up, down, hidden_bias, resid, cotangent, gain, bias, out_bias):
    rows, features = u.shape
    hidden = hidden_bias.shape[1]
    steps = hidden // HIDDEN_BLOCK
    return call(
        functools.partial(feed_kernel, up, down, steps),
        "feed",
        (steps + rows // ROWS,),
        [fixed(u.shape), column_spec(1, steps), *up.specs, *down.specs]
        + [later_spec(features, steps), later_spec(features, steps, True)]
        + [fixed(a.shape) for a in (gain, bias, out_bias)],
        [column_spec(rows, steps), later_spec(features, steps), later_spec(features, steps)]
        + [later_turned(features, steps), fixed((8, features))],
        [shaped(rows, hidden, BF16), shaped(rows, features, BF16), shaped(rows, features, BF16)]
        + [shaped(features, rows, BF16), shaped(8, features, F32)],
        [u, hidden_bias, *up.operands, *down.operands, resid, cotangent, gain, bias, out_bias],
        prefetch=[at],
        scratch=[
            pltpu.VMEM((features, HIDDEN_BLOCK), BF16),
            pltpu.VMEM((features, HIDDEN_BLOCK), BF16),
            pltpu.VMEM((rows, features), F32),
        ],
    )


def feed_back_kernel(turn, groups, up, down, steps, at_ref, d_ref, ut_ref, pre_ref, *refs):
    n, m = len(up.operands), len(down.operands)
    up_refs, down_refs = refs[:n], refs[n : n + m]
    resid_ref, attn_ref, dy_ref, wo_ref, gain_ref = refs[n + m : n + m + 5]
    refs = refs[n + m + 5 :]
    send_ref, keep_ref, hid_ref, d_resid_ref, sum_ref, turned_ref = refs[:6]
    d_o_refs = refs[6 : 6 + groups]
    up_hold, down_hold, total_ref = refs[6 + groups :]
    step = pl.program_id(0)
    rows, features = d_ref.shape
    half = features // NC

    @pl.when(step == 0)
    def _():
        total_ref[...] = jnp.zeros_like(total_ref)
        sum_ref[...] = jnp.zeros_like(sum_ref)

    @pl.when(step < steps)
    def _():
        up.load(at_ref, step, up_refs, up_hold)
        down.load(at_ref, step, down_refs, down_hold)
        column_sum = 0.0
        d_pres = []
        for r in range(0, rows, ROWS):
            part = slice(r, r + ROWS)
            d_act = dot(d_ref[part, :], down_hold[...], NN)
            z = pre_ref[part, :].astype(F32)
            square, t = gelu_tanh_of(z)
            gate = 0.5 + 0.5 * t
            slope = gate + (1.0 - t * t) * (
                z * (0.5 * GELU_C + (1.5 * GELU_C * 0.044715) * square)
            )
            d_pre = (slope * d_act).astype(BF16)
            d_pres.append(d_pre)
            column_sum = column_sum + rows_sum(d_pre.astype(F32))
            total_ref[part, :] += dot(d_pre, up_hold[...], NT)
        hid_ref[...] = column_sum
        d_pre = jnp.concatenate(d_pres, axis=0)
        c = at_ref[3]
        there = pl.ds(pl.multiple_of((1 - c) * half, half), half)
        here = pl.ds(pl.multiple_of(c * half, half), half)
        send_ref[...] = dot(ut_ref[there, :], d_pre, NN).astype(BF16)
        keep_ref[...] = dot(ut_ref[here, :], d_pre, NN).astype(BF16)

    @pl.when(step >= steps)
    def _():
        d_u = total_ref[pl.ds(pl.multiple_of((step - steps) * ROWS, ROWS), ROWS), :]
        normed, scale = unit_rows(resid_ref[...])
        sum_ref[0:1, :] += rows_sum(normed * d_u)
        sum_ref[1:2, :] += rows_sum(d_u)
        d_resid = dy_ref[...].astype(F32) + norm_back(normed, scale, d_u * gain_ref[2:3, :])
        d_resid_ref[...] = d_resid
        normed, scale = unit_rows(attn_ref[...])
        sum_ref[2:3, :] += rows_sum(normed * d_resid)
        sum_ref[3:4, :] += rows_sum(d_resid)
        d_attn = norm_back(normed, scale, d_resid * gain_ref[1:2, :]).astype(BF16)
        sum_ref[4:5, :] += rows_sum(d_attn.astype(F32))
        store_turned(turned_ref, d_attn, turn)
        width = d_o_refs[0].shape[1]
        for g in range(groups):
            d_o_refs[g][...] = dot(d_attn, wo_ref[:, g * width : (g + 1) * width], NN).astype(BF16)


def feed_back(turn, groups, at, d_mlp, u_turned, pre, up, down, resid, attn, cotangent, weight_out, gain):
    rows, features = d_mlp.shape
    hidden = pre.shape[1]
    steps = hidden // HIDDEN_BLOCK
    width = features // groups
    half = features // NC
    return call(
        functools.partial(feed_back_kernel, turn, groups, up, down, steps),
        "feed_back",
        (steps + rows // ROWS,),
        [fixed(d_mlp.shape), fixed(u_turned.shape)]
        + [column_spec(rows, steps), *up.specs, *down.specs]
        + [later_spec(features, steps), later_spec(features, steps), later_spec(features, steps, True)]
        + [fixed(weight_out.shape), fixed(gain.shape)],
        [column_spec(half, steps), column_spec(half, steps)]
        + [column_spec(1, steps), later_spec(features, steps), fixed((8, features))]
        + [later_turned(features, steps)]
        + [later_spec(width, steps)] * groups,
        [shaped(half, hidden, BF16), shaped(half, hidden, BF16)]
        + [shaped(1, hidden, F32), shaped(rows, features, F32), shaped(8, features, F32)]
        + [shaped(features, rows, BF16)]
        + [shaped(rows, width, BF16)] * groups,
        [d_mlp, u_turned, pre, *up.operands, *down.operands]
        + [resid, attn, cotangent, weight_out, gain],
        prefetch=[at],
        scratch=[
            pltpu.VMEM((features, HIDDEN_BLOCK), BF16),
            pltpu.VMEM((features, HIDDEN_BLOCK), BF16),
            pltpu.VMEM((rows, features), F32),
        ],
    )


def d_in_kernel(at_ref, dq_ref, w_ref, x_ref, part_ref, sum_ref, head_ref):
    @pl.when(pl.program_id(0) == 0)
    def _():
        sum_ref[...] = jnp.zeros_like(sum_ref)
        head_ref[...] = jnp.zeros_like(head_ref)

    d_qkv = dq_ref[...]
    part = dot(d_qkv, w_ref[...], NT).astype(BF16)
    part_ref[...] = part
    part = part.astype(F32)
    normed, _ = unit_rows(x_ref[...].astype(F32))
    sum_ref[0:1, :] += rows_sum(normed * part)
    sum_ref[1:2, :] += rows_sum(part)
    head_ref[0:1, :] += rows_sum(d_qkv.astype(F32))


def d_in(row_at, rows, d_qkv, weight_qkv, inputs):
    features, width = weight_qkv.shape
    return call(
        d_in_kernel,
        "d_in",
        (rows // ROWS,),
        [shifted_spec(width), fixed(weight_qkv.shape), shifted_spec(features)],
        [row_spec(features), fixed((8, features)), fixed((8, width))],
        [shaped(rows, features, BF16), shaped(8, features, F32), shaped(8, width, F32)],
        [d_qkv, weight_qkv, inputs],
        prefetch=[row_at],
    )


def last_kernel(terms, at_ref, *refs):
    x_ref, d_resid_ref, gain_ref, out_ref = refs[terms:]
    d_u = sum(r[...].astype(F32) for r in refs[:terms])
    normed, scale = unit_rows(x_ref[...].astype(F32))
    out_ref[...] = (d_resid_ref[...] + norm_back(normed, scale, d_u * gain_ref[0:1, :])).astype(BF16)


def last(row_at, parts, inputs, d_resid, gain):
    rows, features = d_resid.shape
    return call(
        functools.partial(last_kernel, len(parts)),
        "last",
        (rows // ROWS,),
        [row_spec(features)] * len(parts) + [shifted_spec(features), row_spec(features), fixed(gain.shape)],
        row_spec(features),
        shaped(rows, features, BF16),
        [*parts, inputs, d_resid, gain],
        prefetch=[row_at],
    )


def grad_rows_kernel(terms, at_ref, left_ref, right_ref, *refs):
    total = dot(left_ref[...], right_ref[...], NN)
    for r in refs[:terms]:
        total = total + r[...].astype(F32)
    refs[terms][...] = total.astype(BF16)


def grad_rows(left, at, right, terms=()):
    _, rows, tokens = left.shape
    columns = right.shape[1]
    block = math.gcd(columns, 512)
    return call(
        functools.partial(grad_rows_kernel, len(terms)),
        "grad_rows",
        (columns // block,),
        [
            pl.BlockSpec((None, rows, tokens), lambda j, at: (at[0], 0, 0)),
            pl.BlockSpec((tokens, block), lambda j, at: (0, j)),
        ]
        + [pl.BlockSpec((None, rows, block), lambda j, at: (at[1], 0, j))] * len(terms),
        pl.BlockSpec((rows, block), lambda j, at: (0, j)),
        shaped(rows, columns, BF16),
        [left, right, *terms],
        prefetch=[at],
    )


def grad_down_kernel(left_ref, pre_ref, out_ref):
    z = pre_ref[...].astype(F32)
    _, t = gelu_tanh_of(z)
    out_ref[...] = dot(left_ref[...], (z * (0.5 + 0.5 * t)).astype(BF16), NN).astype(BF16)


def grad_down_of(d_mlp_turned, pre):
    features, rows = d_mlp_turned.shape
    hidden = pre.shape[1]
    column = lambda size: pl.BlockSpec((size, 512), lambda j: (0, j))
    return call(
        grad_down_kernel,
        "grad_down",
        (hidden // 512,),
        [fixed(d_mlp_turned.shape), column(rows)],
        column(features),
        shaped(features, hidden, BF16),
        [d_mlp_turned, pre],
    )


def merge_kernel(outs, ups, at_ref, *refs):
    out_refs, up_refs, both_refs, to_ref = refs[:outs], refs[outs : outs + ups], refs[outs + ups : -1], refs[-1]

    def fill(parts):
        to_ref[...] = sum(r[...].astype(F32) for r in (*parts, *both_refs)).astype(BF16)

    @pl.when(pl.program_id(0) == 0)
    def _():
        fill(out_refs)

    @pl.when(pl.program_id(0) > 0)
    def _():
        fill(up_refs)


def merge(at, rows, outs, ups, group, both=()):
    width = outs[0].shape[1] // 2
    hidden = ups[0].shape[1] // 2
    steps = hidden // width
    pick_row = lambda a, at: at[0] if a.shape[0] > rows else 0
    specs = [pl.BlockSpec((rows, width), lambda j, at, a=a: (pick_row(a, at), group)) for a in outs]
    specs += [
        pl.BlockSpec(
            (rows, width),
            lambda j, at, a=a: (pick_row(a, at), group * steps + jnp.maximum(j - 1, 0)),
        )
        for a in ups
    ]
    specs += [pl.BlockSpec((rows, width), lambda j, at, a=a: (pick_row(a, at), j)) for a in both]
    return call(
        functools.partial(merge_kernel, len(outs), len(ups)),
        "merge",
        (1 + steps,),
        specs,
        pl.BlockSpec((rows, width), lambda j, at: (0, j)),
        shaped(rows, width + hidden, BF16),
        [*outs, *ups, *both],
        prefetch=[at],
    )


def tie(*values):
    return lax.optimization_barrier(values)


def pick(array, index, axis=0):
    return lax.dynamic_index_in_dim(array, index, axis, keepdims=False)


def add(a, b):
    return (a.astype(F32) + b.astype(F32)).astype(BF16)


def flips(bit):
    return [(i, i ^ bit) for i in range(NZ * NX * NC)]


def z_pairs(shift):
    return [(i, (i + shift * NX * NC) % (NZ * NX * NC)) for i in range(NZ * NX * NC)]


def swap_core(a):
    return lax.ppermute(a, "dp", flips(1))


def swap_x(a):
    return lax.ppermute(a, "dp", flips(NC))


def swap_y(a):
    return lax.ppermute(a, "tensor", [(0, 1), (1, 0)])


def spread_z(shard):
    return [shard] + [lax.ppermute(shard, "dp", z_pairs(k)) for k in range(1, NZ)]


def assemble_qkv_kernel(pos_ref, *refs):
    out_ref = refs[-1]
    z, x, c = pos_ref[0], pos_ref[1], pos_ref[2]
    kinds, _, width = refs[0].shape[1:]
    for n, ref in enumerate(refs[:-1]):
        for k in range(NZ):
            to = out_ref.at[
                lax.rem(z - k + NZ, NZ), lax.bitwise_xor(x, n % 2), lax.bitwise_xor(c, n // 2)
            ]
            for p in range(width // PAIR):
                for kind in range(kinds):
                    at = (p * kinds + kind) * PAIR
                    to[:, at : at + PAIR] = ref[k, kind, :, p * PAIR : (p + 1) * PAIR]


def assemble_qkv(position, pieces):
    _, kinds, rows, width = pieces[0].shape
    step = 16
    out = pl.pallas_call(
        assemble_qkv_kernel,
        grid_spec=pltpu.PrefetchScalarGridSpec(
            num_scalar_prefetch=1,
            grid=(rows // step,),
            in_specs=[pl.BlockSpec((NZ, kinds, step, width), lambda i, pos: (0, 0, i, 0))] * 4,
            out_specs=pl.BlockSpec(
                (NZ, NX, NC, step, kinds * width), lambda i, pos: (0, 0, 0, i, 0)
            ),
        ),
        out_shape=jax.ShapeDtypeStruct((NZ, NX, NC, rows, kinds * width), BF16),
        compiler_params=pltpu.CompilerParams(
            dimension_semantics=("arbitrary",), vmem_limit_bytes=24 << 20
        ),
        cost_estimate=SMALL,
        name="assemble_qkv",
    )(position, *pieces)
    return out.reshape(-1, kinds * width)


class Staged:
    turn = True

    def __init__(self):
        index = lax.axis_index("dp")
        self.z, self.x, self.c = index // (NX * NC), (index // NC) % NX, index % NC
        self.position = jnp.stack([self.z, self.x, self.c]).astype(jnp.int32)

    def gather_first(self, u1, shard_qkv, shard_out, shard_up, shard_down):
        self.hidden = shard_up.shape[1]
        first = spread_z(shard_qkv)
        u1, *first, shard = tie(u1, *first, jnp.concatenate([shard_up, shard_out], axis=1))
        column = jnp.stack(first)
        own = spread_z(shard)
        both_down = jnp.concatenate([shard_down, swap_y(shard_down)], axis=1)
        from_x, both_down, *own = tie(swap_x(column), both_down, *own)
        self.own = jnp.stack(own)
        self.own_x, self.other = swap_x(self.own), swap_y(self.own)
        self.down = lax.all_gather(both_down, "dp", axis=0, tiled=True)
        pieces = [column, from_x]
        pieces += [swap_core(a) for a in pieces]
        return u1, assemble_qkv(self.position, pieces)

    def beside_forward(self, index, values):
        if index == 0:
            *values, self.own, self.own_x, self.other = tie(*values, self.own, self.own_x, self.other)
            self.other_x = swap_x(self.other)
            self.cores = [swap_core(a) for a in (self.own, self.own_x, self.other)]
        if index == 1:
            n = len(values)
            values = tie(*values, *self.cores)
            values, self.cores = values[:n], list(values[n:])
        if index == 2:
            *values, self.other_x = tie(*values, self.other_x)
            self.cores.append(swap_core(self.other_x))
        return values

    def gather_last(self, *attended):
        groups = [
            [self.own, self.own_x, *self.cores[:2]],
            [self.other, self.other_x, *self.cores[2:]],
        ]
        up = piece_blocks(groups, self.hidden)
        return attended, [p for g in groups for p in g], up, whole_blocks(self.down)

    def reduce_down(self, grad):
        self.down = lax.psum_scatter(grad, "dp", scatter_dimension=0, tiled=True)

    def rows_times(self, left, index, right, terms=()):
        parts = NC if not terms else NC * NX
        left = left.reshape(parts, -1, left.shape[-1])
        return grad_rows(left, jnp.stack(index), right, terms)

    def reduce_first(self, send, keep, turned, o_own, d_o_rows):
        up_there = swap_core(send)
        out_there = swap_core(self.rows_times(turned, [1 - self.c, self.c], o_own))
        out_keep = self.rows_times(turned, [self.c, self.c], o_own)
        out_there, up_there, out_keep, *d_o_rows = tie(out_there, up_there, out_keep, *d_o_rows)
        self.outs, self.ups = [out_keep, out_there], [keep, up_there]
        zero = jnp.zeros((1,), jnp.int32)
        send, *d_o_rows = tie(merge(zero, keep.shape[0], self.outs, self.ups, 1), *d_o_rows)
        self.from_y = swap_y(send)
        return d_o_rows

    def beside_backward(self, index, d_qkv):
        if index == 2:
            d_qkv, self.from_y = tie(d_qkv, self.from_y)
            rows = self.from_y.shape[0] // NX

            def part(x):
                return merge(jnp.reshape(x, (1,)), rows, self.outs, self.ups, 0, [self.from_y])

            send, d_qkv = tie(part(1 - self.x), d_qkv)
            self.from_x, self.here = swap_x(send), part
        if index == 3:
            d_qkv, self.from_x = tie(d_qkv, self.from_x)
        return d_qkv

    def reduce_z(self, total):
        total = total.reshape(NZ, -1, total.shape[1])
        out = pick(total, self.z).astype(F32)
        for k in range(1, NZ):
            piece = pick(total, lax.rem(self.z + k, NZ))
            out = out + lax.ppermute(piece, "dp", z_pairs(k)).astype(F32)
        return out

    def tail(self, turned, d_qkv, d_in_own, terms):
        send = self.rows_times(turned, [1 - self.c, self.c], d_qkv)
        there = swap_core(send)
        d_qkv, send, *parts = tie(d_qkv, send, *self.outs, *self.ups)
        self.outs, self.ups = parts[:2], parts[2:]
        there, total = tie(there, add(self.here(self.x), self.from_x))
        from_core = there.reshape(NX, -1, there.shape[-1])
        parts = lambda x, d_qkv: self.rows_times(turned, [self.c * NX + x, x], d_qkv, [from_core])
        send, d_qkv = tie(parts(1 - self.x, d_qkv), d_qkv)
        own = d_in_own(d_qkv)
        keep = parts(self.x, d_qkv)
        there, received, keep, first, *rest = tie(swap_x(send), terms[1], keep, *own)
        own = [first, *rest]
        total = self.reduce_z(total)
        qkv = self.reduce_z(add(keep, there))
        width = self.outs[0].shape[1] // 2
        return own, total[:, width:], total[:, :width], qkv, [None, received]

    def reduce_down_last(self, terms):
        *terms, down = tie(*terms, self.down)
        half = down.shape[1] // 2
        return terms, down[:, :half].astype(F32) + swap_y(down[:, half:]).astype(F32)

    def exchange(self, parts):
        return [parts[0], swap_y(parts[1])]

    def total(self, vector):
        for bit in (1, NC, NX * NC, 2 * NX * NC):
            vector = vector + lax.ppermute(vector, "dp", flips(bit))
        return vector + swap_y(vector)


class Plain:
    turn = False

    def __init__(self):
        self.n = lax.axis_size("tensor")
        self.position = jnp.zeros((3,), jnp.int32)
        self.rank = lax.axis_index("tensor")

    def gather_groups(self, shard):
        own = lax.all_gather(shard, "dp", axis=0, tiled=True)
        every = lax.all_gather(own, "tensor", axis=0)
        return jnp.concatenate([pick(every, (self.rank + g) % self.n) for g in range(self.n)], axis=1)

    def gather_first(self, u1, shard_qkv, *shards):
        weights = [self.gather_groups(w) for w in shards]
        self.weights = [weights[:1], *(whole_blocks(w) for w in weights[1:])]
        every = lax.all_gather(shard_qkv, "dp", axis=1, tiled=True)
        pairs = jnp.split(every, every.shape[2] // PAIR, axis=2)
        return u1, jnp.concatenate([p[j] for p in pairs for j in range(3)], axis=1)

    def beside_forward(self, index, values):
        return values

    def gather_last(self, *attended):
        return attended, *self.weights

    def reduce_rows(self, grad):
        grads = self.absolute(jnp.split(grad, self.n, axis=1))
        own = lax.psum_scatter(grads, "tensor", scatter_dimension=0, tiled=True)
        return lax.psum_scatter(own[0], "dp", scatter_dimension=0, tiled=True).astype(F32)

    def reduce_down(self, grad):
        self.down = self.reduce_rows(grad)

    def reduce_first(self, send, keep, turned, o_own, d_o_rows):
        self.up = self.reduce_rows(jnp.concatenate([keep, send], axis=0))
        self.out = self.reduce_rows(dot(turned, o_own, NN).astype(BF16))
        return d_o_rows

    def beside_backward(self, index, d_qkv):
        return d_qkv

    def tail(self, turned, d_qkv, d_in_own, terms):
        grad = dot(turned, d_qkv, NN).astype(BF16)
        qkv = lax.psum_scatter(grad, "dp", scatter_dimension=0, tiled=True).astype(F32)
        return d_in_own(d_qkv), self.up, self.out, qkv, terms

    def reduce_down_last(self, terms):
        return terms, self.down

    def absolute(self, parts):
        order = (jnp.arange(self.n) - self.rank) % self.n
        return jnp.take(jnp.stack(parts), order, axis=0)

    def exchange(self, parts):
        got = lax.all_to_all(self.absolute(parts), "tensor", 0, 0, tiled=True)
        return [pick(got, (self.rank + g) % self.n) for g in range(self.n)]

    def total(self, vector):
        return lax.psum(vector, ("dp", "tensor"))


def per_device(
    staged,
    inputs,
    cotangent,
    segment_ids,
    w_qkv,
    w_out,
    w_fc1,
    w_fc2,
    norm_gain,
    norm_bias,
    head_bias,
    out_bias,
    fc1_bias,
):
    n = lax.axis_size("tensor")
    rank = lax.axis_index("tensor")
    comm = Staged() if staged else Plain()
    tokens, features = inputs.shape
    seqs, length = segment_ids.shape
    own_rows = tokens // n
    width = w_qkv.shape[2]
    hidden = w_fc1.shape[1]

    def group_slice(array, g, size, axis=0):
        return lax.dynamic_slice_in_dim(array, ((rank + g) % n) * size, size, axis)

    def scalar(value):
        return jnp.reshape(value, (1,)).astype(jnp.int32)

    row_at = [scalar(((rank + g) % n) * (own_rows // ROWS)) for g in range(n)]

    u1, turned1 = first_norm(comm.turn, inputs, norm_gain, norm_bias)
    u1, weight_qkv = comm.gather_first(
        u1,
        w_qkv.astype(BF16),
        w_out.T.astype(BF16),
        w_fc1.astype(BF16),
        w_fc2.T.astype(BF16),
    )
    pairs = width // PAIR
    heads_bias = group_slice(head_bias, 0, width, 1)
    qkv_bias = jnp.stack([heads_bias[0], jnp.zeros((width,), F32), heads_bias[1]])
    qkv_bias = qkv_bias.reshape(3, pairs, PAIR).transpose(1, 0, 2).reshape(-1)
    qkv = (dot(u1, weight_qkv, NN) + qkv_bias).astype(BF16)

    starts, lo = segment_bounds(segment_ids)
    blocks = length // QB
    halves = 2 if n == 2 and seqs == 1 else 1
    half = blocks // halves
    places = [(rank + g) % halves for g in range(halves)]
    per_call = math.gcd(pairs, 2)
    calls = pairs // per_call
    o_rows, lse_rows = ([[None] * calls for _ in range(halves)] for _ in range(2))
    received = [None] * calls
    index = 0
    for g in reversed(range(halves)):
        for i in range(calls):
            o, lse = attention_forward(
                i * per_call, per_call, qkv, starts, lo, scalar(places[g] * half), half
            )
            qkv, o, lse = comm.beside_forward(index, [qkv, o, lse])
            o_rows[g][i], lse_rows[g][i] = o, lse
            if g > 0:
                received[i] = comm.exchange([None, o])[1]
            index += 1
    if halves < n:
        whole = jnp.concatenate(o_rows[0], axis=1)
        o_groups = comm.exchange([group_slice(whole, g, own_rows) for g in range(n)])
        _, weight_out, up, down = comm.gather_last()
    else:
        o_groups, weight_out, up, down = comm.gather_last(*o_rows[0], *received)
        o_rows[0] = list(o_groups[:calls])

    at = jnp.concatenate([row_at[0], comm.position])
    attn, resid, u2, o_own, turned2, weight_out = middle(
        comm.turn, at, o_groups, weight_out, inputs, norm_gain, norm_bias, out_bias
    )
    hidden_bias = jnp.concatenate([group_slice(fc1_bias, g, hidden) for g in range(n)])
    pre, output, d_mlp, d_mlp_turned, sums3 = feed(
        at, u2, up, down, hidden_bias[None], resid, cotangent, norm_gain, norm_bias, out_bias
    )
    send, keep, bias_hidden, d_resid, sums12, turned_attn, *d_o = feed_back(
        comm.turn,
        n,
        at,
        d_mlp,
        turned2,
        pre,
        up,
        down,
        resid,
        attn,
        cotangent,
        weight_out,
        norm_gain,
    )
    d_mlp_turned, *d_o = tie(d_mlp_turned, *d_o)
    d_o_rows = comm.exchange(d_o)
    grad_down, *d_o_rows = tie(grad_down_of(d_mlp_turned, pre), *d_o_rows)
    comm.reduce_down(grad_down)
    if halves < n:
        order = (jnp.arange(n) - rank) % n
        d_o_rows = [jnp.take(jnp.stack(d_o_rows), order, axis=0).reshape(tokens, width)]
    d_o_rows = comm.reduce_first(send, keep, turned_attn, o_own, d_o_rows)

    d_qkv = None
    for pair in range(pairs):
        i, column = divmod(pair, per_call)
        d_qkv = attention_backward(
            pair,
            qkv,
            [o[i] for o in o_rows],
            d_o_rows,
            [l[i] for l in lse_rows],
            column,
            starts,
            lo,
            scalar(places[0]),
            d_qkv,
        )
        d_qkv = comm.beside_backward(pair, d_qkv)

    d_u1_parts, sums0, head_sums = [None] * n, 0.0, 0.0
    for g in reversed(range(1, n)):
        d_u1_parts[g], sums, head_row = d_in(row_at[g], own_rows, d_qkv, weight_qkv, inputs)
        d_u1_parts[g], d_qkv = tie(d_u1_parts[g], d_qkv)
        sums0, head_sums = sums0 + sums, head_sums + head_row[0]
    d_u1_terms = comm.exchange(d_u1_parts) if staged else None
    (d_u1_parts[0], sums, head_row), grad_up, grad_out, grad_qkv, d_u1_terms = comm.tail(
        turned1,
        d_qkv,
        lambda d_qkv: d_in(row_at[0], own_rows, d_qkv, weight_qkv, inputs),
        d_u1_terms,
    )
    sums0, head_sums = sums0 + sums, head_sums + head_row[0]
    if staged:
        d_u1_terms = [d_u1_parts[0], *d_u1_terms[1:]]
    else:
        d_u1_terms = comm.exchange(d_u1_parts)

    hidden_full = jnp.roll(bias_hidden[0], rank * hidden)
    head_terms = head_sums.reshape(pairs, 3, PAIR).transpose(1, 0, 2).reshape(3, width)[0::2]
    head_full = lax.dynamic_update_slice_in_dim(
        jnp.zeros(head_bias.shape, F32), head_terms, rank * width, 1
    )
    gains = [sums0[0], sums12[2], sums12[0], sums3[0]]
    shifts = [sums0[1], sums12[3], sums12[1], sums3[1]]
    rows = jnp.stack(gains + shifts + [sums12[4], sums3[2]])
    small = jnp.concatenate([rows, head_full, hidden_full.reshape(-1, features)])
    small, *d_u1_terms = tie(small, *d_u1_terms)
    small = comm.total(small)
    d_u1_terms, grad_down = comm.reduce_down_last(d_u1_terms)
    d_inputs = last(row_at[0], d_u1_terms, inputs, d_resid, norm_gain)

    grad_qkv = grad_qkv.reshape(-1, pairs, 3, PAIR).transpose(2, 0, 1, 3).reshape(3, -1, width)
    return (
        output,
        d_inputs,
        grad_qkv,
        grad_out.T,
        grad_up,
        grad_down.T,
        small[0:4],
        small[4:8],
        small[10:12],
        small[8:10],
        small[12:].reshape(-1),
    )


def solution(mesh):
    staged = mesh.shape["dp"] == NZ * NX * NC and mesh.shape["tensor"] == 2
    return jax.shard_map(
        functools.partial(per_device, staged),
        mesh=mesh,
        in_specs=(
            P("dp", None),
            P("dp", None),
            P("dp", None),
            P(None, "dp", "tensor"),
            P("tensor", "dp"),
            P("dp", "tensor"),
            P("tensor", "dp"),
            P(),
            P(),
            P(),
            P(),
            P(),
        ),
        out_specs=(
            P(("dp", "tensor"), None),
            P(("dp", "tensor"), None),
            P(None, "dp", "tensor"),
            P("tensor", "dp"),
            P("dp", "tensor"),
            P("tensor", "dp"),
            P(),
            P(),
            P(),
            P(),
            P(),
        ),
        check_vma=False,
    )
```

```python
import functools
import math

import jax
import jax.numpy as jnp
from jax import lax
from jax.experimental import pallas as pl
from jax.experimental.pallas import tpu as pltpu
from jax.sharding import PartitionSpec as P

HD = 64
QB = 256
KB = 256
MAX_SEGMENT = 1024
max_chunks = MAX_SEGMENT // KB + 1
SCORE_SCALE = 0.125 * math.log2(math.e)
NEG = -1e30
EPS = 1e-05
BF16 = jnp.bfloat16
F32 = jnp.float32
NT = (((1,), (1,)), ((), ()))
NN = (((1,), (0,)), ((), ()))
TN = (((0,), (0,)), ((), ()))

SMALL = pl.CostEstimate(flops=1, bytes_accessed=1, transcendentals=0)
VMEM = 60 << 20
PAIR = 2 * HD


def dot(a, b, dims):
    return lax.dot_general(a, b, dims, preferred_element_type=jnp.float32)


def split_pair(block):
    lane = lax.broadcasted_iota(jnp.int32, block.shape, 1)
    zero = jnp.zeros_like(block)
    return (jnp.where(lane < HD, block, zero), jnp.where(lane >= HD, block, zero))


def fwd_kernel(pairs, lo_ref, off_ref, *refs):
    q_refs, k_refs, v_refs = refs[:pairs], refs[pairs : 2 * pairs], refs[2 * pairs : 3 * pairs]
    start_ref, o_ref, l_ref, vt_ref = refs[3 * pairs :]
    step = pl.program_id(1)
    block = off_ref[0] + step

    @pl.when(step == 0)
    def _():
        for pair in range(pairs):
            vt_ref[pair] = v_refs[pair][...].T

    pair_step = math.gcd(pairs, 4)
    row_start = start_ref[...]
    query_pos = block * QB + lax.broadcasted_iota(jnp.int32, (1, QB), 1)
    first = lo_ref[pl.program_id(0), block]
    count = block + 1 - first
    base = pl.multiple_of(first * KB, KB)

    for chunks in range(1, max_chunks + 1):

        @pl.when(count == chunks)
        def _(size=chunks * KB):
            window = pl.ds(base, size)
            key_pos = lax.broadcasted_iota(jnp.int32, (size, QB), 0) + base
            ok = (key_pos >= row_start) & (key_pos <= query_pos)
            for pair in range(pairs):
                q_heads = split_pair(q_refs[pair][...])
                keys = k_refs[pair][window, :]
                outs = []
                for h in range(2):
                    s = jnp.where(ok, dot(keys, q_heads[h], NT) * SCORE_SCALE, NEG)
                    peak = jnp.max(s, axis=0, keepdims=True)
                    p = jnp.exp2(s - peak)
                    total = jnp.sum(p, axis=0, keepdims=True)
                    vt = vt_ref[pair, h * HD : (h + 1) * HD, window]
                    outs.append(dot(vt, p.astype(BF16), NN) / total)
                    l_ref[pair, h : h + 1, :] = peak + jnp.log2(total)
                cols = slice(pair * PAIR, (pair + 1) * PAIR)
                o_ref[:, cols] = jnp.concatenate(outs, axis=0).T.astype(BF16)


def attention_forward(first, pairs, qkv, starts, lo, offset, blocks):
    seqs, length = starts.shape
    nq = length // QB
    every = range(first, first + pairs)

    def rows_at(p):
        return pl.BlockSpec((QB, PAIR), lambda s, b, lo, off: (s * nq + off[0] + b, 3 * p))

    def all_at(p, kind):
        return pl.BlockSpec((length, PAIR), lambda s, b, lo, off: (s, 3 * p + kind))

    grid_spec = pltpu.PrefetchScalarGridSpec(
        num_scalar_prefetch=2,
        grid=(seqs, blocks),
        in_specs=[rows_at(p) for p in every]
        + [all_at(p, kind) for kind in (1, 2) for p in every]
        + [pl.BlockSpec((None, 1, QB), lambda s, b, lo, off: (s, 0, off[0] + b))],
        out_specs=[
            pl.BlockSpec((QB, pairs * PAIR), lambda s, b, lo, off: (s * blocks + b, 0)),
            pl.BlockSpec((None, pairs, 2, QB), lambda s, b, lo, off: (s, 0, 0, b)),
        ],
        scratch_shapes=[pltpu.VMEM((pairs, PAIR, length), BF16)],
    )
    return pl.pallas_call(
        functools.partial(fwd_kernel, pairs),
        grid_spec=grid_spec,
        out_shape=(
            jax.ShapeDtypeStruct((seqs * blocks * QB, pairs * PAIR), BF16),
            jax.ShapeDtypeStruct((seqs, pairs, 2, blocks * QB), F32),
        ),
        compiler_params=pltpu.CompilerParams(
            dimension_semantics=("arbitrary",) * 2, vmem_limit_bytes=VMEM
        ),
        cost_estimate=SMALL,
        name="attention_forward",
    )(lo, offset, *[qkv] * (3 * pairs), starts[:, None, :])


def bwd_kernel(halves, lo_ref, place_ref, q_ref, k_ref, v_ref, start_ref, *refs):
    o_refs, do_refs, l_refs = refs[:halves], refs[halves : 2 * halves], refs[2 * halves : 3 * halves]
    out_ref, kt_ref, dk_ref, dv_ref = refs[-4:]
    block = pl.program_id(1)
    blocks = pl.num_programs(1)
    @pl.when(block == 0)
    def _():
        kt_ref[...] = k_ref[...].T
        dk_ref[...] = jnp.zeros_like(dk_ref)
        dv_ref[...] = jnp.zeros_like(dv_ref)

    mine = block // (blocks // halves) == place_ref[0]

    def pick(two, index=slice(None)):
        if halves == 1:
            return two[0][index]
        return jnp.where(mine, two[0][index], two[1][index])

    row_start = start_ref[...]
    query_pos = block * QB + lax.broadcasted_iota(jnp.int32, (1, QB), 1)
    key_iota = lax.broadcasted_iota(jnp.int32, (KB, QB), 0)
    first = lo_ref[pl.program_id(0), block]
    last = (block + 1) * (QB // KB)
    rows = pl.ds(pl.multiple_of(block * QB, QB), QB)
    q_heads = split_pair(q_ref[...])
    g_pair = pick(do_refs)
    g_heads = split_pair(g_pair)
    prod = (g_pair.astype(F32) * pick(o_refs).astype(F32)).T
    deltas = [jnp.sum(prod[h * HD : (h + 1) * HD], axis=0, keepdims=True) for h in range(2)]
    lses = [pick(l_refs, slice(h, h + 1)) for h in range(2)]

    def chunk(j, carry):
        base = pl.multiple_of(j * KB, KB)
        window = pl.ds(base, KB)
        keys = k_ref[window, :]
        vals = v_ref[window, :]
        key_pos = key_iota + base
        ok = (key_pos >= row_start) & (key_pos <= query_pos)
        new = []
        dv = dv_ref[window, :]
        dk = dk_ref[window, :]
        for h in range(2):
            s = jnp.where(ok, dot(keys, q_heads[h], NT) * SCORE_SCALE, NEG)
            p = jnp.exp2(s - lses[h])
            dp = dot(vals, g_heads[h], NT)
            ds = (p * (dp - deltas[h])).astype(BF16)
            dv = dv + dot(p.astype(BF16), g_heads[h], NN)
            dk = dk + dot(ds, q_heads[h], NN)
            kt = kt_ref[h * HD : (h + 1) * HD, window]
            new.append(carry[h] + dot(kt, ds, NN))
        dv_ref[window, :] = dv
        dk_ref[window, :] = dk
        return tuple(new)

    dq = lax.fori_loop(first, last, chunk, tuple(jnp.zeros((HD, QB), F32) for _ in range(2)))
    out_ref[rows, :PAIR] = (jnp.concatenate(dq, axis=0) * 0.125).T.astype(BF16)

    @pl.when(block == blocks - 1)
    def _():
        out_ref[:, PAIR : 2 * PAIR] = (dk_ref[...] * 0.125).astype(BF16)
        out_ref[:, 2 * PAIR :] = dv_ref[...].astype(BF16)


def attention_backward(pair, qkv, o_rows, d_o_rows, lse_rows, column, starts, lo, place, before):
    seqs, length = starts.shape
    nq = length // QB
    halves = len(o_rows)
    half = nq // halves

    def row(g, s, b, place):
        if halves == 1:
            return s, b, s * nq + b
        at = jnp.clip(b - jnp.bitwise_xor(place[0], g) * half, 0, half - 1)
        return s, at, at

    def rows_of(g, col):
        return pl.BlockSpec((QB, PAIR), lambda s, b, lo, place: (row(g, s, b, place)[2], col))

    def lse_of(g):
        return pl.BlockSpec(
            (None, None, 2, QB), lambda s, b, lo, place: (s, column, 0, row(g, s, b, place)[1])
        )

    in_specs = [
        pl.BlockSpec((QB, PAIR), lambda s, b, lo, place: (s * nq + b, 3 * pair)),
        pl.BlockSpec((length, PAIR), lambda s, b, lo, place: (s, 3 * pair + 1)),
        pl.BlockSpec((length, PAIR), lambda s, b, lo, place: (s, 3 * pair + 2)),
        pl.BlockSpec((None, 1, QB), lambda s, b, lo, place: (s, 0, b)),
        *[rows_of(g, column) for g in range(halves)],
        *[rows_of(g, pair) for g in range(halves)],
        *[lse_of(g) for g in range(halves)],
    ]
    operands = [qkv, qkv, qkv, starts[:, None, :], *o_rows, *d_o_rows, *lse_rows]
    alias = {}
    if before is not None:
        alias = {2 + len(operands): 0}
        in_specs.append(pl.BlockSpec(memory_space=pl.ANY))
        operands.append(before)
    return pl.pallas_call(
        functools.partial(bwd_kernel, halves),
        grid_spec=pltpu.PrefetchScalarGridSpec(
            num_scalar_prefetch=2,
            grid=(seqs, nq),
            in_specs=in_specs,
            out_specs=pl.BlockSpec((length, 3 * PAIR), lambda s, b, lo, place: (s, pair)),
            scratch_shapes=[
                pltpu.VMEM((PAIR, length), BF16),
                pltpu.VMEM((length, PAIR), F32),
                pltpu.VMEM((length, PAIR), F32),
            ],
        ),
        out_shape=jax.ShapeDtypeStruct(qkv.shape, BF16),
        input_output_aliases=alias,
        compiler_params=pltpu.CompilerParams(
            dimension_semantics=("arbitrary", "arbitrary"), vmem_limit_bytes=VMEM
        ),
        cost_estimate=SMALL,
        name="attention_backward",
    )(lo, place, *operands)


def segment_bounds(segment_ids):
    starts = jnp.sum((segment_ids[:, None, :] < segment_ids[:, :, None]).astype(jnp.int32), axis=2)
    return starts, starts[:, ::QB] // KB


ROWS = 256
HIDDEN_BLOCK = 1024
NZ, NX, NC = 4, 2, 2


def unit_rows(v):
    centered = v - jnp.mean(v, axis=-1, keepdims=True)
    scale = lax.rsqrt(jnp.mean(centered * centered, axis=-1, keepdims=True) + EPS)
    return centered * scale, scale


def norm_back(normed, scale, inner):
    return scale * (
        inner
        - jnp.mean(inner, axis=-1, keepdims=True)
        - normed * jnp.mean(inner * normed, axis=-1, keepdims=True)
    )


def rows_sum(v):
    return jnp.sum(v, axis=0, keepdims=True)


def store_turned(ref, block, by_device):
    turned = block.T
    if not by_device:
        ref[...] = turned
        return
    size = turned.shape[0] // (NZ * NX * NC)
    for z in range(NZ):
        for x in range(NX):
            for c in range(NC):
                old = ((z * NX + x) * NC + c) * size
                new = ((c * NX + x) * NZ + z) * size
                ref[new : new + size, :] = turned[old : old + size]


def turned_spec(features):
    return pl.BlockSpec((features, ROWS), lambda i, *_: (0, i))


def fixed(shape):
    return pl.BlockSpec(shape, lambda *_: (0,) * len(shape), pipeline_mode=pl.Buffered(1))


def call(body, name, grid, ins, outs, shapes, operands, prefetch=(), scratch=(), vmem=VMEM, micros=0):
    return pl.pallas_call(
        body,
        grid_spec=pltpu.PrefetchScalarGridSpec(
            num_scalar_prefetch=len(prefetch),
            grid=grid,
            in_specs=ins,
            out_specs=outs,
            scratch_shapes=scratch,
        ),
        out_shape=shapes,
        compiler_params=pltpu.CompilerParams(
            dimension_semantics=("arbitrary",) * len(grid), vmem_limit_bytes=vmem
        ),
        cost_estimate=pl.CostEstimate(
            flops=1 + int(micros * 1.1e9), bytes_accessed=1, transcendentals=0
        ),
        name=name,
    )(*prefetch, *operands)


def shaped(rows, cols, dtype):
    return jax.ShapeDtypeStruct((rows, cols), dtype)


def row_spec(cols):
    return pl.BlockSpec((ROWS, cols), lambda i, *_: (i, 0))


def shifted_spec(cols):
    return pl.BlockSpec((ROWS, cols), lambda i, at, *_: (at[0] + i, 0))


def first_norm_kernel(turn, x_ref, gain_ref, bias_ref, u_ref, turned_ref):
    normed, _ = unit_rows(x_ref[...].astype(F32))
    u = (normed * gain_ref[0:1, :] + bias_ref[0:1, :]).astype(BF16)
    u_ref[...] = u
    store_turned(turned_ref, u, turn)


def first_norm(turn, inputs, gain, bias):
    tokens, features = inputs.shape
    return call(
        functools.partial(first_norm_kernel, turn),
        "first_norm",
        (tokens // ROWS,),
        [row_spec(features), fixed(gain.shape), fixed(bias.shape)],
        [row_spec(features), turned_spec(features)],
        [shaped(tokens, features, BF16), shaped(features, tokens, BF16)],
        [inputs, gain, bias],
        vmem=24 << 20,
    )


class Blocks:
    def __init__(self, operands, specs, load):
        self.operands, self.specs, self.load = operands, specs, load


def whole_blocks(weight):
    steps = weight.shape[1] // HIDDEN_BLOCK
    spec = pl.BlockSpec(
        (weight.shape[0], HIDDEN_BLOCK), lambda j, *_: (0, jnp.minimum(j, steps - 1))
    )

    def load(at_ref, step, refs, hold_ref):
        hold_ref[...] = refs[0][...]

    return Blocks([weight], [spec], load)


def piece_blocks(groups, columns):
    rows = groups[0][0].shape[1]
    steps = columns // HIDDEN_BLOCK
    operands, specs = [], []
    for g, pieces in enumerate(groups):
        for piece in pieces:
            operands.append(piece)
            specs.append(
                pl.BlockSpec(
                    (NZ, rows, HIDDEN_BLOCK),
                    lambda j, *_, g=g: (0, 0, jnp.clip(j - g * steps, 0, steps - 1)),
                )
            )

    def load(at_ref, step, refs, hold_ref):
        for g in range(len(groups)):

            @pl.when(step // steps == g)
            def _(g=g):
                place_pieces(at_ref, refs[4 * g : 4 * g + 4], hold_ref, rows)

    return Blocks(operands, specs, load)


def place_pieces(at_ref, refs, hold_ref, rows):
    z, x, c = at_ref[1], at_ref[2], at_ref[3]
    for n, ref in enumerate(refs):
        dx, dc = n % 2, n // 2
        for k in range(NZ):
            index = lax.rem(z - k + NZ, NZ) * NX + lax.bitwise_xor(x, dx)
            row = pl.multiple_of((index * NC + lax.bitwise_xor(c, dc)) * rows, rows)
            hold_ref[pl.ds(row, rows), :] = ref[k]


def middle_kernel(turn, groups, pieces, at_ref, *refs):
    o_refs, w_refs = refs[:groups], refs[groups : groups + pieces]
    x_ref, gain_ref, bias_ref, ob_ref = refs[groups + pieces : groups + pieces + 4]
    attn_ref, resid_ref, u_ref, o_ref, turned_ref, w_ref = refs[groups + pieces + 4 :]
    width = w_refs[0].shape[2] if pieces > 1 else 0

    @pl.when(pl.program_id(0) == 0)
    def _():
        if pieces == 1:
            w_ref[...] = w_refs[0][...]
        else:
            for g in range(pieces // 4):
                place_pieces(
                    at_ref,
                    w_refs[4 * g : 4 * g + 4],
                    w_ref.at[:, g * width : (g + 1) * width],
                    w_refs[0].shape[1],
                )

    attn = ob_ref[0:1, :]
    width = o_refs[0].shape[1]
    for g in range(groups):
        cols = slice(g * width, (g + 1) * width)
        o_ref[:, cols] = o_refs[g][...]
        attn = attn + dot(o_refs[g][...], w_ref[:, cols], NT)
    attn_ref[...] = attn
    normed, _ = unit_rows(attn)
    resid = x_ref[...].astype(F32) + normed * gain_ref[1:2, :] + bias_ref[1:2, :]
    resid_ref[...] = resid
    normed, _ = unit_rows(resid)
    u = (normed * gain_ref[2:3, :] + bias_ref[2:3, :]).astype(BF16)
    u_ref[...] = u
    store_turned(turned_ref, u, turn)


def middle(turn, at, o_groups, weight_out, inputs, gain, bias, out_bias):
    rows, width = o_groups[0].shape
    features = inputs.shape[1]
    if len(weight_out) == 1:
        weight_specs = [fixed(weight_out[0].shape)]
    else:
        part = features * 4 // len(weight_out)
        last = weight_out[0].shape[2] // part - 1
        shape = (NZ, weight_out[0].shape[1], part)
        spec = pl.BlockSpec(shape, lambda *_: (0, 0, last), pipeline_mode=pl.Buffered(1))
        weight_specs = [spec] * len(weight_out)
    return call(
        functools.partial(middle_kernel, turn, len(o_groups), len(weight_out)),
        "middle",
        (rows // ROWS,),
        [row_spec(width)] * len(o_groups)
        + weight_specs
        + [shifted_spec(features)]
        + [fixed(a.shape) for a in (gain, bias, out_bias)],
        [row_spec(features)] * 4 + [turned_spec(features), fixed((features, features))],
        [shaped(rows, features, d) for d in (F32, F32, BF16, BF16)]
        + [shaped(features, rows, BF16), shaped(features, features, BF16)],
        [*o_groups, *weight_out, inputs, gain, bias, out_bias],
        prefetch=[at],
    )


GELU_C = math.sqrt(2.0 / math.pi)


def gelu_tanh_of(z):
    square = z * z
    return square, jnp.tanh(z * (GELU_C + (GELU_C * 0.044715) * square))


def later_spec(cols, steps, shift=False):
    if shift:
        return pl.BlockSpec((ROWS, cols), lambda j, at, *_: (at[0] + jnp.maximum(j - steps, 0), 0))
    return pl.BlockSpec((ROWS, cols), lambda j, *_: (jnp.maximum(j - steps, 0), 0))


def later_turned(features, steps):
    return pl.BlockSpec((features, ROWS), lambda j, *_: (0, jnp.maximum(j - steps, 0)))


def column_spec(rows, steps):
    return pl.BlockSpec((rows, HIDDEN_BLOCK), lambda j, *_: (0, jnp.minimum(j, steps - 1)))


def feed_kernel(up, down, steps, at_ref, u_ref, b_ref, *refs):
    n, m = len(up.operands), len(down.operands)
    up_refs, down_refs = refs[:n], refs[n : n + m]
    resid_ref, dy_ref, gain_ref, bias_ref, ob_ref = refs[n + m : n + m + 5]
    pre_ref, out_ref, d_ref, turned_ref, sum_ref, up_hold, down_hold, total_ref = refs[n + m + 5 :]
    step = pl.program_id(0)
    rows = u_ref.shape[0]

    @pl.when(step == 0)
    def _():
        total_ref[...] = jnp.zeros_like(total_ref)
        sum_ref[...] = jnp.zeros_like(sum_ref)

    @pl.when(step < steps)
    def _():
        up.load(at_ref, step, up_refs, up_hold)
        down.load(at_ref, step, down_refs, down_hold)
        for r in range(0, rows, ROWS):
            part = slice(r, r + ROWS)
            z = dot(u_ref[part, :], up_hold[...], NN) + b_ref[...]
            pre_ref[part, :] = z.astype(BF16)
            _, t = gelu_tanh_of(z)
            act = (z * (0.5 + 0.5 * t)).astype(BF16)
            total_ref[part, :] += dot(act, down_hold[...], NT)

    @pl.when(step >= steps)
    def _():
        mlp = total_ref[pl.ds(pl.multiple_of((step - steps) * ROWS, ROWS), ROWS), :] + ob_ref[1:2, :]
        normed, scale = unit_rows(mlp)
        out_ref[...] = (resid_ref[...] + normed * gain_ref[3:4, :] + bias_ref[3:4, :]).astype(BF16)
        dy = dy_ref[...].astype(F32)
        d_mlp = norm_back(normed, scale, dy * gain_ref[3:4, :]).astype(BF16)
        d_ref[...] = d_mlp
        store_turned(turned_ref, d_mlp, False)
        sum_ref[0:1, :] += rows_sum(normed * dy)
        sum_ref[1:2, :] += rows_sum(dy)
        sum_ref[2:3, :] += rows_sum(d_mlp.astype(F32))


def feed(at, u, up, down, hidden_bias, resid, cotangent, gain, bias, out_bias):
    rows, features = u.shape
    hidden = hidden_bias.shape[1]
    steps = hidden // HIDDEN_BLOCK
    return call(
        functools.partial(feed_kernel, up, down, steps),
        "feed",
        (steps + rows // ROWS,),
        [fixed(u.shape), column_spec(1, steps), *up.specs, *down.specs]
        + [later_spec(features, steps), later_spec(features, steps, True)]
        + [fixed(a.shape) for a in (gain, bias, out_bias)],
        [column_spec(rows, steps), later_spec(features, steps), later_spec(features, steps)]
        + [later_turned(features, steps), fixed((8, features))],
        [shaped(rows, hidden, BF16), shaped(rows, features, BF16), shaped(rows, features, BF16)]
        + [shaped(features, rows, BF16), shaped(8, features, F32)],
        [u, hidden_bias, *up.operands, *down.operands, resid, cotangent, gain, bias, out_bias],
        prefetch=[at],
        scratch=[
            pltpu.VMEM((features, HIDDEN_BLOCK), BF16),
            pltpu.VMEM((features, HIDDEN_BLOCK), BF16),
            pltpu.VMEM((rows, features), F32),
        ],
    )


def feed_back_kernel(turn, groups, up, down, steps, at_ref, d_ref, ut_ref, pre_ref, *refs):
    n, m = len(up.operands), len(down.operands)
    up_refs, down_refs = refs[:n], refs[n : n + m]
    resid_ref, attn_ref, dy_ref, wo_ref, gain_ref = refs[n + m : n + m + 5]
    refs = refs[n + m + 5 :]
    send_ref, keep_ref, hid_ref, d_resid_ref, sum_ref, turned_ref = refs[:6]
    d_o_refs = refs[6 : 6 + groups]
    up_hold, down_hold, total_ref = refs[6 + groups :]
    step = pl.program_id(0)
    rows, features = d_ref.shape
    half = features // NC

    @pl.when(step == 0)
    def _():
        total_ref[...] = jnp.zeros_like(total_ref)
        sum_ref[...] = jnp.zeros_like(sum_ref)

    @pl.when(step < steps)
    def _():
        up.load(at_ref, step, up_refs, up_hold)
        down.load(at_ref, step, down_refs, down_hold)
        column_sum = 0.0
        d_pres = []
        for r in range(0, rows, ROWS):
            part = slice(r, r + ROWS)
            d_act = dot(d_ref[part, :], down_hold[...], NN)
            z = pre_ref[part, :].astype(F32)
            square, t = gelu_tanh_of(z)
            gate = 0.5 + 0.5 * t
            slope = gate + (1.0 - t * t) * (
                z * (0.5 * GELU_C + (1.5 * GELU_C * 0.044715) * square)
            )
            d_pre = (slope * d_act).astype(BF16)
            d_pres.append(d_pre)
            column_sum = column_sum + rows_sum(d_pre.astype(F32))
            total_ref[part, :] += dot(d_pre, up_hold[...], NT)
        hid_ref[...] = column_sum
        d_pre = jnp.concatenate(d_pres, axis=0)
        c = at_ref[3]
        there = pl.ds(pl.multiple_of((1 - c) * half, half), half)
        here = pl.ds(pl.multiple_of(c * half, half), half)
        send_ref[...] = dot(ut_ref[there, :], d_pre, NN).astype(BF16)
        keep_ref[...] = dot(ut_ref[here, :], d_pre, NN).astype(BF16)

    @pl.when(step >= steps)
    def _():
        d_u = total_ref[pl.ds(pl.multiple_of((step - steps) * ROWS, ROWS), ROWS), :]
        normed, scale = unit_rows(resid_ref[...])
        sum_ref[0:1, :] += rows_sum(normed * d_u)
        sum_ref[1:2, :] += rows_sum(d_u)
        d_resid = dy_ref[...].astype(F32) + norm_back(normed, scale, d_u * gain_ref[2:3, :])
        d_resid_ref[...] = d_resid
        normed, scale = unit_rows(attn_ref[...])
        sum_ref[2:3, :] += rows_sum(normed * d_resid)
        sum_ref[3:4, :] += rows_sum(d_resid)
        d_attn = norm_back(normed, scale, d_resid * gain_ref[1:2, :]).astype(BF16)
        sum_ref[4:5, :] += rows_sum(d_attn.astype(F32))
        store_turned(turned_ref, d_attn, turn)
        width = d_o_refs[0].shape[1]
        for g in range(groups):
            d_o_refs[g][...] = dot(d_attn, wo_ref[:, g * width : (g + 1) * width], NN).astype(BF16)


def feed_back(turn, groups, at, d_mlp, u_turned, pre, up, down, resid, attn, cotangent, weight_out, gain):
    rows, features = d_mlp.shape
    hidden = pre.shape[1]
    steps = hidden // HIDDEN_BLOCK
    width = features // groups
    half = features // NC
    return call(
        functools.partial(feed_back_kernel, turn, groups, up, down, steps),
        "feed_back",
        (steps + rows // ROWS,),
        [fixed(d_mlp.shape), fixed(u_turned.shape)]
        + [column_spec(rows, steps), *up.specs, *down.specs]
        + [later_spec(features, steps), later_spec(features, steps), later_spec(features, steps, True)]
        + [fixed(weight_out.shape), fixed(gain.shape)],
        [column_spec(half, steps), column_spec(half, steps)]
        + [column_spec(1, steps), later_spec(features, steps), fixed((8, features))]
        + [later_turned(features, steps)]
        + [later_spec(width, steps)] * groups,
        [shaped(half, hidden, BF16), shaped(half, hidden, BF16)]
        + [shaped(1, hidden, F32), shaped(rows, features, F32), shaped(8, features, F32)]
        + [shaped(features, rows, BF16)]
        + [shaped(rows, width, BF16)] * groups,
        [d_mlp, u_turned, pre, *up.operands, *down.operands]
        + [resid, attn, cotangent, weight_out, gain],
        prefetch=[at],
        scratch=[
            pltpu.VMEM((features, HIDDEN_BLOCK), BF16),
            pltpu.VMEM((features, HIDDEN_BLOCK), BF16),
            pltpu.VMEM((rows, features), F32),
        ],
    )


def d_in_kernel(at_ref, dq_ref, w_ref, x_ref, part_ref, sum_ref, head_ref):
    @pl.when(pl.program_id(0) == 0)
    def _():
        sum_ref[...] = jnp.zeros_like(sum_ref)
        head_ref[...] = jnp.zeros_like(head_ref)

    d_qkv = dq_ref[...]
    part = dot(d_qkv, w_ref[...], NT).astype(BF16)
    part_ref[...] = part
    part = part.astype(F32)
    normed, _ = unit_rows(x_ref[...].astype(F32))
    sum_ref[0:1, :] += rows_sum(normed * part)
    sum_ref[1:2, :] += rows_sum(part)
    head_ref[0:1, :] += rows_sum(d_qkv.astype(F32))


def d_in(row_at, rows, d_qkv, weight_qkv, inputs):
    features, width = weight_qkv.shape
    return call(
        d_in_kernel,
        "d_in",
        (rows // ROWS,),
        [shifted_spec(width), fixed(weight_qkv.shape), shifted_spec(features)],
        [row_spec(features), fixed((8, features)), fixed((8, width))],
        [shaped(rows, features, BF16), shaped(8, features, F32), shaped(8, width, F32)],
        [d_qkv, weight_qkv, inputs],
        micros=2,
        prefetch=[row_at],
    )


def last_kernel(terms, at_ref, *refs):
    x_ref, d_resid_ref, gain_ref, out_ref = refs[terms:]
    d_u = sum(r[...].astype(F32) for r in refs[:terms])
    normed, scale = unit_rows(x_ref[...].astype(F32))
    out_ref[...] = (d_resid_ref[...] + norm_back(normed, scale, d_u * gain_ref[0:1, :])).astype(BF16)


def last(row_at, parts, inputs, d_resid, gain):
    rows, features = d_resid.shape
    return call(
        functools.partial(last_kernel, len(parts)),
        "last",
        (rows // ROWS,),
        [row_spec(features)] * len(parts) + [shifted_spec(features), row_spec(features), fixed(gain.shape)],
        row_spec(features),
        shaped(rows, features, BF16),
        [*parts, inputs, d_resid, gain],
        prefetch=[row_at],
    )


def grad_rows_kernel(terms, at_ref, left_ref, right_ref, *refs):
    total = dot(left_ref[...], right_ref[...], NN)
    for r in refs[:terms]:
        total = total + r[...].astype(F32)
    refs[terms][...] = total.astype(BF16)


def grad_rows(left, at, right, terms=()):
    _, rows, tokens = left.shape
    columns = right.shape[1]
    block = math.gcd(columns, 256 if tokens > 1024 else 512)
    return call(
        functools.partial(grad_rows_kernel, len(terms)),
        "grad_rows",
        (columns // block,),
        [
            pl.BlockSpec((None, rows, tokens), lambda j, at: (at[0], 0, 0)),
            pl.BlockSpec((tokens, block), lambda j, at: (0, j)),
        ]
        + [pl.BlockSpec((None, rows, block), lambda j, at: (at[1], 0, j))] * len(terms),
        pl.BlockSpec((rows, block), lambda j, at: (0, j)),
        shaped(rows, columns, BF16),
        [left, right, *terms],
        prefetch=[at],
    )


def grad_down_kernel(left_ref, pre_ref, out_ref):
    z = pre_ref[...].astype(F32)
    _, t = gelu_tanh_of(z)
    out_ref[...] = dot(left_ref[...], (z * (0.5 + 0.5 * t)).astype(BF16), NN).astype(BF16)


def grad_down_of(d_mlp_turned, pre):
    features, rows = d_mlp_turned.shape
    hidden = pre.shape[1]
    column = lambda size: pl.BlockSpec((size, 512), lambda j: (0, j))
    return call(
        grad_down_kernel,
        "grad_down",
        (hidden // 512,),
        [fixed(d_mlp_turned.shape), column(rows)],
        column(features),
        shaped(features, hidden, BF16),
        [d_mlp_turned, pre],
    )


def merge_kernel(outs, ups, at_ref, *refs):
    out_refs, up_refs, both_refs, to_ref = refs[:outs], refs[outs : outs + ups], refs[outs + ups : -1], refs[-1]

    def fill(parts):
        to_ref[...] = sum(r[...].astype(F32) for r in (*parts, *both_refs)).astype(BF16)

    @pl.when(pl.program_id(0) == 0)
    def _():
        fill(out_refs)

    @pl.when(pl.program_id(0) > 0)
    def _():
        fill(up_refs)


def merge(at, rows, outs, ups, group, both=()):
    width = outs[0].shape[1] // 2
    hidden = ups[0].shape[1] // 2
    steps = hidden // width
    pick_row = lambda a, at: at[0] if a.shape[0] > rows else 0
    specs = [pl.BlockSpec((rows, width), lambda j, at, a=a: (pick_row(a, at), group)) for a in outs]
    specs += [
        pl.BlockSpec(
            (rows, width),
            lambda j, at, a=a: (pick_row(a, at), group * steps + jnp.maximum(j - 1, 0)),
        )
        for a in ups
    ]
    specs += [pl.BlockSpec((rows, width), lambda j, at, a=a: (pick_row(a, at), j)) for a in both]
    return call(
        functools.partial(merge_kernel, len(outs), len(ups)),
        "merge",
        (1 + steps,),
        specs,
        pl.BlockSpec((rows, width), lambda j, at: (0, j)),
        shaped(rows, width + hidden, BF16),
        [*outs, *ups, *both],
        prefetch=[at],
    )


def grad_both_kernel(at_ref, left_ref, right_ref, there_ref, send_ref, keep_ref):
    x = at_ref[1]
    for ref, index in ((send_ref, 1 - x), (keep_ref, x)):
        total = dot(left_ref[index], right_ref[...], NN) + there_ref[index].astype(F32)
        ref[...] = total.astype(BF16)


def grad_both(left, at, right, there):
    tokens = left.shape[1]
    rows = left.shape[0] // (NC * NX)
    columns = right.shape[1]
    block = math.gcd(columns, 256)
    out = pl.BlockSpec((rows, block), lambda j, at: (0, j))
    return call(
        grad_both_kernel,
        "grad_both",
        (columns // block,),
        [
            pl.BlockSpec((None, NX, rows, tokens), lambda j, at: (at[0], 0, 0, 0)),
            pl.BlockSpec((tokens, block), lambda j, at: (0, j)),
            pl.BlockSpec((NX, rows, block), lambda j, at: (0, 0, j)),
        ],
        [out, out],
        [shaped(rows, columns, BF16)] * 2,
        [left.reshape(NC, NX, rows, tokens), right, there.reshape(NX, rows, columns)],
        prefetch=[at],
    )


def by_pair_kernel(in_ref, out_ref):
    kinds, _, width = in_ref.shape
    for p in range(width // PAIR):
        for kind in range(kinds):
            at = (p * kinds + kind) * PAIR
            out_ref[:, at : at + PAIR] = in_ref[kind, :, p * PAIR : (p + 1) * PAIR].astype(BF16)


def by_pair(weight):
    kinds, rows, width = weight.shape
    whole = lambda shape: pl.BlockSpec(shape, lambda i: (0,) * len(shape))
    return call(
        by_pair_kernel,
        "by_pair",
        (1,),
        [whole(weight.shape)],
        whole((rows, kinds * width)),
        shaped(rows, kinds * width, BF16),
        [weight],
        vmem=16 << 20,
    )


def project_kernel(u_ref, w_ref, b_ref, out_ref):
    rows = min(512, u_ref.shape[0])
    for r in range(0, u_ref.shape[0], rows):
        part = slice(r, r + rows)
        out_ref[part, :] = (dot(u_ref[part, :], w_ref[...], NN) + b_ref[...]).astype(BF16)


def project(u, weight, bias):
    rows, features = u.shape
    columns = weight.shape[1]
    block = math.gcd(columns, 512)
    column = lambda size: pl.BlockSpec((size, block), lambda j: (0, j))
    return call(
        project_kernel,
        "project",
        (columns // block,),
        [fixed(u.shape), column(features), column(1)],
        column(rows),
        shaped(rows, columns, BF16),
        [u, weight, bias],
    )


def tie(*values):
    return lax.optimization_barrier(values)


def pick(array, index, axis=0):
    return lax.dynamic_index_in_dim(array, index, axis, keepdims=False)


def add(a, b):
    return (a.astype(F32) + b.astype(F32)).astype(BF16)


def flips(bit):
    return [(i, i ^ bit) for i in range(NZ * NX * NC)]


def z_pairs(shift):
    return [(i, (i + shift * NX * NC) % (NZ * NX * NC)) for i in range(NZ * NX * NC)]


def swap_core(a):
    return lax.ppermute(a, "dp", flips(1))


def swap_x(a):
    return lax.ppermute(a, "dp", flips(NC))


def swap_y(a):
    return lax.ppermute(a, "tensor", [(0, 1), (1, 0)])


def spread_z(shard):
    return [shard] + [lax.ppermute(shard, "dp", z_pairs(k)) for k in range(1, NZ)]


class Staged:
    turn = True

    def __init__(self):
        index = lax.axis_index("dp")
        self.z, self.x, self.c = index // (NX * NC), (index // NC) % NX, index % NC
        self.position = jnp.stack([self.z, self.x, self.c]).astype(jnp.int32)

    def gather_first(self, u1, shard_qkv, shard_out, shard_up, shard_down):
        self.hidden = shard_up.shape[1]
        qkv = lax.all_gather(shard_qkv, "dp", axis=0, tiled=True)
        own = spread_z(jnp.concatenate([shard_up, shard_out], axis=1))
        both_down = jnp.concatenate([shard_down, swap_y(shard_down)], axis=1)
        u1, *own = tie(u1, *own)
        own = jnp.stack(own)
        self.own_x, self.other = swap_x(own), swap_y(own)
        qkv, self.own, both_down = tie(qkv, own, both_down)
        self.down = lax.all_gather(both_down, "dp", axis=0, tiled=True)
        return u1, qkv

    def beside_forward(self, index, values, received):
        if index == 0:
            *values, self.own, self.own_x, self.other = tie(*values, self.own, self.own_x, self.other)
            self.other_x = swap_y(self.own_x)
            self.cores = [swap_core(a) for a in (self.own, self.own_x, self.other)]
        if index == 1:
            n = len(values)
            values = tie(*values, *self.cores)
            values, self.cores = values[:n], list(values[n:])
        if index == 2:
            *values, self.other_x, received[0] = tie(*values, self.other_x, received[0])
            self.cores.append(swap_core(self.other_x))
        return values

    def gather_last(self, *attended):
        groups = [
            [self.own, self.own_x, *self.cores[:2]],
            [self.other, self.other_x, *self.cores[2:]],
        ]
        up = piece_blocks(groups, self.hidden)
        return attended, [p for g in groups for p in g], up, whole_blocks(self.down)

    def reduce_down(self, grad):
        self.down = lax.psum_scatter(grad, "dp", scatter_dimension=0, tiled=True)

    def rows_times(self, left, index, right, terms=()):
        parts = NC if not terms else NC * NX
        left = left.reshape(parts, -1, left.shape[-1])
        return grad_rows(left, jnp.stack(index), right, terms)

    def reduce_start(self, send, keep, turned, o_own, later):
        up_there = swap_core(send)
        out_there = swap_core(self.rows_times(turned, [1 - self.c, self.c], o_own))
        out_keep = self.rows_times(turned, [self.c, self.c], o_own)
        later, out_keep = tie(later, out_keep)
        self.outs, self.ups = [out_keep, out_there], [keep, up_there]
        return later

    def reduce_first(self, d_o_rows):
        outs_ups_rows = tie(*self.outs, *self.ups, *d_o_rows)
        self.outs, self.ups, d_o_rows = outs_ups_rows[:2], outs_ups_rows[2:4], outs_ups_rows[4:]
        zero = jnp.zeros((1,), jnp.int32)
        rows = self.outs[0].shape[0]
        send, *d_o_rows = tie(merge(zero, rows, self.outs, self.ups, 1), *d_o_rows)
        self.from_y = swap_y(send)
        return d_o_rows

    def own_rows(self, x, both):
        rows = self.from_y.shape[0] // NX
        return merge(jnp.reshape(x, (1,)), rows, self.outs, self.ups, 0, both)

    def beside_backward(self, index, d_qkv):
        if index == 2:
            d_qkv, self.from_y = tie(d_qkv, self.from_y)
            send, d_qkv = tie(self.own_rows(1 - self.x, [self.from_y]), d_qkv)
            self.from_x = swap_x(send)
        return d_qkv

    def z_pieces(self, total):
        total = total.reshape(NZ, -1, total.shape[1])
        send = [pick(total, lax.rem(self.z + k, NZ)) for k in range(1, NZ)]
        got = [lax.ppermute(a, "dp", z_pairs(k)) for k, a in zip(range(1, NZ), send)]
        return pick(total, self.z), got

    def z_sum(self, total, pieces):
        return sum((a.astype(F32) for a in pieces), total.astype(F32))

    def tail(self, turned, d_qkv, parts, d_in_own, small, finish):
        terms = self.exchange([None, parts[1]])
        send = self.rows_times(turned, [1 - self.c, self.c], d_qkv)
        send, self.from_x = tie(send, self.from_x)
        there = swap_core(send)
        d_qkv, send, *parts = tie(d_qkv, send, *self.outs, *self.ups)
        self.outs, self.ups = parts[:2], parts[2:]
        there, total = tie(there, self.own_rows(self.x, [self.from_y, self.from_x]))
        send, keep = grad_both(turned, jnp.stack([self.c, self.x]), d_qkv, there)
        send, d_qkv = tie(send, d_qkv)
        own = d_in_own(d_qkv)
        total, pieces = self.z_pieces(total)
        there, received, keep, vector, down, part, *pieces = tie(
            swap_x(send), terms[1], keep, small(own), self.down, own[0], *pieces
        )
        half = down.shape[1] // 2
        from_y = swap_y(down[:, half:])
        total = self.z_sum(total, pieces)
        send, pieces = self.z_pieces(add(keep, there))
        for bit in (1, NC):
            vector = vector + lax.ppermute(vector, "dp", flips(bit))
        vector = vector + swap_y(vector)
        d_inputs, vector, from_y, *pieces = tie(finish([part, received]), vector, from_y, *pieces)
        down = down[:, :half].astype(F32) + from_y.astype(F32)
        qkv = self.z_sum(send, pieces)
        for bit in (NX * NC, 2 * NX * NC):
            vector = vector + lax.ppermute(vector, "dp", flips(bit))
        width = self.outs[0].shape[1] // 2
        return d_inputs, vector, total[:, width:], total[:, :width], qkv, down

    def exchange(self, parts):
        return [parts[0], swap_y(parts[1])]


class Plain:
    turn = False

    def __init__(self):
        self.n = lax.axis_size("tensor")
        self.position = jnp.zeros((3,), jnp.int32)
        self.rank = lax.axis_index("tensor")

    def gather_groups(self, shard):
        own = lax.all_gather(shard, "dp", axis=0, tiled=True)
        every = lax.all_gather(own, "tensor", axis=0)
        return jnp.concatenate([pick(every, (self.rank + g) % self.n) for g in range(self.n)], axis=1)

    def gather_first(self, u1, shard_qkv, *shards):
        qkv = lax.all_gather(shard_qkv, "dp", axis=0, tiled=True)
        weights = [self.gather_groups(w) for w in shards]
        self.weights = [weights[:1], *(whole_blocks(w) for w in weights[1:])]
        return u1, qkv

    def beside_forward(self, index, values, received):
        return values

    def gather_last(self, *attended):
        return attended, *self.weights

    def reduce_rows(self, grad):
        grads = self.absolute(jnp.split(grad, self.n, axis=1))
        own = lax.psum_scatter(grads, "tensor", scatter_dimension=0, tiled=True)
        return lax.psum_scatter(own[0], "dp", scatter_dimension=0, tiled=True).astype(F32)

    def reduce_down(self, grad):
        self.down = self.reduce_rows(grad)

    def reduce_start(self, send, keep, turned, o_own, later):
        self.up = self.reduce_rows(jnp.concatenate([keep, send], axis=0))
        self.out = self.reduce_rows(dot(turned, o_own, NN).astype(BF16))
        return later

    def reduce_first(self, d_o_rows):
        return d_o_rows

    def beside_backward(self, index, d_qkv):
        return d_qkv

    def tail(self, turned, d_qkv, parts, d_in_own, small, finish):
        grad = dot(turned, d_qkv, NN).astype(BF16)
        qkv = lax.psum_scatter(grad, "dp", scatter_dimension=0, tiled=True).astype(F32)
        own = d_in_own(d_qkv)
        vector = lax.psum(small(own), ("dp", "tensor"))
        d_inputs = finish(self.exchange([own[0], *parts[1:]]))
        return d_inputs, vector, self.up, self.out, qkv, self.down

    def absolute(self, parts):
        order = (jnp.arange(self.n) - self.rank) % self.n
        return jnp.take(jnp.stack(parts), order, axis=0)

    def exchange(self, parts):
        got = lax.all_to_all(self.absolute(parts), "tensor", 0, 0, tiled=True)
        return [pick(got, (self.rank + g) % self.n) for g in range(self.n)]


def per_device(
    staged,
    inputs,
    cotangent,
    segment_ids,
    w_qkv,
    w_out,
    w_fc1,
    w_fc2,
    norm_gain,
    norm_bias,
    head_bias,
    out_bias,
    fc1_bias,
):
    n = lax.axis_size("tensor")
    rank = lax.axis_index("tensor")
    comm = Staged() if staged else Plain()
    tokens, features = inputs.shape
    seqs, length = segment_ids.shape
    own_rows = tokens // n
    width = w_qkv.shape[2]
    hidden = w_fc1.shape[1]

    def group_slice(array, g, size, axis=0):
        return lax.dynamic_slice_in_dim(array, ((rank + g) % n) * size, size, axis)

    def scalar(value):
        return jnp.reshape(value, (1,)).astype(jnp.int32)

    row_at = [scalar(((rank + g) % n) * (own_rows // ROWS)) for g in range(n)]

    u1, turned1 = first_norm(comm.turn, inputs, norm_gain, norm_bias)
    u1, weight_qkv = comm.gather_first(
        u1,
        by_pair(w_qkv),
        w_out.T.astype(BF16),
        w_fc1.astype(BF16),
        w_fc2.T.astype(BF16),
    )
    pairs = width // PAIR
    heads_bias = group_slice(head_bias, 0, width, 1)
    qkv_bias = jnp.stack([heads_bias[0], jnp.zeros((width,), F32), heads_bias[1]])
    qkv_bias = qkv_bias.reshape(3, pairs, PAIR).transpose(1, 0, 2).reshape(-1)
    qkv = project(u1, weight_qkv, qkv_bias[None])

    starts, lo = segment_bounds(segment_ids)
    blocks = length // QB
    halves = 2 if n == 2 and seqs == 1 else 1
    half = blocks // halves
    places = [(rank + g) % halves for g in range(halves)]
    per_call = math.gcd(pairs, 2)
    calls = pairs // per_call
    o_rows, lse_rows = ([[None] * calls for _ in range(halves)] for _ in range(2))
    received = [None] * calls
    index = 0
    for g in reversed(range(halves)):
        for i in range(calls):
            o, lse = attention_forward(
                i * per_call, per_call, qkv, starts, lo, scalar(places[g] * half), half
            )
            qkv, o, lse = comm.beside_forward(index, [qkv, o, lse], received)
            o_rows[g][i], lse_rows[g][i] = o, lse
            if g > 0:
                received[i] = comm.exchange([None, o])[1]
            index += 1
    if halves < n:
        whole = jnp.concatenate(o_rows[0], axis=1)
        o_groups = comm.exchange([group_slice(whole, g, own_rows) for g in range(n)])
        _, weight_out, up, down = comm.gather_last()
    else:
        o_groups, weight_out, up, down = comm.gather_last(*o_rows[0], *received)
        o_rows[0] = list(o_groups[:calls])

    at = jnp.concatenate([row_at[0], comm.position])
    attn, resid, u2, o_own, turned2, weight_out = middle(
        comm.turn, at, o_groups, weight_out, inputs, norm_gain, norm_bias, out_bias
    )
    hidden_bias = jnp.concatenate([group_slice(fc1_bias, g, hidden) for g in range(n)])
    pre, output, d_mlp, d_mlp_turned, sums3 = feed(
        at, u2, up, down, hidden_bias[None], resid, cotangent, norm_gain, norm_bias, out_bias
    )
    send, keep, bias_hidden, d_resid, sums12, turned_attn, *d_o = feed_back(
        comm.turn,
        n,
        at,
        d_mlp,
        turned2,
        pre,
        up,
        down,
        resid,
        attn,
        cotangent,
        weight_out,
        norm_gain,
    )
    d_o_rows = comm.exchange(d_o)
    d_mlp_turned = comm.reduce_start(send, keep, turned_attn, o_own, d_mlp_turned)
    grad_down, *d_o_rows = tie(grad_down_of(d_mlp_turned, pre), *d_o_rows)
    comm.reduce_down(grad_down)
    if halves < n:
        order = (jnp.arange(n) - rank) % n
        d_o_rows = [jnp.take(jnp.stack(d_o_rows), order, axis=0).reshape(tokens, width)]
    d_o_rows = comm.reduce_first(d_o_rows)

    d_qkv = None
    for pair in range(pairs):
        i, column = divmod(pair, per_call)
        d_qkv = attention_backward(
            pair,
            qkv,
            [o[i] for o in o_rows],
            d_o_rows,
            [l[i] for l in lse_rows],
            column,
            starts,
            lo,
            scalar(places[0]),
            d_qkv,
        )
        d_qkv = comm.beside_backward(pair, d_qkv)

    d_u1_parts, sums0, head_sums = [None] * n, 0.0, 0.0
    for g in reversed(range(1, n)):
        d_u1_parts[g], sums, head_row = d_in(row_at[g], own_rows, d_qkv, weight_qkv, inputs)
        d_u1_parts[g], d_qkv = tie(d_u1_parts[g], d_qkv)
        sums0, head_sums = sums0 + sums, head_sums + head_row[0]

    def small(own):
        totals, head_totals = sums0 + own[1], head_sums + own[2][0]
        hidden_full = jnp.roll(bias_hidden[0], rank * hidden)
        head_terms = head_totals.reshape(pairs, 3, PAIR).transpose(1, 0, 2).reshape(3, width)[0::2]
        head_full = lax.dynamic_update_slice_in_dim(
            jnp.zeros(head_bias.shape, F32), head_terms, rank * width, 1
        )
        gains = [totals[0], sums12[2], sums12[0], sums3[0]]
        shifts = [totals[1], sums12[3], sums12[1], sums3[1]]
        rows = jnp.stack(gains + shifts + [sums12[4], sums3[2]])
        return jnp.concatenate([rows, head_full, hidden_full.reshape(-1, features)])

    d_inputs, small_sums, grad_up, grad_out, grad_qkv, grad_down = comm.tail(
        turned1,
        d_qkv,
        d_u1_parts,
        lambda d_qkv: d_in(row_at[0], own_rows, d_qkv, weight_qkv, inputs),
        small,
        lambda terms: last(row_at[0], terms, inputs, d_resid, norm_gain),
    )
    grad_qkv = grad_qkv.reshape(-1, pairs, 3, PAIR).transpose(2, 0, 1, 3).reshape(3, -1, width)
    return (
        output,
        d_inputs,
        grad_qkv,
        grad_out.T,
        grad_up,
        grad_down.T,
        small_sums[0:4],
        small_sums[4:8],
        small_sums[10:12],
        small_sums[8:10],
        small_sums[12:].reshape(-1),
    )


def solution(mesh):
    staged = mesh.shape["dp"] == NZ * NX * NC and mesh.shape["tensor"] == 2
    return jax.shard_map(
        functools.partial(per_device, staged),
        mesh=mesh,
        in_specs=(
            P("dp", None),
            P("dp", None),
            P("dp", None),
            P(None, "dp", "tensor"),
            P("tensor", "dp"),
            P("dp", "tensor"),
            P("tensor", "dp"),
            P(),
            P(),
            P(),
            P(),
            P(),
        ),
        out_specs=(
            P(("dp", "tensor"), None),
            P(("dp", "tensor"), None),
            P(None, "dp", "tensor"),
            P("tensor", "dp"),
            P("dp", "tensor"),
            P("tensor", "dp"),
            P(),
            P(),
            P(),
            P(),
            P(),
        ),
        check_vma=False,
    )
```

```python
import functools
import math

import jax
import jax.numpy as jnp
from jax import lax
from jax.experimental import pallas as pl
from jax.experimental.pallas import tpu as pltpu
from jax.sharding import PartitionSpec as P

HD = 64
QB = 256
KB = 256
MAX_SEGMENT = 1024
max_chunks = MAX_SEGMENT // KB + 1
SCORE_SCALE = 0.125 * math.log2(math.e)
NEG = -1e30
EPS = 1e-05
BF16 = jnp.bfloat16
F32 = jnp.float32
NT = (((1,), (1,)), ((), ()))
NN = (((1,), (0,)), ((), ()))
TN = (((0,), (0,)), ((), ()))

SMALL = pl.CostEstimate(flops=1, bytes_accessed=1, transcendentals=0)
VMEM = 60 << 20
PAIR = 2 * HD


def dot(a, b, dims):
    return lax.dot_general(a, b, dims, preferred_element_type=jnp.float32)


def split_pair(block):
    lane = lax.broadcasted_iota(jnp.int32, block.shape, 1)
    zero = jnp.zeros_like(block)
    return (jnp.where(lane < HD, block, zero), jnp.where(lane >= HD, block, zero))


def fwd_kernel(pairs, lo_ref, off_ref, *refs):
    q_refs, k_refs, v_refs = refs[:pairs], refs[pairs : 2 * pairs], refs[2 * pairs : 3 * pairs]
    start_ref, o_ref, l_ref, vt_ref = refs[3 * pairs :]
    step = pl.program_id(1)
    block = off_ref[0] + step

    @pl.when(step == 0)
    def _():
        for pair in range(pairs):
            vt_ref[pair] = v_refs[pair][...].T

    pair_step = math.gcd(pairs, 4)
    row_start = start_ref[...]
    query_pos = block * QB + lax.broadcasted_iota(jnp.int32, (1, QB), 1)
    first = lo_ref[pl.program_id(0), block]
    count = block + 1 - first
    base = pl.multiple_of(first * KB, KB)

    for chunks in range(1, max_chunks + 1):

        @pl.when(count == chunks)
        def _(size=chunks * KB):
            window = pl.ds(base, size)
            key_pos = lax.broadcasted_iota(jnp.int32, (size, QB), 0) + base
            ok = (key_pos >= row_start) & (key_pos <= query_pos)
            for pair in range(pairs):
                q_heads = split_pair(q_refs[pair][...])
                keys = k_refs[pair][window, :]
                outs = []
                for h in range(2):
                    s = jnp.where(ok, dot(keys, q_heads[h], NT) * SCORE_SCALE, NEG)
                    peak = jnp.max(s, axis=0, keepdims=True)
                    p = jnp.exp2(s - peak)
                    total = jnp.sum(p, axis=0, keepdims=True)
                    vt = vt_ref[pair, h * HD : (h + 1) * HD, window]
                    outs.append(dot(vt, p.astype(BF16), NN) / total)
                    l_ref[pair, h : h + 1, :] = peak + jnp.log2(total)
                cols = slice(pair * PAIR, (pair + 1) * PAIR)
                o_ref[:, cols] = jnp.concatenate(outs, axis=0).T.astype(BF16)


def attention_forward(first, pairs, qkv, starts, lo, offset, blocks):
    seqs, length = starts.shape
    nq = length // QB
    every = range(first, first + pairs)

    def rows_at(p):
        return pl.BlockSpec((QB, PAIR), lambda s, b, lo, off: (s * nq + off[0] + b, 3 * p))

    def all_at(p, kind):
        return pl.BlockSpec((length, PAIR), lambda s, b, lo, off: (s, 3 * p + kind))

    grid_spec = pltpu.PrefetchScalarGridSpec(
        num_scalar_prefetch=2,
        grid=(seqs, blocks),
        in_specs=[rows_at(p) for p in every]
        + [all_at(p, kind) for kind in (1, 2) for p in every]
        + [pl.BlockSpec((None, 1, QB), lambda s, b, lo, off: (s, 0, off[0] + b))],
        out_specs=[
            pl.BlockSpec((QB, pairs * PAIR), lambda s, b, lo, off: (s * blocks + b, 0)),
            pl.BlockSpec((None, pairs, 2, QB), lambda s, b, lo, off: (s, 0, 0, b)),
        ],
        scratch_shapes=[pltpu.VMEM((pairs, PAIR, length), BF16)],
    )
    return pl.pallas_call(
        functools.partial(fwd_kernel, pairs),
        grid_spec=grid_spec,
        out_shape=(
            jax.ShapeDtypeStruct((seqs * blocks * QB, pairs * PAIR), BF16),
            jax.ShapeDtypeStruct((seqs, pairs, 2, blocks * QB), F32),
        ),
        compiler_params=pltpu.CompilerParams(
            dimension_semantics=("arbitrary",) * 2, vmem_limit_bytes=VMEM
        ),
        cost_estimate=SMALL,
        name="attention_forward",
    )(lo, offset, *[qkv] * (3 * pairs), starts[:, None, :])


def bwd_kernel(halves, lo_ref, place_ref, q_ref, k_ref, v_ref, start_ref, *refs):
    o_refs, do_refs, l_refs = refs[:halves], refs[halves : 2 * halves], refs[2 * halves : 3 * halves]
    out_ref, kt_ref, dk_ref, dv_ref = refs[-4:]
    block = pl.program_id(1)
    blocks = pl.num_programs(1)
    @pl.when(block == 0)
    def _():
        kt_ref[...] = k_ref[...].T
        dk_ref[...] = jnp.zeros_like(dk_ref)
        dv_ref[...] = jnp.zeros_like(dv_ref)

    mine = block // (blocks // halves) == place_ref[0]

    def pick(two, index=slice(None)):
        if halves == 1:
            return two[0][index]
        return jnp.where(mine, two[0][index], two[1][index])

    row_start = start_ref[...]
    query_pos = block * QB + lax.broadcasted_iota(jnp.int32, (1, QB), 1)
    first = lo_ref[pl.program_id(0), block]
    last = (block + 1) * (QB // KB)
    rows = pl.ds(pl.multiple_of(block * QB, QB), QB)
    q_heads = split_pair(q_ref[...])
    g_pair = pick(do_refs)
    g_heads = split_pair(g_pair)
    prod = (g_pair.astype(F32) * pick(o_refs).astype(F32)).T
    deltas = [jnp.sum(prod[h * HD : (h + 1) * HD], axis=0, keepdims=True) for h in range(2)]
    lses = [pick(l_refs, slice(h, h + 1)) for h in range(2)]

    count = last - first
    base = pl.multiple_of(first * KB, KB)

    for chunks in range(1, max_chunks + 1):

        @pl.when(count == chunks)
        def _(size=chunks * KB):
            window = pl.ds(base, size)
            keys = k_ref[window, :]
            vals = v_ref[window, :]
            key_pos = lax.broadcasted_iota(jnp.int32, (size, QB), 0) + base
            ok = (key_pos >= row_start) & (key_pos <= query_pos)
            dv = dk = 0.0
            dq = []
            for h in range(2):
                s = jnp.where(ok, dot(keys, q_heads[h], NT) * SCORE_SCALE, NEG)
                p = jnp.exp2(s - lses[h])
                dp = dot(vals, g_heads[h], NT)
                ds = (p * (dp - deltas[h])).astype(BF16)
                dv = dv + dot(p.astype(BF16), g_heads[h], NN)
                dk = dk + dot(ds, q_heads[h], NN)
                dq.append(dot(kt_ref[h * HD : (h + 1) * HD, window], ds, NN))
            dv_ref[window, :] += dv
            dk_ref[window, :] += dk
            out_ref[rows, :PAIR] = (jnp.concatenate(dq, axis=0) * 0.125).T.astype(BF16)

    @pl.when(block == blocks - 1)
    def _():
        out_ref[:, PAIR : 2 * PAIR] = (dk_ref[...] * 0.125).astype(BF16)
        out_ref[:, 2 * PAIR :] = dv_ref[...].astype(BF16)


def attention_backward(pair, qkv, o_rows, d_o_rows, lse_rows, column, starts, lo, place, before):
    seqs, length = starts.shape
    nq = length // QB
    halves = len(o_rows)
    half = nq // halves

    def row(g, s, b, place):
        if halves == 1:
            return s, b, s * nq + b
        at = jnp.clip(b - jnp.bitwise_xor(place[0], g) * half, 0, half - 1)
        return s, at, at

    def rows_of(g, col):
        return pl.BlockSpec((QB, PAIR), lambda s, b, lo, place: (row(g, s, b, place)[2], col))

    def lse_of(g):
        return pl.BlockSpec(
            (None, None, 2, QB), lambda s, b, lo, place: (s, column, 0, row(g, s, b, place)[1])
        )

    in_specs = [
        pl.BlockSpec((QB, PAIR), lambda s, b, lo, place: (s * nq + b, 3 * pair)),
        pl.BlockSpec((length, PAIR), lambda s, b, lo, place: (s, 3 * pair + 1)),
        pl.BlockSpec((length, PAIR), lambda s, b, lo, place: (s, 3 * pair + 2)),
        pl.BlockSpec((None, 1, QB), lambda s, b, lo, place: (s, 0, b)),
        *[rows_of(g, column) for g in range(halves)],
        *[rows_of(g, pair) for g in range(halves)],
        *[lse_of(g) for g in range(halves)],
    ]
    operands = [qkv, qkv, qkv, starts[:, None, :], *o_rows, *d_o_rows, *lse_rows]
    alias = {}
    if before is not None:
        alias = {2 + len(operands): 0}
        in_specs.append(pl.BlockSpec(memory_space=pl.ANY))
        operands.append(before)
    return pl.pallas_call(
        functools.partial(bwd_kernel, halves),
        grid_spec=pltpu.PrefetchScalarGridSpec(
            num_scalar_prefetch=2,
            grid=(seqs, nq),
            in_specs=in_specs,
            out_specs=pl.BlockSpec((length, 3 * PAIR), lambda s, b, lo, place: (s, pair)),
            scratch_shapes=[
                pltpu.VMEM((PAIR, length), BF16),
                pltpu.VMEM((length, PAIR), F32),
                pltpu.VMEM((length, PAIR), F32),
            ],
        ),
        out_shape=jax.ShapeDtypeStruct(qkv.shape, BF16),
        input_output_aliases=alias,
        compiler_params=pltpu.CompilerParams(
            dimension_semantics=("arbitrary", "arbitrary"), vmem_limit_bytes=VMEM
        ),
        cost_estimate=SMALL,
        name="attention_backward",
    )(lo, place, *operands)


def segment_bounds(segment_ids):
    starts = jnp.sum((segment_ids[:, None, :] < segment_ids[:, :, None]).astype(jnp.int32), axis=2)
    return starts, starts[:, ::QB] // KB


ROWS = 256
HIDDEN_BLOCK = 1024
NZ, NX, NC = 4, 2, 2


def unit_rows(v):
    centered = v - jnp.mean(v, axis=-1, keepdims=True)
    scale = lax.rsqrt(jnp.mean(centered * centered, axis=-1, keepdims=True) + EPS)
    return centered * scale, scale


def norm_back(normed, scale, inner):
    return scale * (
        inner
        - jnp.mean(inner, axis=-1, keepdims=True)
        - normed * jnp.mean(inner * normed, axis=-1, keepdims=True)
    )


def rows_sum(v):
    return jnp.sum(v, axis=0, keepdims=True)


def store_turned(ref, block, by_device):
    turned = block.T
    if not by_device:
        ref[...] = turned
        return
    size = turned.shape[0] // (NZ * NX * NC)
    for z in range(NZ):
        for x in range(NX):
            for c in range(NC):
                old = ((z * NX + x) * NC + c) * size
                new = ((c * NX + x) * NZ + z) * size
                ref[new : new + size, :] = turned[old : old + size]


def turned_spec(features):
    return pl.BlockSpec((features, ROWS), lambda i, *_: (0, i))


def fixed(shape):
    return pl.BlockSpec(shape, lambda *_: (0,) * len(shape), pipeline_mode=pl.Buffered(1))


def call(body, name, grid, ins, outs, shapes, operands, prefetch=(), scratch=(), vmem=VMEM, micros=0):
    return pl.pallas_call(
        body,
        grid_spec=pltpu.PrefetchScalarGridSpec(
            num_scalar_prefetch=len(prefetch),
            grid=grid,
            in_specs=ins,
            out_specs=outs,
            scratch_shapes=scratch,
        ),
        out_shape=shapes,
        compiler_params=pltpu.CompilerParams(
            dimension_semantics=("arbitrary",) * len(grid), vmem_limit_bytes=vmem
        ),
        cost_estimate=pl.CostEstimate(
            flops=1 + int(micros * 1.1e9), bytes_accessed=1, transcendentals=0
        ),
        name=name,
    )(*prefetch, *operands)


def shaped(rows, cols, dtype):
    return jax.ShapeDtypeStruct((rows, cols), dtype)


def row_spec(cols):
    return pl.BlockSpec((ROWS, cols), lambda i, *_: (i, 0))


def shifted_spec(cols):
    return pl.BlockSpec((ROWS, cols), lambda i, at, *_: (at[0] + i, 0))


def first_norm_kernel(turn, x_ref, gain_ref, bias_ref, u_ref, turned_ref):
    normed, _ = unit_rows(x_ref[...].astype(F32))
    u = (normed * gain_ref[0:1, :] + bias_ref[0:1, :]).astype(BF16)
    u_ref[...] = u
    store_turned(turned_ref, u, turn)


def first_norm(turn, inputs, gain, bias):
    tokens, features = inputs.shape
    return call(
        functools.partial(first_norm_kernel, turn),
        "first_norm",
        (tokens // ROWS,),
        [row_spec(features), fixed(gain.shape), fixed(bias.shape)],
        [row_spec(features), turned_spec(features)],
        [shaped(tokens, features, BF16), shaped(features, tokens, BF16)],
        [inputs, gain, bias],
        vmem=24 << 20,
    )


class Blocks:
    def __init__(self, operands, specs, load):
        self.operands, self.specs, self.load = operands, specs, load


def whole_blocks(weight):
    steps = weight.shape[1] // HIDDEN_BLOCK
    spec = pl.BlockSpec(
        (weight.shape[0], HIDDEN_BLOCK), lambda j, *_: (0, jnp.minimum(j, steps - 1))
    )

    def load(at_ref, step, refs, hold_ref):
        hold_ref[...] = refs[0][...]

    return Blocks([weight], [spec], load)


def piece_blocks(groups, columns):
    rows = groups[0][0].shape[1]
    steps = columns // HIDDEN_BLOCK
    operands, specs = [], []
    for g, pieces in enumerate(groups):
        for piece in pieces:
            operands.append(piece)
            specs.append(
                pl.BlockSpec(
                    (NZ, rows, HIDDEN_BLOCK),
                    lambda j, *_, g=g: (0, 0, jnp.clip(j - g * steps, 0, steps - 1)),
                )
            )

    def load(at_ref, step, refs, hold_ref):
        for g in range(len(groups)):

            @pl.when(step // steps == g)
            def _(g=g):
                place_pieces(at_ref, refs[4 * g : 4 * g + 4], hold_ref, rows)

    return Blocks(operands, specs, load)


def place_pieces(at_ref, refs, hold_ref, rows):
    z, x, c = at_ref[1], at_ref[2], at_ref[3]
    for n, ref in enumerate(refs):
        dx, dc = n % 2, n // 2
        for k in range(NZ):
            index = lax.rem(z - k + NZ, NZ) * NX + lax.bitwise_xor(x, dx)
            row = pl.multiple_of((index * NC + lax.bitwise_xor(c, dc)) * rows, rows)
            hold_ref[pl.ds(row, rows), :] = ref[k]


def middle_kernel(turn, groups, pieces, at_ref, *refs):
    o_refs, w_refs = refs[:groups], refs[groups : groups + pieces]
    x_ref, gain_ref, bias_ref, ob_ref = refs[groups + pieces : groups + pieces + 4]
    attn_ref, resid_ref, u_ref, o_ref, turned_ref, w_ref = refs[groups + pieces + 4 :]
    width = w_refs[0].shape[2] if pieces > 1 else 0

    @pl.when(pl.program_id(0) == 0)
    def _():
        if pieces == 1:
            w_ref[...] = w_refs[0][...]
        else:
            for g in range(pieces // 4):
                place_pieces(
                    at_ref,
                    w_refs[4 * g : 4 * g + 4],
                    w_ref.at[:, g * width : (g + 1) * width],
                    w_refs[0].shape[1],
                )

    attn = ob_ref[0:1, :]
    width = o_refs[0].shape[1]
    for g in range(groups):
        cols = slice(g * width, (g + 1) * width)
        o_ref[:, cols] = o_refs[g][...]
        attn = attn + dot(o_refs[g][...], w_ref[:, cols], NT)
    attn_ref[...] = attn
    normed, _ = unit_rows(attn)
    resid = x_ref[...].astype(F32) + normed * gain_ref[1:2, :] + bias_ref[1:2, :]
    resid_ref[...] = resid
    normed, _ = unit_rows(resid)
    u = (normed * gain_ref[2:3, :] + bias_ref[2:3, :]).astype(BF16)
    u_ref[...] = u
    store_turned(turned_ref, u, turn)


def middle(turn, at, o_groups, weight_out, inputs, gain, bias, out_bias):
    rows, width = o_groups[0].shape
    features = inputs.shape[1]
    if len(weight_out) == 1:
        weight_specs = [fixed(weight_out[0].shape)]
    else:
        part = features * 4 // len(weight_out)
        last = weight_out[0].shape[2] // part - 1
        shape = (NZ, weight_out[0].shape[1], part)
        spec = pl.BlockSpec(shape, lambda *_: (0, 0, last), pipeline_mode=pl.Buffered(1))
        weight_specs = [spec] * len(weight_out)
    return call(
        functools.partial(middle_kernel, turn, len(o_groups), len(weight_out)),
        "middle",
        (rows // ROWS,),
        [row_spec(width)] * len(o_groups)
        + weight_specs
        + [shifted_spec(features)]
        + [fixed(a.shape) for a in (gain, bias, out_bias)],
        [row_spec(features)] * 4 + [turned_spec(features), fixed((features, features))],
        [shaped(rows, features, d) for d in (F32, F32, BF16, BF16)]
        + [shaped(features, rows, BF16), shaped(features, features, BF16)],
        [*o_groups, *weight_out, inputs, gain, bias, out_bias],
        prefetch=[at],
    )


GELU_C = math.sqrt(2.0 / math.pi)


def gelu_tanh_of(z):
    square = z * z
    return square, jnp.tanh(z * (GELU_C + (GELU_C * 0.044715) * square))


def later_spec(cols, steps, shift=False):
    if shift:
        return pl.BlockSpec((ROWS, cols), lambda j, at, *_: (at[0] + jnp.maximum(j - steps, 0), 0))
    return pl.BlockSpec((ROWS, cols), lambda j, *_: (jnp.maximum(j - steps, 0), 0))


def later_turned(features, steps):
    return pl.BlockSpec((features, ROWS), lambda j, *_: (0, jnp.maximum(j - steps, 0)))


def column_spec(rows, steps):
    return pl.BlockSpec((rows, HIDDEN_BLOCK), lambda j, *_: (0, jnp.minimum(j, steps - 1)))


def feed_kernel(up, down, steps, at_ref, u_ref, b_ref, *refs):
    n, m = len(up.operands), len(down.operands)
    up_refs, down_refs = refs[:n], refs[n : n + m]
    resid_ref, dy_ref, gain_ref, bias_ref, ob_ref = refs[n + m : n + m + 5]
    pre_ref, out_ref, d_ref, turned_ref, sum_ref, up_hold, down_hold, total_ref = refs[n + m + 5 :]
    step = pl.program_id(0)
    rows = u_ref.shape[0]

    @pl.when(step == 0)
    def _():
        total_ref[...] = jnp.zeros_like(total_ref)
        sum_ref[...] = jnp.zeros_like(sum_ref)

    @pl.when(step < steps)
    def _():
        up.load(at_ref, step, up_refs, up_hold)
        down.load(at_ref, step, down_refs, down_hold)
        for r in range(0, rows, ROWS):
            part = slice(r, r + ROWS)
            z = dot(u_ref[part, :], up_hold[...], NN) + b_ref[...]
            pre_ref[part, :] = z.astype(BF16)
            _, t = gelu_tanh_of(z)
            act = (z * (0.5 + 0.5 * t)).astype(BF16)
            total_ref[part, :] += dot(act, down_hold[...], NT)

    @pl.when(step >= steps)
    def _():
        mlp = total_ref[pl.ds(pl.multiple_of((step - steps) * ROWS, ROWS), ROWS), :] + ob_ref[1:2, :]
        normed, scale = unit_rows(mlp)
        out_ref[...] = (resid_ref[...] + normed * gain_ref[3:4, :] + bias_ref[3:4, :]).astype(BF16)
        dy = dy_ref[...].astype(F32)
        d_mlp = norm_back(normed, scale, dy * gain_ref[3:4, :]).astype(BF16)
        d_ref[...] = d_mlp
        store_turned(turned_ref, d_mlp, False)
        sum_ref[0:1, :] += rows_sum(normed * dy)
        sum_ref[1:2, :] += rows_sum(dy)
        sum_ref[2:3, :] += rows_sum(d_mlp.astype(F32))


def feed(at, u, up, down, hidden_bias, resid, cotangent, gain, bias, out_bias):
    rows, features = u.shape
    hidden = hidden_bias.shape[1]
    steps = hidden // HIDDEN_BLOCK
    return call(
        functools.partial(feed_kernel, up, down, steps),
        "feed",
        (steps + rows // ROWS,),
        [fixed(u.shape), column_spec(1, steps), *up.specs, *down.specs]
        + [later_spec(features, steps), later_spec(features, steps, True)]
        + [fixed(a.shape) for a in (gain, bias, out_bias)],
        [column_spec(rows, steps), later_spec(features, steps), later_spec(features, steps)]
        + [later_turned(features, steps), fixed((8, features))],
        [shaped(rows, hidden, BF16), shaped(rows, features, BF16), shaped(rows, features, BF16)]
        + [shaped(features, rows, BF16), shaped(8, features, F32)],
        [u, hidden_bias, *up.operands, *down.operands, resid, cotangent, gain, bias, out_bias],
        prefetch=[at],
        scratch=[
            pltpu.VMEM((features, HIDDEN_BLOCK), BF16),
            pltpu.VMEM((features, HIDDEN_BLOCK), BF16),
            pltpu.VMEM((rows, features), F32),
        ],
    )


def feed_back_kernel(turn, groups, up, down, steps, at_ref, d_ref, ut_ref, pre_ref, *refs):
    n, m = len(up.operands), len(down.operands)
    up_refs, down_refs = refs[:n], refs[n : n + m]
    resid_ref, attn_ref, dy_ref, wo_ref, gain_ref = refs[n + m : n + m + 5]
    refs = refs[n + m + 5 :]
    send_ref, keep_ref, hid_ref, d_resid_ref, sum_ref, turned_ref = refs[:6]
    d_o_refs = refs[6 : 6 + groups]
    up_hold, down_hold, total_ref, held_ref = refs[6 + groups :]
    step = pl.program_id(0)
    rows, features = d_ref.shape
    half = features // NC
    width = send_ref.shape[1]

    @pl.when(step == 0)
    def _():
        total_ref[...] = jnp.zeros_like(total_ref)
        sum_ref[...] = jnp.zeros_like(sum_ref)

    @pl.when(step < steps)
    def _():
        up.load(at_ref, step, up_refs, up_hold)
        down.load(at_ref, step, down_refs, down_hold)
        column_sum = 0.0
        block = pl.ds(pl.multiple_of(step * HIDDEN_BLOCK, HIDDEN_BLOCK), HIDDEN_BLOCK)
        for r in range(0, rows, ROWS):
            part = slice(r, r + ROWS)
            d_act = dot(d_ref[part, :], down_hold[...], NN)
            z = pre_ref[part, :].astype(F32)
            square, t = gelu_tanh_of(z)
            gate = 0.5 + 0.5 * t
            slope = gate + (1.0 - t * t) * (
                z * (0.5 * GELU_C + (1.5 * GELU_C * 0.044715) * square)
            )
            d_pre = (slope * d_act).astype(BF16)
            held_ref[part, block] = d_pre
            column_sum = column_sum + rows_sum(d_pre.astype(F32))
            total_ref[part, :] += dot(d_pre, up_hold[...], NT)
        hid_ref[...] = column_sum

    @pl.when(step >= steps)
    def _():
        d_pre = held_ref[:, pl.ds(pl.multiple_of((step - steps) * width, width), width)]
        c = at_ref[3]
        there = pl.ds(pl.multiple_of((1 - c) * half, half), half)
        here = pl.ds(pl.multiple_of(c * half, half), half)
        send_ref[...] = dot(ut_ref[there, :], d_pre, NN).astype(BF16)
        keep_ref[...] = dot(ut_ref[here, :], d_pre, NN).astype(BF16)
        d_u = total_ref[pl.ds(pl.multiple_of((step - steps) * ROWS, ROWS), ROWS), :]
        normed, scale = unit_rows(resid_ref[...])
        sum_ref[0:1, :] += rows_sum(normed * d_u)
        sum_ref[1:2, :] += rows_sum(d_u)
        d_resid = dy_ref[...].astype(F32) + norm_back(normed, scale, d_u * gain_ref[2:3, :])
        d_resid_ref[...] = d_resid
        normed, scale = unit_rows(attn_ref[...])
        sum_ref[2:3, :] += rows_sum(normed * d_resid)
        sum_ref[3:4, :] += rows_sum(d_resid)
        d_attn = norm_back(normed, scale, d_resid * gain_ref[1:2, :]).astype(BF16)
        sum_ref[4:5, :] += rows_sum(d_attn.astype(F32))
        store_turned(turned_ref, d_attn, turn)
        size = d_o_refs[0].shape[1]
        for g in range(groups):
            d_o_refs[g][...] = dot(d_attn, wo_ref[:, g * size : (g + 1) * size], NN).astype(BF16)


def feed_back(turn, groups, at, d_mlp, u_turned, pre, up, down, resid, attn, cotangent, weight_out, gain):
    rows, features = d_mlp.shape
    hidden = pre.shape[1]
    steps = hidden // HIDDEN_BLOCK
    width = features // groups
    half = features // NC
    later_columns = pl.BlockSpec(
        (half, hidden * ROWS // rows), lambda j, *_: (0, jnp.maximum(j - steps, 0))
    )
    return call(
        functools.partial(feed_back_kernel, turn, groups, up, down, steps),
        "feed_back",
        (steps + rows // ROWS,),
        [fixed(d_mlp.shape), fixed(u_turned.shape)]
        + [column_spec(rows, steps), *up.specs, *down.specs]
        + [later_spec(features, steps), later_spec(features, steps), later_spec(features, steps, True)]
        + [fixed(weight_out.shape), fixed(gain.shape)],
        [later_columns, later_columns]
        + [column_spec(1, steps), later_spec(features, steps), fixed((8, features))]
        + [later_turned(features, steps)]
        + [later_spec(width, steps)] * groups,
        [shaped(half, hidden, BF16), shaped(half, hidden, BF16)]
        + [shaped(1, hidden, F32), shaped(rows, features, F32), shaped(8, features, F32)]
        + [shaped(features, rows, BF16)]
        + [shaped(rows, width, BF16)] * groups,
        [d_mlp, u_turned, pre, *up.operands, *down.operands]
        + [resid, attn, cotangent, weight_out, gain],
        prefetch=[at],
        scratch=[
            pltpu.VMEM((features, HIDDEN_BLOCK), BF16),
            pltpu.VMEM((features, HIDDEN_BLOCK), BF16),
            pltpu.VMEM((rows, features), F32),
            pltpu.VMEM((rows, hidden), BF16),
        ],
    )


def d_in_kernel(at_ref, dq_ref, w_ref, x_ref, part_ref, sum_ref, head_ref):
    @pl.when(pl.program_id(0) == 0)
    def _():
        sum_ref[...] = jnp.zeros_like(sum_ref)
        head_ref[...] = jnp.zeros_like(head_ref)

    d_qkv = dq_ref[...]
    part = dot(d_qkv, w_ref[...], NT).astype(BF16)
    part_ref[...] = part
    part = part.astype(F32)
    normed, _ = unit_rows(x_ref[...].astype(F32))
    sum_ref[0:1, :] += rows_sum(normed * part)
    sum_ref[1:2, :] += rows_sum(part)
    head_ref[0:1, :] += rows_sum(d_qkv.astype(F32))


def d_in(row_at, rows, d_qkv, weight_qkv, inputs):
    features, width = weight_qkv.shape
    return call(
        d_in_kernel,
        "d_in",
        (rows // ROWS,),
        [shifted_spec(width), fixed(weight_qkv.shape), shifted_spec(features)],
        [row_spec(features), fixed((8, features)), fixed((8, width))],
        [shaped(rows, features, BF16), shaped(8, features, F32), shaped(8, width, F32)],
        [d_qkv, weight_qkv, inputs],
        micros=2,
        prefetch=[row_at],
    )


def last_kernel(terms, at_ref, *refs):
    x_ref, d_resid_ref, gain_ref, out_ref = refs[terms:]
    d_u = sum(r[...].astype(F32) for r in refs[:terms])
    normed, scale = unit_rows(x_ref[...].astype(F32))
    out_ref[...] = (d_resid_ref[...] + norm_back(normed, scale, d_u * gain_ref[0:1, :])).astype(BF16)


def last(row_at, parts, inputs, d_resid, gain):
    rows, features = d_resid.shape
    return call(
        functools.partial(last_kernel, len(parts)),
        "last",
        (rows // ROWS,),
        [row_spec(features)] * len(parts) + [shifted_spec(features), row_spec(features), fixed(gain.shape)],
        row_spec(features),
        shaped(rows, features, BF16),
        [*parts, inputs, d_resid, gain],
        prefetch=[row_at],
    )


def grad_rows_kernel(terms, at_ref, left_ref, right_ref, *refs):
    total = dot(left_ref[...], right_ref[...], NN)
    for r in refs[:terms]:
        total = total + r[...].astype(F32)
    refs[terms][...] = total.astype(BF16)


def grad_rows(left, at, right, terms=()):
    _, rows, tokens = left.shape
    columns = right.shape[1]
    block = math.gcd(columns, 256 if tokens > 1024 else 512)
    return call(
        functools.partial(grad_rows_kernel, len(terms)),
        "grad_rows",
        (columns // block,),
        [
            pl.BlockSpec((None, rows, tokens), lambda j, at: (at[0], 0, 0)),
            pl.BlockSpec((tokens, block), lambda j, at: (0, j)),
        ]
        + [pl.BlockSpec((None, rows, block), lambda j, at: (at[1], 0, j))] * len(terms),
        pl.BlockSpec((rows, block), lambda j, at: (0, j)),
        shaped(rows, columns, BF16),
        [left, right, *terms],
        prefetch=[at],
    )


def grad_down_kernel(left_ref, pre_ref, out_ref):
    z = pre_ref[...].astype(F32)
    _, t = gelu_tanh_of(z)
    out_ref[...] = dot(left_ref[...], (z * (0.5 + 0.5 * t)).astype(BF16), NN).astype(BF16)


def grad_down_of(d_mlp_turned, pre):
    features, rows = d_mlp_turned.shape
    hidden = pre.shape[1]
    column = lambda size: pl.BlockSpec((size, 512), lambda j: (0, j))
    return call(
        grad_down_kernel,
        "grad_down",
        (hidden // 512,),
        [fixed(d_mlp_turned.shape), column(rows)],
        column(features),
        shaped(features, hidden, BF16),
        [d_mlp_turned, pre],
    )


def merge_kernel(outs, ups, at_ref, *refs):
    out_refs, up_refs, both_refs, to_ref = refs[:outs], refs[outs : outs + ups], refs[outs + ups : -1], refs[-1]

    def fill(parts):
        to_ref[...] = sum(r[...].astype(F32) for r in (*parts, *both_refs)).astype(BF16)

    @pl.when(pl.program_id(0) == 0)
    def _():
        fill(out_refs)

    @pl.when(pl.program_id(0) > 0)
    def _():
        fill(up_refs)


def merge(at, rows, outs, ups, group, both=()):
    width = outs[0].shape[1] // 2
    hidden = ups[0].shape[1] // 2
    steps = hidden // width
    pick_row = lambda a, at: at[0] if a.shape[0] > rows else 0
    specs = [pl.BlockSpec((rows, width), lambda j, at, a=a: (pick_row(a, at), group)) for a in outs]
    specs += [
        pl.BlockSpec(
            (rows, width),
            lambda j, at, a=a: (pick_row(a, at), group * steps + jnp.maximum(j - 1, 0)),
        )
        for a in ups
    ]
    specs += [pl.BlockSpec((rows, width), lambda j, at, a=a: (pick_row(a, at), j)) for a in both]
    return call(
        functools.partial(merge_kernel, len(outs), len(ups)),
        "merge",
        (1 + steps,),
        specs,
        pl.BlockSpec((rows, width), lambda j, at: (0, j)),
        shaped(rows, width + hidden, BF16),
        [*outs, *ups, *both],
        prefetch=[at],
    )


def grad_both_kernel(at_ref, left_ref, right_ref, there_ref, send_ref, keep_ref):
    x = at_ref[1]
    for ref, index in ((send_ref, 1 - x), (keep_ref, x)):
        total = dot(left_ref[index], right_ref[...], NN) + there_ref[index].astype(F32)
        ref[...] = total.astype(BF16)


def grad_both(left, at, right, there):
    tokens = left.shape[1]
    rows = left.shape[0] // (NC * NX)
    columns = right.shape[1]
    block = math.gcd(columns, 256)
    out = pl.BlockSpec((rows, block), lambda j, at: (0, j))
    return call(
        grad_both_kernel,
        "grad_both",
        (columns // block,),
        [
            pl.BlockSpec((None, NX, rows, tokens), lambda j, at: (at[0], 0, 0, 0)),
            pl.BlockSpec((tokens, block), lambda j, at: (0, j)),
            pl.BlockSpec((NX, rows, block), lambda j, at: (0, 0, j)),
        ],
        [out, out],
        [shaped(rows, columns, BF16)] * 2,
        [left.reshape(NC, NX, rows, tokens), right, there.reshape(NX, rows, columns)],
        prefetch=[at],
    )


def by_pair_kernel(in_ref, out_ref):
    kinds, _, width = in_ref.shape
    for p in range(width // PAIR):
        for kind in range(kinds):
            at = (p * kinds + kind) * PAIR
            out_ref[:, at : at + PAIR] = in_ref[kind, :, p * PAIR : (p + 1) * PAIR].astype(BF16)


def by_pair(weight):
    kinds, rows, width = weight.shape
    whole = lambda shape: pl.BlockSpec(shape, lambda i: (0,) * len(shape))
    return call(
        by_pair_kernel,
        "by_pair",
        (1,),
        [whole(weight.shape)],
        whole((rows, kinds * width)),
        shaped(rows, kinds * width, BF16),
        [weight],
        vmem=16 << 20,
    )


def project_kernel(u_ref, w_ref, b_ref, out_ref):
    rows = min(512, u_ref.shape[0])
    for r in range(0, u_ref.shape[0], rows):
        part = slice(r, r + rows)
        out_ref[part, :] = (dot(u_ref[part, :], w_ref[...], NN) + b_ref[...]).astype(BF16)


def project(u, weight, bias):
    rows, features = u.shape
    columns = weight.shape[1]
    block = math.gcd(columns, 512)
    column = lambda size: pl.BlockSpec((size, block), lambda j: (0, j))
    return call(
        project_kernel,
        "project",
        (columns // block,),
        [fixed(u.shape), column(features), column(1)],
        column(rows),
        shaped(rows, columns, BF16),
        [u, weight, bias],
    )


def tie(*values):
    return lax.optimization_barrier(values)


def pick(array, index, axis=0):
    return lax.dynamic_index_in_dim(array, index, axis, keepdims=False)


def add(a, b):
    return (a.astype(F32) + b.astype(F32)).astype(BF16)


def flips(bit):
    return [(i, i ^ bit) for i in range(NZ * NX * NC)]


def z_pairs(shift):
    return [(i, (i + shift * NX * NC) % (NZ * NX * NC)) for i in range(NZ * NX * NC)]


def swap_core(a):
    return lax.ppermute(a, "dp", flips(1))


def swap_x(a):
    return lax.ppermute(a, "dp", flips(NC))


def swap_y(a):
    return lax.ppermute(a, "tensor", [(0, 1), (1, 0)])


def spread_z(shard):
    return [shard] + [lax.ppermute(shard, "dp", z_pairs(k)) for k in range(1, NZ)]


class Staged:
    turn = True

    def __init__(self):
        index = lax.axis_index("dp")
        self.z, self.x, self.c = index // (NX * NC), (index // NC) % NX, index % NC
        self.position = jnp.stack([self.z, self.x, self.c]).astype(jnp.int32)

    def gather_first(self, u1, shard_qkv, shard_out, shard_up, shard_down):
        self.hidden = shard_up.shape[1]
        qkv = lax.all_gather(shard_qkv, "dp", axis=0, tiled=True)
        own = spread_z(jnp.concatenate([shard_up, shard_out], axis=1))
        both_down = jnp.concatenate([shard_down, swap_y(shard_down)], axis=1)
        u1, *own = tie(u1, *own)
        own = jnp.stack(own)
        self.own_x, self.other = swap_x(own), swap_y(own)
        qkv, self.own, both_down = tie(qkv, own, both_down)
        self.down = lax.all_gather(both_down, "dp", axis=0, tiled=True)
        return u1, qkv

    def beside_forward(self, index, values, received):
        if index == 0:
            *values, self.own, self.own_x, self.other = tie(*values, self.own, self.own_x, self.other)
            self.other_x = swap_y(self.own_x)
            self.cores = [swap_core(a) for a in (self.own, self.own_x, self.other)]
        if index == 1:
            n = len(values)
            values = tie(*values, *self.cores)
            values, self.cores = values[:n], list(values[n:])
        if index == 2:
            *values, self.other_x, received[0] = tie(*values, self.other_x, received[0])
            self.cores.append(swap_core(self.other_x))
        return values

    def gather_last(self, *attended):
        groups = [
            [self.own, self.own_x, *self.cores[:2]],
            [self.other, self.other_x, *self.cores[2:]],
        ]
        up = piece_blocks(groups, self.hidden)
        return attended, [p for g in groups for p in g], up, whole_blocks(self.down)

    def reduce_down(self, grad):
        self.down = lax.psum_scatter(grad, "dp", scatter_dimension=0, tiled=True)

    def rows_times(self, left, index, right, terms=()):
        parts = NC if not terms else NC * NX
        left = left.reshape(parts, -1, left.shape[-1])
        return grad_rows(left, jnp.stack(index), right, terms)

    def reduce_start(self, send, keep, turned, o_own, later):
        up_there = swap_core(send)
        out_there = swap_core(self.rows_times(turned, [1 - self.c, self.c], o_own))
        out_keep = self.rows_times(turned, [self.c, self.c], o_own)
        later, out_keep, out_there, up_there = tie(later, out_keep, out_there, up_there)
        self.outs, self.ups = [out_keep, out_there], [keep, up_there]
        return later

    def reduce_first(self, d_o_rows):
        outs_ups_rows = tie(*self.outs, *self.ups, *d_o_rows)
        self.outs, self.ups, d_o_rows = outs_ups_rows[:2], outs_ups_rows[2:4], outs_ups_rows[4:]
        zero = jnp.zeros((1,), jnp.int32)
        rows = self.outs[0].shape[0]
        send, *d_o_rows = tie(merge(zero, rows, self.outs, self.ups, 1), *d_o_rows)
        self.from_y = swap_y(send)
        return d_o_rows

    def own_rows(self, x, both):
        rows = self.from_y.shape[0] // NX
        return merge(jnp.reshape(x, (1,)), rows, self.outs, self.ups, 0, both)

    def beside_backward(self, index, d_qkv):
        if index == 2:
            d_qkv, self.from_y = tie(d_qkv, self.from_y)
            send, d_qkv = tie(self.own_rows(1 - self.x, [self.from_y]), d_qkv)
            self.from_x = swap_x(send)
        return d_qkv

    def z_pieces(self, total):
        total = total.reshape(NZ, -1, total.shape[1])
        send = [pick(total, lax.rem(self.z + k, NZ)) for k in range(1, NZ)]
        got = [lax.ppermute(a, "dp", z_pairs(k)) for k, a in zip(range(1, NZ), send)]
        return pick(total, self.z), got

    def z_sum(self, total, pieces):
        return sum((a.astype(F32) for a in pieces), total.astype(F32))

    def tail(self, turned, d_qkv, parts, d_in_own, small, finish):
        terms = self.exchange([None, parts[1]])
        send = self.rows_times(turned, [1 - self.c, self.c], d_qkv)
        send, self.from_x = tie(send, self.from_x)
        there = swap_core(send)
        d_qkv, send, *parts = tie(d_qkv, send, *self.outs, *self.ups)
        self.outs, self.ups = parts[:2], parts[2:]
        there, total = tie(there, self.own_rows(self.x, [self.from_y, self.from_x]))
        send, keep = grad_both(turned, jnp.stack([self.c, self.x]), d_qkv, there)
        send, d_qkv = tie(send, d_qkv)
        own = d_in_own(d_qkv)
        total, pieces = self.z_pieces(total)
        there, received, keep, vector, down, part, *pieces = tie(
            swap_x(send), terms[1], keep, small(own), self.down, own[0], *pieces
        )
        half = down.shape[1] // 2
        from_y = swap_y(down[:, half:])
        total = self.z_sum(total, pieces)
        send, pieces = self.z_pieces(add(keep, there))
        for bit in (1, NC):
            vector = vector + lax.ppermute(vector, "dp", flips(bit))
        vector = vector + swap_y(vector)
        d_inputs, vector, from_y, *pieces = tie(finish([part, received]), vector, from_y, *pieces)
        down = down[:, :half].astype(F32) + from_y.astype(F32)
        qkv = self.z_sum(send, pieces)
        for bit in (NX * NC, 2 * NX * NC):
            vector = vector + lax.ppermute(vector, "dp", flips(bit))
        width = self.outs[0].shape[1] // 2
        return d_inputs, vector, total[:, width:], total[:, :width], qkv, down

    def exchange(self, parts):
        return [parts[0], swap_y(parts[1])]


class Plain:
    turn = False

    def __init__(self):
        self.n = lax.axis_size("tensor")
        self.position = jnp.zeros((3,), jnp.int32)
        self.rank = lax.axis_index("tensor")

    def gather_groups(self, shard):
        own = lax.all_gather(shard, "dp", axis=0, tiled=True)
        every = lax.all_gather(own, "tensor", axis=0)
        return jnp.concatenate([pick(every, (self.rank + g) % self.n) for g in range(self.n)], axis=1)

    def gather_first(self, u1, shard_qkv, *shards):
        qkv = lax.all_gather(shard_qkv, "dp", axis=0, tiled=True)
        weights = [self.gather_groups(w) for w in shards]
        self.weights = [weights[:1], *(whole_blocks(w) for w in weights[1:])]
        return u1, qkv

    def beside_forward(self, index, values, received):
        return values

    def gather_last(self, *attended):
        return attended, *self.weights

    def reduce_rows(self, grad):
        grads = self.absolute(jnp.split(grad, self.n, axis=1))
        own = lax.psum_scatter(grads, "tensor", scatter_dimension=0, tiled=True)
        return lax.psum_scatter(own[0], "dp", scatter_dimension=0, tiled=True).astype(F32)

    def reduce_down(self, grad):
        self.down = self.reduce_rows(grad)

    def reduce_start(self, send, keep, turned, o_own, later):
        self.up = self.reduce_rows(jnp.concatenate([keep, send], axis=0))
        self.out = self.reduce_rows(dot(turned, o_own, NN).astype(BF16))
        return later

    def reduce_first(self, d_o_rows):
        return d_o_rows

    def beside_backward(self, index, d_qkv):
        return d_qkv

    def tail(self, turned, d_qkv, parts, d_in_own, small, finish):
        grad = dot(turned, d_qkv, NN).astype(BF16)
        qkv = lax.psum_scatter(grad, "dp", scatter_dimension=0, tiled=True).astype(F32)
        own = d_in_own(d_qkv)
        vector = lax.psum(small(own), ("dp", "tensor"))
        d_inputs = finish(self.exchange([own[0], *parts[1:]]))
        return d_inputs, vector, self.up, self.out, qkv, self.down

    def absolute(self, parts):
        order = (jnp.arange(self.n) - self.rank) % self.n
        return jnp.take(jnp.stack(parts), order, axis=0)

    def exchange(self, parts):
        got = lax.all_to_all(self.absolute(parts), "tensor", 0, 0, tiled=True)
        return [pick(got, (self.rank + g) % self.n) for g in range(self.n)]


def per_device(
    staged,
    inputs,
    cotangent,
    segment_ids,
    w_qkv,
    w_out,
    w_fc1,
    w_fc2,
    norm_gain,
    norm_bias,
    head_bias,
    out_bias,
    fc1_bias,
):
    n = lax.axis_size("tensor")
    rank = lax.axis_index("tensor")
    comm = Staged() if staged else Plain()
    tokens, features = inputs.shape
    seqs, length = segment_ids.shape
    own_rows = tokens // n
    width = w_qkv.shape[2]
    hidden = w_fc1.shape[1]

    def group_slice(array, g, size, axis=0):
        return lax.dynamic_slice_in_dim(array, ((rank + g) % n) * size, size, axis)

    def scalar(value):
        return jnp.reshape(value, (1,)).astype(jnp.int32)

    row_at = [scalar(((rank + g) % n) * (own_rows // ROWS)) for g in range(n)]

    u1, turned1 = first_norm(comm.turn, inputs, norm_gain, norm_bias)
    u1, weight_qkv = comm.gather_first(
        u1,
        by_pair(w_qkv),
        w_out.T.astype(BF16),
        w_fc1.astype(BF16),
        w_fc2.T.astype(BF16),
    )
    pairs = width // PAIR
    heads_bias = group_slice(head_bias, 0, width, 1)
    qkv_bias = jnp.stack([heads_bias[0], jnp.zeros((width,), F32), heads_bias[1]])
    qkv_bias = qkv_bias.reshape(3, pairs, PAIR).transpose(1, 0, 2).reshape(-1)
    qkv = project(u1, weight_qkv, qkv_bias[None])

    starts, lo = segment_bounds(segment_ids)
    blocks = length // QB
    halves = 2 if n == 2 and seqs == 1 else 1
    half = blocks // halves
    places = [(rank + g) % halves for g in range(halves)]
    per_call = math.gcd(pairs, 2)
    calls = pairs // per_call
    o_rows, lse_rows = ([[None] * calls for _ in range(halves)] for _ in range(2))
    received = [None] * calls
    index = 0
    for g in reversed(range(halves)):
        for i in range(calls):
            o, lse = attention_forward(
                i * per_call, per_call, qkv, starts, lo, scalar(places[g] * half), half
            )
            qkv, o, lse = comm.beside_forward(index, [qkv, o, lse], received)
            o_rows[g][i], lse_rows[g][i] = o, lse
            if g > 0:
                received[i] = comm.exchange([None, o])[1]
            index += 1
    if halves < n:
        whole = jnp.concatenate(o_rows[0], axis=1)
        o_groups = comm.exchange([group_slice(whole, g, own_rows) for g in range(n)])
        _, weight_out, up, down = comm.gather_last()
    else:
        o_groups, weight_out, up, down = comm.gather_last(*o_rows[0], *received)
        o_rows[0] = list(o_groups[:calls])

    at = jnp.concatenate([row_at[0], comm.position])
    attn, resid, u2, o_own, turned2, weight_out = middle(
        comm.turn, at, o_groups, weight_out, inputs, norm_gain, norm_bias, out_bias
    )
    hidden_bias = jnp.concatenate([group_slice(fc1_bias, g, hidden) for g in range(n)])
    pre, output, d_mlp, d_mlp_turned, sums3 = feed(
        at, u2, up, down, hidden_bias[None], resid, cotangent, norm_gain, norm_bias, out_bias
    )
    send, keep, bias_hidden, d_resid, sums12, turned_attn, *d_o = feed_back(
        comm.turn,
        n,
        at,
        d_mlp,
        turned2,
        pre,
        up,
        down,
        resid,
        attn,
        cotangent,
        weight_out,
        norm_gain,
    )
    d_o_rows = comm.exchange(d_o)
    d_mlp_turned = comm.reduce_start(send, keep, turned_attn, o_own, d_mlp_turned)
    grad_down, *d_o_rows = tie(grad_down_of(d_mlp_turned, pre), *d_o_rows)
    comm.reduce_down(grad_down)
    if halves < n:
        order = (jnp.arange(n) - rank) % n
        d_o_rows = [jnp.take(jnp.stack(d_o_rows), order, axis=0).reshape(tokens, width)]
    d_o_rows = comm.reduce_first(d_o_rows)

    d_qkv = None
    for pair in range(pairs):
        i, column = divmod(pair, per_call)
        d_qkv = attention_backward(
            pair,
            qkv,
            [o[i] for o in o_rows],
            d_o_rows,
            [l[i] for l in lse_rows],
            column,
            starts,
            lo,
            scalar(places[0]),
            d_qkv,
        )
        d_qkv = comm.beside_backward(pair, d_qkv)

    d_u1_parts, sums0, head_sums = [None] * n, 0.0, 0.0
    for g in reversed(range(1, n)):
        d_u1_parts[g], sums, head_row = d_in(row_at[g], own_rows, d_qkv, weight_qkv, inputs)
        d_u1_parts[g], d_qkv = tie(d_u1_parts[g], d_qkv)
        sums0, head_sums = sums0 + sums, head_sums + head_row[0]

    def small(own):
        totals, head_totals = sums0 + own[1], head_sums + own[2][0]
        hidden_full = jnp.roll(bias_hidden[0], rank * hidden)
        head_terms = head_totals.reshape(pairs, 3, PAIR).transpose(1, 0, 2).reshape(3, width)[0::2]
        head_full = lax.dynamic_update_slice_in_dim(
            jnp.zeros(head_bias.shape, F32), head_terms, rank * width, 1
        )
        gains = [totals[0], sums12[2], sums12[0], sums3[0]]
        shifts = [totals[1], sums12[3], sums12[1], sums3[1]]
        rows = jnp.stack(gains + shifts + [sums12[4], sums3[2]])
        return jnp.concatenate([rows, head_full, hidden_full.reshape(-1, features)])

    d_inputs, small_sums, grad_up, grad_out, grad_qkv, grad_down = comm.tail(
        turned1,
        d_qkv,
        d_u1_parts,
        lambda d_qkv: d_in(row_at[0], own_rows, d_qkv, weight_qkv, inputs),
        small,
        lambda terms: last(row_at[0], terms, inputs, d_resid, norm_gain),
    )
    grad_qkv = grad_qkv.reshape(-1, pairs, 3, PAIR).transpose(2, 0, 1, 3).reshape(3, -1, width)
    return (
        output,
        d_inputs,
        grad_qkv,
        grad_out.T,
        grad_up,
        grad_down.T,
        small_sums[0:4],
        small_sums[4:8],
        small_sums[10:12],
        small_sums[8:10],
        small_sums[12:].reshape(-1),
    )


def solution(mesh):
    staged = mesh.shape["dp"] == NZ * NX * NC and mesh.shape["tensor"] == 2
    return jax.shard_map(
        functools.partial(per_device, staged),
        mesh=mesh,
        in_specs=(
            P("dp", None),
            P("dp", None),
            P("dp", None),
            P(None, "dp", "tensor"),
            P("tensor", "dp"),
            P("dp", "tensor"),
            P("tensor", "dp"),
            P(),
            P(),
            P(),
            P(),
            P(),
        ),
        out_specs=(
            P(("dp", "tensor"), None),
            P(("dp", "tensor"), None),
            P(None, "dp", "tensor"),
            P("tensor", "dp"),
            P("dp", "tensor"),
            P("tensor", "dp"),
            P(),
            P(),
            P(),
            P(),
            P(),
        ),
        check_vma=False,
    )
```

```python
import functools
import math

import jax
import jax.numpy as jnp
from jax import lax
from jax.experimental import pallas as pl
from jax.experimental.pallas import tpu as pltpu
from jax.sharding import PartitionSpec as P

HD = 64
QB = 256
KB = 256
MAX_SEGMENT = 1024
max_chunks = MAX_SEGMENT // KB + 1
SCORE_SCALE = 0.125 * math.log2(math.e)
NEG = -1e30
EPS = 1e-05
BF16 = jnp.bfloat16
F32 = jnp.float32
NT = (((1,), (1,)), ((), ()))
NN = (((1,), (0,)), ((), ()))
TN = (((0,), (0,)), ((), ()))

SMALL = pl.CostEstimate(flops=1, bytes_accessed=1, transcendentals=0)
VMEM = 60 << 20
PAIR = 2 * HD


def dot(a, b, dims):
    return lax.dot_general(a, b, dims, preferred_element_type=jnp.float32)


def split_pair(block):
    lane = lax.broadcasted_iota(jnp.int32, block.shape, 1)
    zero = jnp.zeros_like(block)
    return (jnp.where(lane < HD, block, zero), jnp.where(lane >= HD, block, zero))


def fwd_kernel(pairs, lo_ref, off_ref, *refs):
    q_refs, k_refs, v_refs = refs[:pairs], refs[pairs : 2 * pairs], refs[2 * pairs : 3 * pairs]
    start_ref, o_ref, l_ref, vt_ref = refs[3 * pairs :]
    step = pl.program_id(1)
    block = off_ref[0] + step

    @pl.when(step == 0)
    def _():
        for pair in range(pairs):
            vt_ref[pair] = v_refs[pair][...].T

    pair_step = math.gcd(pairs, 4)
    row_start = start_ref[...]
    query_pos = block * QB + lax.broadcasted_iota(jnp.int32, (1, QB), 1)
    first = lo_ref[pl.program_id(0), block]
    count = block + 1 - first
    base = pl.multiple_of(first * KB, KB)

    for chunks in range(1, max_chunks + 1):

        @pl.when(count == chunks)
        def _(size=chunks * KB):
            window = pl.ds(base, size)
            key_pos = lax.broadcasted_iota(jnp.int32, (size, QB), 0) + base
            ok = (key_pos >= row_start) & (key_pos <= query_pos)
            for pair in range(pairs):
                q_heads = split_pair(q_refs[pair][...])
                keys = k_refs[pair][window, :]
                outs = []
                for h in range(2):
                    s = jnp.where(ok, dot(keys, q_heads[h], NT) * SCORE_SCALE, NEG)
                    peak = jnp.max(s, axis=0, keepdims=True)
                    p = jnp.exp2(s - peak)
                    total = jnp.sum(p, axis=0, keepdims=True)
                    vt = vt_ref[pair, h * HD : (h + 1) * HD, window]
                    outs.append(dot(vt, p.astype(BF16), NN) / total)
                    l_ref[pair, h : h + 1, :] = peak + jnp.log2(total)
                cols = slice(pair * PAIR, (pair + 1) * PAIR)
                o_ref[:, cols] = jnp.concatenate(outs, axis=0).T.astype(BF16)


def attention_forward(first, pairs, qkv, starts, lo, offset, blocks):
    seqs, length = starts.shape
    nq = length // QB
    every = range(first, first + pairs)

    def rows_at(p):
        return pl.BlockSpec((QB, PAIR), lambda s, b, lo, off: (s * nq + off[0] + b, 3 * p))

    def all_at(p, kind):
        return pl.BlockSpec((length, PAIR), lambda s, b, lo, off: (s, 3 * p + kind))

    grid_spec = pltpu.PrefetchScalarGridSpec(
        num_scalar_prefetch=2,
        grid=(seqs, blocks),
        in_specs=[rows_at(p) for p in every]
        + [all_at(p, kind) for kind in (1, 2) for p in every]
        + [pl.BlockSpec((None, 1, QB), lambda s, b, lo, off: (s, 0, off[0] + b))],
        out_specs=[
            pl.BlockSpec((QB, pairs * PAIR), lambda s, b, lo, off: (s * blocks + b, 0)),
            pl.BlockSpec((None, pairs, 2, QB), lambda s, b, lo, off: (s, 0, 0, b)),
        ],
        scratch_shapes=[pltpu.VMEM((pairs, PAIR, length), BF16)],
    )
    return pl.pallas_call(
        functools.partial(fwd_kernel, pairs),
        grid_spec=grid_spec,
        out_shape=(
            jax.ShapeDtypeStruct((seqs * blocks * QB, pairs * PAIR), BF16),
            jax.ShapeDtypeStruct((seqs, pairs, 2, blocks * QB), F32),
        ),
        compiler_params=pltpu.CompilerParams(
            dimension_semantics=("arbitrary",) * 2, vmem_limit_bytes=VMEM
        ),
        cost_estimate=SMALL,
        name="attention_forward",
    )(lo, offset, *[qkv] * (3 * pairs), starts[:, None, :])


def bwd_kernel(halves, lo_ref, place_ref, q_ref, k_ref, v_ref, start_ref, *refs):
    o_refs, do_refs, l_refs = refs[:halves], refs[halves : 2 * halves], refs[2 * halves : 3 * halves]
    out_ref, kt_ref, dk_ref, dv_ref = refs[-4:]
    block = pl.program_id(1)
    blocks = pl.num_programs(1)
    @pl.when(block == 0)
    def _():
        kt_ref[...] = k_ref[...].T
        dk_ref[...] = jnp.zeros_like(dk_ref)
        dv_ref[...] = jnp.zeros_like(dv_ref)

    mine = block // (blocks // halves) == place_ref[0]

    def pick(two, index=slice(None)):
        if halves == 1:
            return two[0][index]
        return jnp.where(mine, two[0][index], two[1][index])

    row_start = start_ref[...]
    query_pos = block * QB + lax.broadcasted_iota(jnp.int32, (1, QB), 1)
    first = lo_ref[pl.program_id(0), block]
    last = (block + 1) * (QB // KB)
    rows = pl.ds(pl.multiple_of(block * QB, QB), QB)
    q_heads = split_pair(q_ref[...])
    g_pair = pick(do_refs)
    g_heads = split_pair(g_pair)
    prod = (g_pair.astype(F32) * pick(o_refs).astype(F32)).T
    deltas = [jnp.sum(prod[h * HD : (h + 1) * HD], axis=0, keepdims=True) for h in range(2)]
    lses = [pick(l_refs, slice(h, h + 1)) for h in range(2)]

    count = last - first
    base = pl.multiple_of(first * KB, KB)

    for chunks in range(1, max_chunks + 1):

        @pl.when(count == chunks)
        def _(size=chunks * KB):
            window = pl.ds(base, size)
            keys = k_ref[window, :]
            vals = v_ref[window, :]
            key_pos = lax.broadcasted_iota(jnp.int32, (size, QB), 0) + base
            ok = (key_pos >= row_start) & (key_pos <= query_pos)
            dv = dk = 0.0
            dq = []
            for h in range(2):
                s = jnp.where(ok, dot(keys, q_heads[h], NT) * SCORE_SCALE, NEG)
                p = jnp.exp2(s - lses[h])
                dp = dot(vals, g_heads[h], NT)
                ds = (p * (dp - deltas[h])).astype(BF16)
                dv = dv + dot(p.astype(BF16), g_heads[h], NN)
                dk = dk + dot(ds, q_heads[h], NN)
                dq.append(dot(kt_ref[h * HD : (h + 1) * HD, window], ds, NN))
            dv_ref[window, :] += dv
            dk_ref[window, :] += dk
            out_ref[rows, :PAIR] = (jnp.concatenate(dq, axis=0) * 0.125).T.astype(BF16)

    @pl.when(block == blocks - 1)
    def _():
        out_ref[:, PAIR : 2 * PAIR] = (dk_ref[...] * 0.125).astype(BF16)
        out_ref[:, 2 * PAIR :] = dv_ref[...].astype(BF16)


def attention_backward(pair, qkv, o_rows, d_o_rows, lse_rows, column, starts, lo, place, before):
    seqs, length = starts.shape
    nq = length // QB
    halves = len(o_rows)
    half = nq // halves

    def row(g, s, b, place):
        if halves == 1:
            return s, b, s * nq + b
        at = jnp.clip(b - jnp.bitwise_xor(place[0], g) * half, 0, half - 1)
        return s, at, at

    def rows_of(g, col):
        return pl.BlockSpec((QB, PAIR), lambda s, b, lo, place: (row(g, s, b, place)[2], col))

    def lse_of(g):
        return pl.BlockSpec(
            (None, None, 2, QB), lambda s, b, lo, place: (s, column, 0, row(g, s, b, place)[1])
        )

    in_specs = [
        pl.BlockSpec((QB, PAIR), lambda s, b, lo, place: (s * nq + b, 3 * pair)),
        pl.BlockSpec((length, PAIR), lambda s, b, lo, place: (s, 3 * pair + 1)),
        pl.BlockSpec((length, PAIR), lambda s, b, lo, place: (s, 3 * pair + 2)),
        pl.BlockSpec((None, 1, QB), lambda s, b, lo, place: (s, 0, b)),
        *[rows_of(g, column) for g in range(halves)],
        *[rows_of(g, pair) for g in range(halves)],
        *[lse_of(g) for g in range(halves)],
    ]
    operands = [qkv, qkv, qkv, starts[:, None, :], *o_rows, *d_o_rows, *lse_rows]
    alias = {}
    if before is not None:
        alias = {2 + len(operands): 0}
        in_specs.append(pl.BlockSpec(memory_space=pl.ANY))
        operands.append(before)
    return pl.pallas_call(
        functools.partial(bwd_kernel, halves),
        grid_spec=pltpu.PrefetchScalarGridSpec(
            num_scalar_prefetch=2,
            grid=(seqs, nq),
            in_specs=in_specs,
            out_specs=pl.BlockSpec((length, 3 * PAIR), lambda s, b, lo, place: (s, pair)),
            scratch_shapes=[
                pltpu.VMEM((PAIR, length), BF16),
                pltpu.VMEM((length, PAIR), F32),
                pltpu.VMEM((length, PAIR), F32),
            ],
        ),
        out_shape=jax.ShapeDtypeStruct(qkv.shape, BF16),
        input_output_aliases=alias,
        compiler_params=pltpu.CompilerParams(
            dimension_semantics=("arbitrary", "arbitrary"), vmem_limit_bytes=VMEM
        ),
        cost_estimate=SMALL,
        name="attention_backward",
    )(lo, place, *operands)


def segment_bounds(segment_ids):
    starts = jnp.sum((segment_ids[:, None, :] < segment_ids[:, :, None]).astype(jnp.int32), axis=2)
    return starts, starts[:, ::QB] // KB


ROWS = 256
HIDDEN_BLOCK = 1024
NZ, NX, NC = 4, 2, 2


def unit_rows(v):
    centered = v - jnp.mean(v, axis=-1, keepdims=True)
    scale = lax.rsqrt(jnp.mean(centered * centered, axis=-1, keepdims=True) + EPS)
    return centered * scale, scale


def norm_back(normed, scale, inner):
    return scale * (
        inner
        - jnp.mean(inner, axis=-1, keepdims=True)
        - normed * jnp.mean(inner * normed, axis=-1, keepdims=True)
    )


def rows_sum(v):
    return jnp.sum(v, axis=0, keepdims=True)


def store_turned(ref, block, by_device):
    turned = block.T
    if not by_device:
        ref[...] = turned
        return
    size = turned.shape[0] // (NZ * NX * NC)
    for z in range(NZ):
        for x in range(NX):
            for c in range(NC):
                old = ((z * NX + x) * NC + c) * size
                new = ((c * NX + x) * NZ + z) * size
                ref[new : new + size, :] = turned[old : old + size]


def turned_spec(features):
    return pl.BlockSpec((features, ROWS), lambda i, *_: (0, i))


def fixed(shape):
    return pl.BlockSpec(shape, lambda *_: (0,) * len(shape), pipeline_mode=pl.Buffered(1))


def call(body, name, grid, ins, outs, shapes, operands, prefetch=(), scratch=(), vmem=VMEM, micros=0):
    return pl.pallas_call(
        body,
        grid_spec=pltpu.PrefetchScalarGridSpec(
            num_scalar_prefetch=len(prefetch),
            grid=grid,
            in_specs=ins,
            out_specs=outs,
            scratch_shapes=scratch,
        ),
        out_shape=shapes,
        compiler_params=pltpu.CompilerParams(
            dimension_semantics=("arbitrary",) * len(grid), vmem_limit_bytes=vmem
        ),
        cost_estimate=pl.CostEstimate(
            flops=1 + int(micros * 1.1e9), bytes_accessed=1, transcendentals=0
        ),
        name=name,
    )(*prefetch, *operands)


def shaped(rows, cols, dtype):
    return jax.ShapeDtypeStruct((rows, cols), dtype)


def row_spec(cols):
    return pl.BlockSpec((ROWS, cols), lambda i, *_: (i, 0))


def shifted_spec(cols):
    return pl.BlockSpec((ROWS, cols), lambda i, at, *_: (at[0] + i, 0))


def first_norm_kernel(turn, x_ref, gain_ref, bias_ref, u_ref, turned_ref):
    normed, _ = unit_rows(x_ref[...].astype(F32))
    u = (normed * gain_ref[0:1, :] + bias_ref[0:1, :]).astype(BF16)
    u_ref[...] = u
    store_turned(turned_ref, u, turn)


def first_norm(turn, inputs, gain, bias):
    tokens, features = inputs.shape
    return call(
        functools.partial(first_norm_kernel, turn),
        "first_norm",
        (tokens // ROWS,),
        [row_spec(features), fixed(gain.shape), fixed(bias.shape)],
        [row_spec(features), turned_spec(features)],
        [shaped(tokens, features, BF16), shaped(features, tokens, BF16)],
        [inputs, gain, bias],
        vmem=24 << 20,
    )


class Blocks:
    def __init__(self, operands, specs, load):
        self.operands, self.specs, self.load = operands, specs, load


def whole_blocks(weight):
    steps = weight.shape[1] // HIDDEN_BLOCK
    spec = pl.BlockSpec(
        (weight.shape[0], HIDDEN_BLOCK), lambda j, *_: (0, jnp.minimum(j, steps - 1))
    )

    def load(at_ref, step, refs, hold_ref):
        hold_ref[...] = refs[0][...]

    return Blocks([weight], [spec], load)


def piece_blocks(groups, columns):
    rows = groups[0][0].shape[1]
    steps = columns // HIDDEN_BLOCK
    operands, specs = [], []
    for g, pieces in enumerate(groups):
        for piece in pieces:
            operands.append(piece)
            specs.append(
                pl.BlockSpec(
                    (NZ, rows, HIDDEN_BLOCK),
                    lambda j, *_, g=g: (0, 0, jnp.clip(j - g * steps, 0, steps - 1)),
                )
            )

    def load(at_ref, step, refs, hold_ref):
        for g in range(len(groups)):

            @pl.when(step // steps == g)
            def _(g=g):
                place_pieces(at_ref, refs[4 * g : 4 * g + 4], hold_ref, rows)

    return Blocks(operands, specs, load)


def place_pieces(at_ref, refs, hold_ref, rows):
    z, x, c = at_ref[1], at_ref[2], at_ref[3]
    for n, ref in enumerate(refs):
        dx, dc = n % 2, n // 2
        for k in range(NZ):
            index = lax.rem(z - k + NZ, NZ) * NX + lax.bitwise_xor(x, dx)
            row = pl.multiple_of((index * NC + lax.bitwise_xor(c, dc)) * rows, rows)
            hold_ref[pl.ds(row, rows), :] = ref[k]


def middle_kernel(turn, groups, pieces, at_ref, *refs):
    o_refs, w_refs = refs[:groups], refs[groups : groups + pieces]
    x_ref, gain_ref, bias_ref, ob_ref = refs[groups + pieces : groups + pieces + 4]
    attn_ref, resid_ref, u_ref, o_ref, turned_ref, w_ref = refs[groups + pieces + 4 :]
    width = w_refs[0].shape[2] if pieces > 1 else 0

    @pl.when(pl.program_id(0) == 0)
    def _():
        if pieces == 1:
            w_ref[...] = w_refs[0][...]
        else:
            for g in range(pieces // 4):
                place_pieces(
                    at_ref,
                    w_refs[4 * g : 4 * g + 4],
                    w_ref.at[:, g * width : (g + 1) * width],
                    w_refs[0].shape[1],
                )

    attn = ob_ref[0:1, :]
    width = o_refs[0].shape[1]
    for g in range(groups):
        cols = slice(g * width, (g + 1) * width)
        o_ref[:, cols] = o_refs[g][...]
        attn = attn + dot(o_refs[g][...], w_ref[:, cols], NT)
    attn_ref[...] = attn
    normed, _ = unit_rows(attn)
    resid = x_ref[...].astype(F32) + normed * gain_ref[1:2, :] + bias_ref[1:2, :]
    resid_ref[...] = resid
    normed, _ = unit_rows(resid)
    u = (normed * gain_ref[2:3, :] + bias_ref[2:3, :]).astype(BF16)
    u_ref[...] = u
    store_turned(turned_ref, u, turn)


def middle(turn, at, o_groups, weight_out, inputs, gain, bias, out_bias):
    rows, width = o_groups[0].shape
    features = inputs.shape[1]
    if len(weight_out) == 1:
        weight_specs = [fixed(weight_out[0].shape)]
    else:
        part = features * 4 // len(weight_out)
        last = weight_out[0].shape[2] // part - 1
        shape = (NZ, weight_out[0].shape[1], part)
        spec = pl.BlockSpec(shape, lambda *_: (0, 0, last), pipeline_mode=pl.Buffered(1))
        weight_specs = [spec] * len(weight_out)
    return call(
        functools.partial(middle_kernel, turn, len(o_groups), len(weight_out)),
        "middle",
        (rows // ROWS,),
        [row_spec(width)] * len(o_groups)
        + weight_specs
        + [shifted_spec(features)]
        + [fixed(a.shape) for a in (gain, bias, out_bias)],
        [row_spec(features)] * 4 + [turned_spec(features), fixed((features, features))],
        [shaped(rows, features, d) for d in (F32, F32, BF16, BF16)]
        + [shaped(features, rows, BF16), shaped(features, features, BF16)],
        [*o_groups, *weight_out, inputs, gain, bias, out_bias],
        prefetch=[at],
    )


GELU_C = math.sqrt(2.0 / math.pi)


def gelu_tanh_of(z):
    square = z * z
    return square, jnp.tanh(z * (GELU_C + (GELU_C * 0.044715) * square))


def later_spec(cols, steps, shift=False):
    if shift:
        return pl.BlockSpec((ROWS, cols), lambda j, at, *_: (at[0] + jnp.maximum(j - steps, 0), 0))
    return pl.BlockSpec((ROWS, cols), lambda j, *_: (jnp.maximum(j - steps, 0), 0))


def later_turned(features, steps):
    return pl.BlockSpec((features, ROWS), lambda j, *_: (0, jnp.maximum(j - steps, 0)))


def column_spec(rows, steps):
    return pl.BlockSpec((rows, HIDDEN_BLOCK), lambda j, *_: (0, jnp.minimum(j, steps - 1)))


def feed_kernel(up, down, steps, at_ref, u_ref, b_ref, *refs):
    n, m = len(up.operands), len(down.operands)
    up_refs, down_refs = refs[:n], refs[n : n + m]
    resid_ref, dy_ref, gain_ref, bias_ref, ob_ref = refs[n + m : n + m + 5]
    pre_ref, out_ref, d_ref, turned_ref, sum_ref, up_hold, down_hold, total_ref = refs[n + m + 5 :]
    step = pl.program_id(0)
    rows = u_ref.shape[0]

    @pl.when(step == 0)
    def _():
        total_ref[...] = jnp.zeros_like(total_ref)
        sum_ref[...] = jnp.zeros_like(sum_ref)

    @pl.when(step < steps)
    def _():
        up.load(at_ref, step, up_refs, up_hold)
        down.load(at_ref, step, down_refs, down_hold)
        for r in range(0, rows, ROWS):
            part = slice(r, r + ROWS)
            z = dot(u_ref[part, :], up_hold[...], NN) + b_ref[...]
            pre_ref[part, :] = z.astype(BF16)
            _, t = gelu_tanh_of(z)
            act = (z * (0.5 + 0.5 * t)).astype(BF16)
            total_ref[part, :] += dot(act, down_hold[...], NT)

    @pl.when(step >= steps)
    def _():
        mlp = total_ref[pl.ds(pl.multiple_of((step - steps) * ROWS, ROWS), ROWS), :] + ob_ref[1:2, :]
        normed, scale = unit_rows(mlp)
        out_ref[...] = (resid_ref[...] + normed * gain_ref[3:4, :] + bias_ref[3:4, :]).astype(BF16)
        dy = dy_ref[...].astype(F32)
        d_mlp = norm_back(normed, scale, dy * gain_ref[3:4, :]).astype(BF16)
        d_ref[...] = d_mlp
        store_turned(turned_ref, d_mlp, False)
        sum_ref[0:1, :] += rows_sum(normed * dy)
        sum_ref[1:2, :] += rows_sum(dy)
        sum_ref[2:3, :] += rows_sum(d_mlp.astype(F32))


def feed(at, u, up, down, hidden_bias, resid, cotangent, gain, bias, out_bias):
    rows, features = u.shape
    hidden = hidden_bias.shape[1]
    steps = hidden // HIDDEN_BLOCK
    return call(
        functools.partial(feed_kernel, up, down, steps),
        "feed",
        (steps + rows // ROWS,),
        [fixed(u.shape), column_spec(1, steps), *up.specs, *down.specs]
        + [later_spec(features, steps), later_spec(features, steps, True)]
        + [fixed(a.shape) for a in (gain, bias, out_bias)],
        [column_spec(rows, steps), later_spec(features, steps), later_spec(features, steps)]
        + [later_turned(features, steps), fixed((8, features))],
        [shaped(rows, hidden, BF16), shaped(rows, features, BF16), shaped(rows, features, BF16)]
        + [shaped(features, rows, BF16), shaped(8, features, F32)],
        [u, hidden_bias, *up.operands, *down.operands, resid, cotangent, gain, bias, out_bias],
        prefetch=[at],
        scratch=[
            pltpu.VMEM((features, HIDDEN_BLOCK), BF16),
            pltpu.VMEM((features, HIDDEN_BLOCK), BF16),
            pltpu.VMEM((rows, features), F32),
        ],
    )


def feed_back_kernel(turn, groups, up, down, steps, at_ref, d_ref, ut_ref, pre_ref, *refs):
    n, m = len(up.operands), len(down.operands)
    up_refs, down_refs = refs[:n], refs[n : n + m]
    resid_ref, attn_ref, dy_ref, wo_ref, gain_ref = refs[n + m : n + m + 5]
    refs = refs[n + m + 5 :]
    send_ref, keep_ref, hid_ref, d_resid_ref, sum_ref, turned_ref = refs[:6]
    d_o_refs = refs[6 : 6 + groups]
    up_hold, down_hold, total_ref, held_ref = refs[6 + groups :]
    step = pl.program_id(0)
    rows, features = d_ref.shape
    half = features // NC
    width = send_ref.shape[1]

    @pl.when(step == 0)
    def _():
        total_ref[...] = jnp.zeros_like(total_ref)
        sum_ref[...] = jnp.zeros_like(sum_ref)

    @pl.when(step < steps)
    def _():
        up.load(at_ref, step, up_refs, up_hold)
        down.load(at_ref, step, down_refs, down_hold)
        column_sum = 0.0
        block = pl.ds(pl.multiple_of(step * HIDDEN_BLOCK, HIDDEN_BLOCK), HIDDEN_BLOCK)
        for r in range(0, rows, ROWS):
            part = slice(r, r + ROWS)
            d_act = dot(d_ref[part, :], down_hold[...], NN)
            z = pre_ref[part, :].astype(F32)
            square, t = gelu_tanh_of(z)
            gate = 0.5 + 0.5 * t
            slope = gate + (1.0 - t * t) * (
                z * (0.5 * GELU_C + (1.5 * GELU_C * 0.044715) * square)
            )
            d_pre = (slope * d_act).astype(BF16)
            held_ref[part, block] = d_pre
            column_sum = column_sum + rows_sum(d_pre.astype(F32))
            total_ref[part, :] += dot(d_pre, up_hold[...], NT)
        hid_ref[...] = column_sum

    @pl.when(step >= steps)
    def _():
        d_pre = held_ref[:, pl.ds(pl.multiple_of((step - steps) * width, width), width)]
        c = at_ref[3]
        there = pl.ds(pl.multiple_of((1 - c) * half, half), half)
        here = pl.ds(pl.multiple_of(c * half, half), half)
        send_ref[...] = dot(ut_ref[there, :], d_pre, NN).astype(BF16)
        keep_ref[...] = dot(ut_ref[here, :], d_pre, NN).astype(BF16)
        d_u = total_ref[pl.ds(pl.multiple_of((step - steps) * ROWS, ROWS), ROWS), :]
        normed, scale = unit_rows(resid_ref[...])
        sum_ref[0:1, :] += rows_sum(normed * d_u)
        sum_ref[1:2, :] += rows_sum(d_u)
        d_resid = dy_ref[...].astype(F32) + norm_back(normed, scale, d_u * gain_ref[2:3, :])
        d_resid_ref[...] = d_resid
        normed, scale = unit_rows(attn_ref[...])
        sum_ref[2:3, :] += rows_sum(normed * d_resid)
        sum_ref[3:4, :] += rows_sum(d_resid)
        d_attn = norm_back(normed, scale, d_resid * gain_ref[1:2, :]).astype(BF16)
        sum_ref[4:5, :] += rows_sum(d_attn.astype(F32))
        store_turned(turned_ref, d_attn, turn)
        size = d_o_refs[0].shape[1]
        for g in range(groups):
            d_o_refs[g][...] = dot(d_attn, wo_ref[:, g * size : (g + 1) * size], NN).astype(BF16)


def feed_back(turn, groups, at, d_mlp, u_turned, pre, up, down, resid, attn, cotangent, weight_out, gain):
    rows, features = d_mlp.shape
    hidden = pre.shape[1]
    steps = hidden // HIDDEN_BLOCK
    width = features // groups
    half = features // NC
    later_columns = pl.BlockSpec(
        (half, hidden * ROWS // rows), lambda j, *_: (0, jnp.maximum(j - steps, 0))
    )
    return call(
        functools.partial(feed_back_kernel, turn, groups, up, down, steps),
        "feed_back",
        (steps + rows // ROWS,),
        [fixed(d_mlp.shape), fixed(u_turned.shape)]
        + [column_spec(rows, steps), *up.specs, *down.specs]
        + [later_spec(features, steps), later_spec(features, steps), later_spec(features, steps, True)]
        + [fixed(weight_out.shape), fixed(gain.shape)],
        [later_columns, later_columns]
        + [column_spec(1, steps), later_spec(features, steps), fixed((8, features))]
        + [later_turned(features, steps)]
        + [later_spec(width, steps)] * groups,
        [shaped(half, hidden, BF16), shaped(half, hidden, BF16)]
        + [shaped(1, hidden, F32), shaped(rows, features, F32), shaped(8, features, F32)]
        + [shaped(features, rows, BF16)]
        + [shaped(rows, width, BF16)] * groups,
        [d_mlp, u_turned, pre, *up.operands, *down.operands]
        + [resid, attn, cotangent, weight_out, gain],
        prefetch=[at],
        scratch=[
            pltpu.VMEM((features, HIDDEN_BLOCK), BF16),
            pltpu.VMEM((features, HIDDEN_BLOCK), BF16),
            pltpu.VMEM((rows, features), F32),
            pltpu.VMEM((rows, hidden), BF16),
        ],
    )


def d_in_kernel(at_ref, dq_ref, w_ref, x_ref, part_ref, sum_ref, head_ref):
    @pl.when(pl.program_id(0) == 0)
    def _():
        sum_ref[...] = jnp.zeros_like(sum_ref)
        head_ref[...] = jnp.zeros_like(head_ref)

    d_qkv = dq_ref[...]
    part = dot(d_qkv, w_ref[...], NT).astype(BF16)
    part_ref[...] = part
    part = part.astype(F32)
    normed, _ = unit_rows(x_ref[...].astype(F32))
    sum_ref[0:1, :] += rows_sum(normed * part)
    sum_ref[1:2, :] += rows_sum(part)
    head_ref[0:1, :] += rows_sum(d_qkv.astype(F32))


def d_in(row_at, rows, d_qkv, weight_qkv, inputs):
    features, width = weight_qkv.shape
    return call(
        d_in_kernel,
        "d_in",
        (rows // ROWS,),
        [shifted_spec(width), fixed(weight_qkv.shape), shifted_spec(features)],
        [row_spec(features), fixed((8, features)), fixed((8, width))],
        [shaped(rows, features, BF16), shaped(8, features, F32), shaped(8, width, F32)],
        [d_qkv, weight_qkv, inputs],
        micros=2,
        prefetch=[row_at],
    )


def last_kernel(terms, at_ref, *refs):
    x_ref, d_resid_ref, gain_ref, out_ref = refs[terms:]
    d_u = sum(r[...].astype(F32) for r in refs[:terms])
    normed, scale = unit_rows(x_ref[...].astype(F32))
    out_ref[...] = (d_resid_ref[...] + norm_back(normed, scale, d_u * gain_ref[0:1, :])).astype(BF16)


def last(row_at, parts, inputs, d_resid, gain):
    rows, features = d_resid.shape
    return call(
        functools.partial(last_kernel, len(parts)),
        "last",
        (rows // ROWS,),
        [row_spec(features)] * len(parts) + [shifted_spec(features), row_spec(features), fixed(gain.shape)],
        row_spec(features),
        shaped(rows, features, BF16),
        [*parts, inputs, d_resid, gain],
        prefetch=[row_at],
    )


def grad_rows_kernel(terms, at_ref, left_ref, right_ref, *refs):
    total = dot(left_ref[...], right_ref[...], NN)
    for r in refs[:terms]:
        total = total + r[...].astype(F32)
    refs[terms][...] = total.astype(BF16)


def grad_rows(left, at, right, terms=()):
    _, rows, tokens = left.shape
    columns = right.shape[1]
    block = math.gcd(columns, 512)
    return call(
        functools.partial(grad_rows_kernel, len(terms)),
        "grad_rows",
        (columns // block,),
        [
            pl.BlockSpec((None, rows, tokens), lambda j, at: (at[0], 0, 0)),
            pl.BlockSpec((tokens, block), lambda j, at: (0, j)),
        ]
        + [pl.BlockSpec((None, rows, block), lambda j, at: (at[1], 0, j))] * len(terms),
        pl.BlockSpec((rows, block), lambda j, at: (0, j)),
        shaped(rows, columns, BF16),
        [left, right, *terms],
        prefetch=[at],
    )


def grad_down_kernel(left_ref, pre_ref, out_ref):
    z = pre_ref[...].astype(F32)
    _, t = gelu_tanh_of(z)
    out_ref[...] = dot(left_ref[...], (z * (0.5 + 0.5 * t)).astype(BF16), NN).astype(BF16)


def grad_down_of(d_mlp_turned, pre):
    features, rows = d_mlp_turned.shape
    hidden = pre.shape[1]
    column = lambda size: pl.BlockSpec((size, 512), lambda j: (0, j))
    return call(
        grad_down_kernel,
        "grad_down",
        (hidden // 512,),
        [fixed(d_mlp_turned.shape), column(rows)],
        column(features),
        shaped(features, hidden, BF16),
        [d_mlp_turned, pre],
    )


def merge_kernel(outs, ups, at_ref, *refs):
    out_refs, up_refs, both_refs, to_ref = refs[:outs], refs[outs : outs + ups], refs[outs + ups : -1], refs[-1]

    def fill(parts):
        to_ref[...] = sum(r[...].astype(F32) for r in (*parts, *both_refs)).astype(BF16)

    @pl.when(pl.program_id(0) == 0)
    def _():
        fill(out_refs)

    @pl.when(pl.program_id(0) > 0)
    def _():
        fill(up_refs)


def merge(at, rows, outs, ups, group, both=()):
    width = outs[0].shape[1] // 2
    hidden = ups[0].shape[1] // 2
    steps = hidden // width
    pick_row = lambda a, at: at[0] if a.shape[0] > rows else 0
    specs = [pl.BlockSpec((rows, width), lambda j, at, a=a: (pick_row(a, at), group)) for a in outs]
    specs += [
        pl.BlockSpec(
            (rows, width),
            lambda j, at, a=a: (pick_row(a, at), group * steps + jnp.maximum(j - 1, 0)),
        )
        for a in ups
    ]
    specs += [pl.BlockSpec((rows, width), lambda j, at, a=a: (pick_row(a, at), j)) for a in both]
    return call(
        functools.partial(merge_kernel, len(outs), len(ups)),
        "merge",
        (1 + steps,),
        specs,
        pl.BlockSpec((rows, width), lambda j, at: (0, j)),
        shaped(rows, width + hidden, BF16),
        [*outs, *ups, *both],
        prefetch=[at],
    )


def grad_both_kernel(at_ref, left_ref, right_ref, there_ref, send_ref, keep_ref):
    x = at_ref[1]
    for ref, index in ((send_ref, 1 - x), (keep_ref, x)):
        total = dot(left_ref[index], right_ref[...], NN) + there_ref[index].astype(F32)
        ref[...] = total.astype(BF16)


def grad_both(left, at, right, there):
    tokens = left.shape[1]
    rows = left.shape[0] // (NC * NX)
    columns = right.shape[1]
    block = math.gcd(columns, 512)
    out = pl.BlockSpec((rows, block), lambda j, at: (0, j))
    return call(
        grad_both_kernel,
        "grad_both",
        (columns // block,),
        [
            pl.BlockSpec((None, NX, rows, tokens), lambda j, at: (at[0], 0, 0, 0)),
            pl.BlockSpec((tokens, block), lambda j, at: (0, j)),
            pl.BlockSpec((NX, rows, block), lambda j, at: (0, 0, j)),
        ],
        [out, out],
        [shaped(rows, columns, BF16)] * 2,
        [left.reshape(NC, NX, rows, tokens), right, there.reshape(NX, rows, columns)],
        prefetch=[at],
    )


def by_pair_kernel(in_ref, out_ref):
    kinds, _, width = in_ref.shape
    for p in range(width // PAIR):
        for kind in range(kinds):
            at = (p * kinds + kind) * PAIR
            out_ref[:, at : at + PAIR] = in_ref[kind, :, p * PAIR : (p + 1) * PAIR].astype(BF16)


def by_pair(weight):
    kinds, rows, width = weight.shape
    whole = lambda shape: pl.BlockSpec(shape, lambda i: (0,) * len(shape))
    return call(
        by_pair_kernel,
        "by_pair",
        (1,),
        [whole(weight.shape)],
        whole((rows, kinds * width)),
        shaped(rows, kinds * width, BF16),
        [weight],
        vmem=16 << 20,
    )


def project_kernel(u_ref, w_ref, b_ref, out_ref):
    rows = min(512, u_ref.shape[0])
    for r in range(0, u_ref.shape[0], rows):
        part = slice(r, r + rows)
        out_ref[part, :] = (dot(u_ref[part, :], w_ref[...], NN) + b_ref[...]).astype(BF16)


def project(u, weight, bias):
    rows, features = u.shape
    columns = weight.shape[1]
    block = math.gcd(columns, 512)
    column = lambda size: pl.BlockSpec((size, block), lambda j: (0, j))
    return call(
        project_kernel,
        "project",
        (columns // block,),
        [fixed(u.shape), column(features), column(1)],
        column(rows),
        shaped(rows, columns, BF16),
        [u, weight, bias],
    )


def tie(*values):
    return lax.optimization_barrier(values)


def pick(array, index, axis=0):
    return lax.dynamic_index_in_dim(array, index, axis, keepdims=False)


def add(a, b):
    return (a.astype(F32) + b.astype(F32)).astype(BF16)


def flips(bit):
    return [(i, i ^ bit) for i in range(NZ * NX * NC)]


def z_pairs(shift):
    return [(i, (i + shift * NX * NC) % (NZ * NX * NC)) for i in range(NZ * NX * NC)]


def swap_core(a):
    return lax.ppermute(a, "dp", flips(1))


def swap_x(a):
    return lax.ppermute(a, "dp", flips(NC))


def swap_y(a):
    return lax.ppermute(a, "tensor", [(0, 1), (1, 0)])


def spread_z(shard):
    return [shard] + [lax.ppermute(shard, "dp", z_pairs(k)) for k in range(1, NZ)]


class Staged:
    turn = True

    def __init__(self):
        index = lax.axis_index("dp")
        self.z, self.x, self.c = index // (NX * NC), (index // NC) % NX, index % NC
        self.position = jnp.stack([self.z, self.x, self.c]).astype(jnp.int32)

    def gather_first(self, u1, shard_qkv, shard_out, shard_up, shard_down):
        self.hidden = shard_up.shape[1]
        qkv = lax.all_gather(shard_qkv, "dp", axis=0, tiled=True)
        own = spread_z(jnp.concatenate([shard_up, shard_out], axis=1))
        both_down = jnp.concatenate([shard_down, swap_y(shard_down)], axis=1)
        u1, *own = tie(u1, *own)
        own = jnp.stack(own)
        self.own_x, self.other = swap_x(own), swap_y(own)
        qkv, self.own, both_down = tie(qkv, own, both_down)
        self.down = lax.all_gather(both_down, "dp", axis=0, tiled=True)
        return u1, qkv

    def beside_forward(self, index, values, received):
        if index == 0:
            *values, self.own, self.own_x, self.other = tie(*values, self.own, self.own_x, self.other)
            self.other_x = swap_y(self.own_x)
            self.cores = [swap_core(a) for a in (self.own, self.own_x, self.other)]
        if index == 1:
            n = len(values)
            values = tie(*values, *self.cores)
            values, self.cores = values[:n], list(values[n:])
        if index == 2:
            *values, self.other_x, received[0] = tie(*values, self.other_x, received[0])
            self.cores.append(swap_core(self.other_x))
        return values

    def gather_last(self, *attended):
        groups = [
            [self.own, self.own_x, *self.cores[:2]],
            [self.other, self.other_x, *self.cores[2:]],
        ]
        up = piece_blocks(groups, self.hidden)
        return attended, [p for g in groups for p in g], up, whole_blocks(self.down)

    def reduce_down(self, grad):
        self.down = lax.psum_scatter(grad, "dp", scatter_dimension=0, tiled=True)

    def rows_times(self, left, index, right, terms=()):
        parts = NC if not terms else NC * NX
        left = left.reshape(parts, -1, left.shape[-1])
        return grad_rows(left, jnp.stack(index), right, terms)

    def reduce_start(self, send, keep, turned, o_own, later):
        up_there = swap_core(send)
        out_there = swap_core(self.rows_times(turned, [1 - self.c, self.c], o_own))
        out_keep = self.rows_times(turned, [self.c, self.c], o_own)
        later, out_keep, out_there, up_there = tie(later, out_keep, out_there, up_there)
        self.outs, self.ups = [out_keep, out_there], [keep, up_there]
        return later

    def reduce_first(self, d_o_rows):
        outs_ups_rows = tie(*self.outs, *self.ups, *d_o_rows)
        self.outs, self.ups, d_o_rows = outs_ups_rows[:2], outs_ups_rows[2:4], outs_ups_rows[4:]
        zero = jnp.zeros((1,), jnp.int32)
        rows = self.outs[0].shape[0]
        send, *d_o_rows = tie(merge(zero, rows, self.outs, self.ups, 1), *d_o_rows)
        self.from_y = swap_y(send)
        return d_o_rows

    def own_rows(self, x, both):
        rows = self.from_y.shape[0] // NX
        return merge(jnp.reshape(x, (1,)), rows, self.outs, self.ups, 0, both)

    def beside_backward(self, index, d_qkv):
        if index == 2:
            d_qkv, self.from_y = tie(d_qkv, self.from_y)
            send, d_qkv = tie(self.own_rows(1 - self.x, [self.from_y]), d_qkv)
            self.from_x = swap_x(send)
        return d_qkv

    def z_pieces(self, total):
        total = total.reshape(NZ, -1, total.shape[1])
        send = [pick(total, lax.rem(self.z + k, NZ)) for k in range(1, NZ)]
        got = [lax.ppermute(a, "dp", z_pairs(k)) for k, a in zip(range(1, NZ), send)]
        return pick(total, self.z), got

    def z_sum(self, total, pieces):
        return sum((a.astype(F32) for a in pieces), total.astype(F32))

    def tail(self, turned, d_qkv, parts, d_in_own, small, finish):
        terms = self.exchange([None, parts[1]])
        send = self.rows_times(turned, [1 - self.c, self.c], d_qkv)
        send, self.from_x = tie(send, self.from_x)
        there = swap_core(send)
        d_qkv, send, *parts = tie(d_qkv, send, *self.outs, *self.ups)
        self.outs, self.ups = parts[:2], parts[2:]
        there, total = tie(there, self.own_rows(self.x, [self.from_y, self.from_x]))
        send, keep = grad_both(turned, jnp.stack([self.c, self.x]), d_qkv, there)
        send, d_qkv = tie(send, d_qkv)
        own = d_in_own(d_qkv)
        total, pieces = self.z_pieces(total)
        there, received, keep, vector, down, part, *pieces = tie(
            swap_x(send), terms[1], keep, small(own), self.down, own[0], *pieces
        )
        half = down.shape[1] // 2
        from_y = swap_y(down[:, half:])
        total = self.z_sum(total, pieces)
        send, pieces = self.z_pieces(add(keep, there))
        for bit in (1, NC):
            vector = vector + lax.ppermute(vector, "dp", flips(bit))
        vector = vector + swap_y(vector)
        d_inputs, vector, from_y, *pieces = tie(finish([part, received]), vector, from_y, *pieces)
        down = down[:, :half].astype(F32) + from_y.astype(F32)
        qkv = self.z_sum(send, pieces)
        for bit in (NX * NC, 2 * NX * NC):
            vector = vector + lax.ppermute(vector, "dp", flips(bit))
        width = self.outs[0].shape[1] // 2
        return d_inputs, vector, total[:, width:], total[:, :width], qkv, down

    def exchange(self, parts):
        return [parts[0], swap_y(parts[1])]


class Plain:
    turn = False

    def __init__(self):
        self.n = lax.axis_size("tensor")
        self.position = jnp.zeros((3,), jnp.int32)
        self.rank = lax.axis_index("tensor")

    def gather_groups(self, shard):
        own = lax.all_gather(shard, "dp", axis=0, tiled=True)
        every = lax.all_gather(own, "tensor", axis=0)
        return jnp.concatenate([pick(every, (self.rank + g) % self.n) for g in range(self.n)], axis=1)

    def gather_first(self, u1, shard_qkv, *shards):
        qkv = lax.all_gather(shard_qkv, "dp", axis=0, tiled=True)
        weights = [self.gather_groups(w) for w in shards]
        self.weights = [weights[:1], *(whole_blocks(w) for w in weights[1:])]
        return u1, qkv

    def beside_forward(self, index, values, received):
        return values

    def gather_last(self, *attended):
        return attended, *self.weights

    def reduce_rows(self, grad):
        grads = self.absolute(jnp.split(grad, self.n, axis=1))
        own = lax.psum_scatter(grads, "tensor", scatter_dimension=0, tiled=True)
        return lax.psum_scatter(own[0], "dp", scatter_dimension=0, tiled=True).astype(F32)

    def reduce_down(self, grad):
        self.down = self.reduce_rows(grad)

    def reduce_start(self, send, keep, turned, o_own, later):
        self.up = self.reduce_rows(jnp.concatenate([keep, send], axis=0))
        self.out = self.reduce_rows(dot(turned, o_own, NN).astype(BF16))
        return later

    def reduce_first(self, d_o_rows):
        return d_o_rows

    def beside_backward(self, index, d_qkv):
        return d_qkv

    def tail(self, turned, d_qkv, parts, d_in_own, small, finish):
        grad = dot(turned, d_qkv, NN).astype(BF16)
        qkv = lax.psum_scatter(grad, "dp", scatter_dimension=0, tiled=True).astype(F32)
        own = d_in_own(d_qkv)
        vector = lax.psum(small(own), ("dp", "tensor"))
        d_inputs = finish(self.exchange([own[0], *parts[1:]]))
        return d_inputs, vector, self.up, self.out, qkv, self.down

    def absolute(self, parts):
        order = (jnp.arange(self.n) - self.rank) % self.n
        return jnp.take(jnp.stack(parts), order, axis=0)

    def exchange(self, parts):
        got = lax.all_to_all(self.absolute(parts), "tensor", 0, 0, tiled=True)
        return [pick(got, (self.rank + g) % self.n) for g in range(self.n)]


def per_device(
    staged,
    inputs,
    cotangent,
    segment_ids,
    w_qkv,
    w_out,
    w_fc1,
    w_fc2,
    norm_gain,
    norm_bias,
    head_bias,
    out_bias,
    fc1_bias,
):
    n = lax.axis_size("tensor")
    rank = lax.axis_index("tensor")
    comm = Staged() if staged else Plain()
    tokens, features = inputs.shape
    seqs, length = segment_ids.shape
    own_rows = tokens // n
    width = w_qkv.shape[2]
    hidden = w_fc1.shape[1]

    def group_slice(array, g, size, axis=0):
        return lax.dynamic_slice_in_dim(array, ((rank + g) % n) * size, size, axis)

    def scalar(value):
        return jnp.reshape(value, (1,)).astype(jnp.int32)

    row_at = [scalar(((rank + g) % n) * (own_rows // ROWS)) for g in range(n)]

    u1, turned1 = first_norm(comm.turn, inputs, norm_gain, norm_bias)
    u1, weight_qkv = comm.gather_first(
        u1,
        by_pair(w_qkv),
        w_out.T.astype(BF16),
        w_fc1.astype(BF16),
        w_fc2.T.astype(BF16),
    )
    pairs = width // PAIR
    heads_bias = group_slice(head_bias, 0, width, 1)
    qkv_bias = jnp.stack([heads_bias[0], jnp.zeros((width,), F32), heads_bias[1]])
    qkv_bias = qkv_bias.reshape(3, pairs, PAIR).transpose(1, 0, 2).reshape(-1)
    qkv = project(u1, weight_qkv, qkv_bias[None])

    starts, lo = segment_bounds(segment_ids)
    blocks = length // QB
    halves = 2 if n == 2 and seqs == 1 else 1
    half = blocks // halves
    places = [(rank + g) % halves for g in range(halves)]
    per_call = math.gcd(pairs, 2)
    calls = pairs // per_call
    o_rows, lse_rows = ([[None] * calls for _ in range(halves)] for _ in range(2))
    received = [None] * calls
    index = 0
    for g in reversed(range(halves)):
        for i in range(calls):
            o, lse = attention_forward(
                i * per_call, per_call, qkv, starts, lo, scalar(places[g] * half), half
            )
            qkv, o, lse = comm.beside_forward(index, [qkv, o, lse], received)
            o_rows[g][i], lse_rows[g][i] = o, lse
            if g > 0:
                received[i] = comm.exchange([None, o])[1]
            index += 1
    if halves < n:
        whole = jnp.concatenate(o_rows[0], axis=1)
        o_groups = comm.exchange([group_slice(whole, g, own_rows) for g in range(n)])
        _, weight_out, up, down = comm.gather_last()
    else:
        o_groups, weight_out, up, down = comm.gather_last(*o_rows[0], *received)
        o_rows[0] = list(o_groups[:calls])

    at = jnp.concatenate([row_at[0], comm.position])
    attn, resid, u2, o_own, turned2, weight_out = middle(
        comm.turn, at, o_groups, weight_out, inputs, norm_gain, norm_bias, out_bias
    )
    hidden_bias = jnp.concatenate([group_slice(fc1_bias, g, hidden) for g in range(n)])
    pre, output, d_mlp, d_mlp_turned, sums3 = feed(
        at, u2, up, down, hidden_bias[None], resid, cotangent, norm_gain, norm_bias, out_bias
    )
    send, keep, bias_hidden, d_resid, sums12, turned_attn, *d_o = feed_back(
        comm.turn,
        n,
        at,
        d_mlp,
        turned2,
        pre,
        up,
        down,
        resid,
        attn,
        cotangent,
        weight_out,
        norm_gain,
    )
    d_o_rows = comm.exchange(d_o)
    d_mlp_turned = comm.reduce_start(send, keep, turned_attn, o_own, d_mlp_turned)
    grad_down, *d_o_rows = tie(grad_down_of(d_mlp_turned, pre), *d_o_rows)
    comm.reduce_down(grad_down)
    if halves < n:
        order = (jnp.arange(n) - rank) % n
        d_o_rows = [jnp.take(jnp.stack(d_o_rows), order, axis=0).reshape(tokens, width)]
    d_o_rows = comm.reduce_first(d_o_rows)

    d_qkv = None
    for pair in range(pairs):
        i, column = divmod(pair, per_call)
        d_qkv = attention_backward(
            pair,
            qkv,
            [o[i] for o in o_rows],
            d_o_rows,
            [l[i] for l in lse_rows],
            column,
            starts,
            lo,
            scalar(places[0]),
            d_qkv,
        )
        d_qkv = comm.beside_backward(pair, d_qkv)

    d_u1_parts, sums0, head_sums = [None] * n, 0.0, 0.0
    for g in reversed(range(1, n)):
        d_u1_parts[g], sums, head_row = d_in(row_at[g], own_rows, d_qkv, weight_qkv, inputs)
        d_u1_parts[g], d_qkv = tie(d_u1_parts[g], d_qkv)
        sums0, head_sums = sums0 + sums, head_sums + head_row[0]

    def small(own):
        totals, head_totals = sums0 + own[1], head_sums + own[2][0]
        hidden_full = jnp.roll(bias_hidden[0], rank * hidden)
        head_terms = head_totals.reshape(pairs, 3, PAIR).transpose(1, 0, 2).reshape(3, width)[0::2]
        head_full = lax.dynamic_update_slice_in_dim(
            jnp.zeros(head_bias.shape, F32), head_terms, rank * width, 1
        )
        gains = [totals[0], sums12[2], sums12[0], sums3[0]]
        shifts = [totals[1], sums12[3], sums12[1], sums3[1]]
        rows = jnp.stack(gains + shifts + [sums12[4], sums3[2]])
        return jnp.concatenate([rows, head_full, hidden_full.reshape(-1, features)])

    d_inputs, small_sums, grad_up, grad_out, grad_qkv, grad_down = comm.tail(
        turned1,
        d_qkv,
        d_u1_parts,
        lambda d_qkv: d_in(row_at[0], own_rows, d_qkv, weight_qkv, inputs),
        small,
        lambda terms: last(row_at[0], terms, inputs, d_resid, norm_gain),
    )
    grad_qkv = grad_qkv.reshape(-1, pairs, 3, PAIR).transpose(2, 0, 1, 3).reshape(3, -1, width)
    return (
        output,
        d_inputs,
        grad_qkv,
        grad_out.T,
        grad_up,
        grad_down.T,
        small_sums[0:4],
        small_sums[4:8],
        small_sums[10:12],
        small_sums[8:10],
        small_sums[12:].reshape(-1),
    )


def solution(mesh):
    staged = mesh.shape["dp"] == NZ * NX * NC and mesh.shape["tensor"] == 2
    return jax.shard_map(
        functools.partial(per_device, staged),
        mesh=mesh,
        in_specs=(
            P("dp", None),
            P("dp", None),
            P("dp", None),
            P(None, "dp", "tensor"),
            P("tensor", "dp"),
            P("dp", "tensor"),
            P("tensor", "dp"),
            P(),
            P(),
            P(),
            P(),
            P(),
        ),
        out_specs=(
            P(("dp", "tensor"), None),
            P(("dp", "tensor"), None),
            P(None, "dp", "tensor"),
            P("tensor", "dp"),
            P("dp", "tensor"),
            P("tensor", "dp"),
            P(),
            P(),
            P(),
            P(),
            P(),
        ),
        check_vma=False,
    )
```
